128 devices in a mesh: wall: 16 (over x, z), span: 8 (over y, core).
Axes of the slice: x: 4, y: 4, z: 4, core: 2. Of those that a mesh axis runs over, the one named last changes fastest.
Arguments:
- velocity: float32 [3, 512, 128, 1024], P(None, 'wall', 'span'), may hold values from -6 to 6
- lower: float32 [512], replicated, may hold values from 0.01 to 0.95, as said below
- upper: float32 [512], replicated, may hold values from 0.01 to 0.965
- stencil: float32 [5, 512], P(None, 'wall'), may hold values from -1 to 1
- inv_volume: float32 [512], P('wall'), may hold values from 0.5 to 4
- forces: float32 [3, 524288], P(None, ('wall', 'span')), may hold values from -6 to 6
- owner: int32 [524288, 1], P(('wall', 'span')), may hold values from 0 to 127; in each aligned block of 4096 rows (0 to 4095, 4096 to 8191, ...) at most 64 rows name the same one
- cells: int32 [524288], P(('wall', 'span')), may hold values from 0 to 524287
- counts: int32 [128], P(('wall', 'span')), may hold values from 1 to 4096, 393216 in all
Outputs:
- derivative: float32 [3, 512, 128, 1024], P(None, 'wall', 'span')
- forcing: float32 [3, 512, 128, 1024], P(None, 'wall', 'span')
The draws below stay inside these ranges and needn't reach their ends.
Inputs may be any that keep to these rules, and one draw needn't show every extreme that they name: Among the 4096 slots of one device no owner is named more than 64 times, a bound that some block reaches. The counts sum to 393216 and some device is full. lower[j] + upper[j] stays below 1 in every row.
All inputs are finite; a program needn't handle non-finite values.
Results may differ from the reference program's by a relative error of at most 0.0003.
Values sent between devices are 32-bit elements; how exact they have to be, the bound alone decides.
A program may use at most 128 MiB of HBM per device.

```python
import math
import jax
import jax.numpy as jnp
import numpy as np
from jax import lax

RY = 32
SZ = 16
NX = 1024
PART_DEV = 4096
NY = 512
NZ = 128
PARTICLES = 524288
CELLS_DEV = 524288
CAP = 64
N_SPAN = 8
DEVICES = 128


def draw_lower(key, part):
    own_key = jax.random.fold_in(key, 4101)
    return jax.random.uniform(own_key, (NY,), jnp.float32, 0.01, 0.03)


def draw_upper(key, part):
    own_key = jax.random.fold_in(key, 4202)
    return jax.random.uniform(own_key, (NY,), jnp.float32, 0.93, 0.965)


def plant(drawn, stream_key, low, largest):
    spot = [jax.random.randint(jax.random.fold_in(stream_key, axis), (), 0, length) for axis, length in enumerate(drawn.shape)]
    main_axis = drawn.shape.index(max(drawn.shape))
    beside = spot[:main_axis] + [(spot[main_axis] + 1) % drawn.shape[main_axis]] + spot[main_axis + 1:]
    return drawn.at[tuple(spot)].set(low).at[tuple(beside)].set(largest)


def levels(stream_key, dims, cuts, smallest, high):
    def one(axis_at, shards_of):
        steps = jax.random.uniform(jax.random.fold_in(jax.random.fold_in(stream_key, 6), axis_at), (shards_of,), jnp.float32, smallest / len(cuts), high / len(cuts))
        return jnp.repeat(jnp.exp(steps), dims[axis_at] // shards_of).reshape((-1,) + (1,) * (len(dims) - axis_at - 1))

    gain = one(*cuts[0])
    for cut in cuts[1:]:
        gain = gain * one(*cut)
    return gain


def split_up(count, total, limit, slope):
    portions = [(1 << 20) // math.isqrt(grade ** slope) + 1 for grade in range(2, count + 1)]
    spare, given = total - limit - (count - 1), [1] * (count - 1)
    while spare > 0:
        free = [i for i in range(count - 1) if given[i] < limit]
        mass, budget = sum([portions[i] for i in free]), spare
        for i in free:
            more = min(limit - given[i], max(1, budget * portions[i] // mass), spare)
            given[i] = given[i] + more
            spare = spare - more
    return np.array([limit] + given)


def ragged(key, count, total, bound, lean):
    if count == 2:
        one = jax.random.randint(key, (), max(1, total - bound), min(bound, total - 1) + 1)
        return jnp.stack([one, total - one])
    lengths = jnp.asarray(split_up(count, total, bound, lean), jnp.int32)
    twos = (count - 1) // 2
    giver, receiver = lengths[1:1 + 2 * twos:2], lengths[2:2 + 2 * twos:2]
    room = jnp.minimum(giver - 1, bound - receiver)
    passed = jax.random.randint(jax.random.fold_in(key, 1), (twos,), 0, 1 << 20) % (room + 1)
    lengths = lengths.at[1:1 + 2 * twos:2].set(giver - passed).at[2:2 + 2 * twos:2].set(receiver + passed)
    return lengths[jax.random.permutation(jax.random.fold_in(key, 2), count)]


def assign_block(key, own, number, rows, number_of, top, most, lean):
    order = jax.random.permutation(key, number_of)
    heavy_load, ordinary = portions_of(number_of, rows * top, most, lean, True), portions_of(number_of, rows * top, most, lean, False)
    places = jnp.arange(number_of)

    def named(sizes, rotation):
        used = int((sizes > 0).sum())
        fixed = max(1, used // 4)
        shifted = fixed + (places - fixed + rotation * (used - fixed)) % max(1, number_of - fixed)
        return jnp.zeros((number_of,), jnp.int32).at[order[jnp.where(places < fixed, places, shifted)]].set(jnp.asarray(sizes, jnp.int32))

    sizes = jnp.where(number % 4 == 0, named(heavy_load, number // 4), named(ordinary, number - number // 4 - 1))
    mixed = jax.random.permutation(jax.random.fold_in(own, 3), number_of)
    source_of, receiver = mixed[0:number_of // 2 * 2:2], mixed[1:number_of // 2 * 2:2]
    margin = jnp.minimum(sizes[source_of] - 1, most - sizes[receiver]) // 2
    margin = jnp.where((source_of == order[0]) | (receiver == order[0]) | (sizes[receiver] == 0), 0, jnp.maximum(margin, 0))
    shifted = jax.random.randint(jax.random.fold_in(own, 4), (number_of // 2,), 0, 1 << 20) % (margin + 1)
    sizes = sizes.at[source_of].add(-shifted).at[receiver].add(shifted)
    items = jnp.searchsorted(jnp.cumsum(sizes), jnp.arange(rows * top), side="right").astype(jnp.int32)
    table = items.reshape(top, rows).T
    table = table[jax.random.permutation(jax.random.fold_in(own, 1), rows)]
    rotation = jax.random.randint(jax.random.fold_in(own, 2), (rows, 1), 0, top)
    return jnp.take_along_axis(table, (jnp.arange(top)[None, :] + rotation) % top, axis=1)


def portions_of(count, total, bound, skew, full):
    portions = [(1 << 20) // math.isqrt(grade ** skew) + 1 for grade in range(1, count + 1)]
    largest = bound if full else min(bound, max(-(-total // count), total * portions[0] // sum(portions)))
    least = 1 if total - largest >= count - 1 else 0
    given, rest = [largest] + [least] * (count - 1), total - largest - least * (count - 1)
    while rest > 0:
        free = [i for i in range(1, count) if given[i] < largest] or [i for i in range(1, count) if given[i] < bound]
        mass, budget = sum([portions[i] for i in free]), rest
        for i in free:
            extra = min(bound - given[i], max(1, budget * portions[i] // mass), rest)
            given[i] = given[i] + extra
            rest = rest - extra
    return np.array(given)


def gaussian(rng, shape, scale, limit, pieces=(), held_as=jnp.bfloat16):
    result = jax.random.normal(rng, shape, jnp.float32) * scale
    if len(pieces) > 0:
        result = levels(rng, shape, pieces, -0.22, 0.18) * result
    return jnp.clip(result, min=-limit, max=limit).astype(held_as)


def setup_inputs(seed: int = 0) -> dict:
    arg_keys = jax.random.split(jax.random.key(seed), 10)
    velocity = gaussian(arg_keys[0], (3, NY, NZ, NX), 1.0, 6.0, ((1, 16), (2, 8)), jnp.float32)
    lower = draw_lower(jax.random.fold_in(arg_keys[9], 71), 0)
    upper = draw_upper(jax.random.fold_in(arg_keys[9], 71), 0)
    stencil = jnp.clip(jax.random.uniform(arg_keys[3], (5, NY), jnp.float32, -1.0, 1.0) * levels(arg_keys[3], (5, NY), ((1, 16),), -0.4, 0.0), -1.0, 1.0)
    inv_volume = jnp.clip(jnp.exp(math.log(4.0) - 2.0794415 * jax.random.uniform(arg_keys[4], (NY,), jnp.float32) ** levels(arg_keys[4], (NY,), ((0, 16),), -0.2, 0.2)), 0.5, 4.0)
    forces = gaussian(arg_keys[5], (3, PARTICLES), 1.0, 6.0, ((1, 128),), jnp.float32)
    owner_keys = jax.random.split(jax.random.fold_in(arg_keys[6], 1), PARTICLES // PART_DEV)
    owner_turns = jax.random.permutation(jax.random.fold_in(arg_keys[6], 3), PARTICLES // PART_DEV)
    owner = jax.vmap(lambda own, number: assign_block(jax.random.fold_in(arg_keys[6], 2), own, number, PART_DEV, DEVICES, 1, CAP, 2))(owner_keys, owner_turns).reshape((PARTICLES, 1))
    cells = plant(jax.random.randint(arg_keys[7], (PARTICLES,), 0, CELLS_DEV), jax.random.fold_in(arg_keys[7], 1), 0, CELLS_DEV - 1).astype(jnp.int32)
    counts = ragged(arg_keys[8], DEVICES, DEVICES * PART_DEV * 3 // 4, PART_DEV, 1).astype(jnp.int32)
    return dict(velocity=velocity, lower=lower, upper=upper, stencil=stencil, inv_volume=inv_volume, forces=forces, owner=owner, cells=cells, counts=counts)


def pivot_rows(sub_diag, super_diag):
    def advance(carried, row_pair):
        lower_row, upper_row = row_pair
        pivot_now = 1.0 - lower_row * carried
        ratio_now = upper_row / pivot_now
        return ratio_now, (pivot_now, ratio_now)
    initial = jnp.zeros((), sub_diag.dtype)
    _unused, (pivots, ratios) = lax.scan(advance, initial, (sub_diag, super_diag))
    return pivots, ratios


def sweep_solve(sub_diag, pivots, ratios, right_side):
    def forward(previous, row_entry):
        lower_row, pivot_row, value_row = row_entry
        current = (value_row - lower_row * previous) / pivot_row
        return current, current
    _unused, reduced = lax.scan(forward, jnp.zeros_like(right_side[0]), (sub_diag, pivots, right_side))

    def backward(following, row_entry):
        ratio_row, reduced_row = row_entry
        current = reduced_row - ratio_row * following
        return current, current
    _unused2, solved = lax.scan(backward, jnp.zeros_like(right_side[0]), (ratios, reduced), reverse=True)
    return solved


def reference(velocity, lower, upper, stencil, inv_volume, forces, owner, cells, counts):
    rows_all = lower.shape[0]
    padded = jnp.pad(velocity, ((0, 0), (2, 2), (0, 0), (0, 0)))
    stencil_sum = stencil[0][None, :, None, None] * padded[:, 0:rows_all]
    for offset in range(1, 5):
        stencil_sum = stencil_sum + stencil[offset][None, :, None, None] * padded[:, offset:offset + rows_all]
    right_side = jnp.moveaxis(stencil_sum, 1, 0)
    pivots, ratios = pivot_rows(lower, upper)
    solved = sweep_solve(lower, pivots, ratios, right_side)
    derivative = jnp.moveaxis(solved, 0, 1)

    particle_index = jnp.arange(PARTICLES, dtype=jnp.int32)
    alive_mask = (particle_index % PART_DEV) < jnp.repeat(counts, PART_DEV)
    owners = owner[:, 0]
    wall_index = owners // N_SPAN
    span_index = owners % N_SPAN
    row_local = cells // (SZ * NX)
    span_local = (cells // NX) % SZ
    stream_index = cells % NX
    flat_index = ((wall_index * RY + row_local) * NZ + span_index * SZ + span_local) * NX + stream_index
    weighted = jnp.where(alive_mask[None, :], forces, 0.0)
    summed = jnp.zeros((3, NY * NZ * NX), forces.dtype).at[:, flat_index].add(weighted)
    forcing = -inv_volume[None, :, None, None] * summed.reshape(3, NY, NZ, NX)
    return derivative, forcing
```

```python
import functools

import jax
import jax.numpy as jnp
from jax import lax
from jax.experimental import pallas as pl
from jax.experimental.pallas import tpu as pltpu
from jax.sharding import PartitionSpec as P

F32 = jnp.float32
MESH = pl.DeviceIdType.MESH
NW, NS = 16, 8
RY, SZ, NX = 32, 16, 1024
SLOTS = 64


def exchange_kernel(
    vel, lu, st, forces, owner, cells, counts,
    halo, bound, coef, part_t, rows_out,
    vbuf, send_a, recv_a, send_f, elim, pbuf, tile_out, tile_in,
    pack, recv1, pack2, recv2,
    dmat, cmat, ymat, zmat, wmat, wgt, red,
    vsem, hs, hr, ts, tr, as_, ar, fs, fr, p1s, p1r, p2s, p2r,
):
    me_w = lax.axis_index("wall")
    me_s = lax.axis_index("span")

    def vcopy(c, h):
        part = (c, slice(None), pl.ds(h * 8, 8), slice(None))
        return pltpu.make_async_copy(vel.at[part], vbuf.at[part], vsem.at[c * 2 + h])

    for c in range(3):
        for h in range(2):
            vcopy(c, h).start()

    barrier = pltpu.get_barrier_semaphore()

    @pl.loop(1, NW)
    def _(k):
        pl.semaphore_signal(
            barrier, inc=1, device_id=(lax.rem(me_w + k, NW), me_s), device_id_type=MESH
        )

    @pl.loop(1, NS)
    def _(k):
        pl.semaphore_signal(
            barrier, inc=1, device_id=(me_w, lax.rem(me_s + k, NS)), device_id_type=MESH
        )

    pl.semaphore_wait(barrier, NW - 1 + NS - 1)

    above = lax.rem(me_w + 1, NW)
    under = lax.rem(me_w + NW - 1, NW)

    def hcopy(way):
        return pltpu.make_async_remote_copy(
            src_ref=vel.at[:, RY - 1] if way == 0 else vel.at[:, 0],
            dst_ref=halo.at[way],
            send_sem=hs.at[way],
            recv_sem=hr.at[way],
            device_id=(above if way == 0 else under, me_s),
            device_id_type=MESH,
        )

    hcopy(0).start()
    hcopy(1).start()

    eye = lax.broadcasted_iota(jnp.int32, (RY, RY), 0) == lax.broadcasted_iota(
        jnp.int32, (RY, RY), 1
    )

    def column(row, mask, n):
        full = jnp.broadcast_to(row, (n, n))
        col = jnp.sum(jnp.where(mask, full, 0.0), axis=1, keepdims=True)
        return jnp.broadcast_to(col, (n, 128))

    stc = [column(st[m : m + 1, :], eye, RY) for m in range(5)]
    tile_out[0:1, :] = stc[0][0:1]
    tile_out[1:2, :] = stc[1][0:1]
    tile_out[2:3, :] = stc[4][RY - 1 : RY]
    tile_out[3:4, :] = stc[3][RY - 1 : RY]
    tile_out[4:8, :] = jnp.zeros((4, 128), F32)

    def tcopy(way):
        return pltpu.make_async_remote_copy(
            src_ref=tile_out,
            dst_ref=tile_in.at[way],
            send_sem=ts.at[way],
            recv_sem=tr.at[way],
            device_id=(above if way == 0 else under, me_s),
            device_id_type=MESH,
        )

    tcopy(0).start()
    tcopy(1).start()

    count = counts[0]
    pack[...] = jnp.zeros((2, NW * NS, 128), F32)
    up_i = lax.broadcasted_iota(jnp.int32, (256, 256), 0)
    up_j = lax.broadcasted_iota(jnp.int32, (256, 256), 1)
    before = (up_i < up_j).astype(F32).astype(jnp.bfloat16)
    ones = jnp.ones((256, 256), jnp.bfloat16)
    ids = lax.broadcasted_iota(jnp.int32, (NW * NS, 256), 0)
    ranks = lax.broadcasted_iota(jnp.int32, (SLOTS, 256), 0).astype(F32)
    lanes = lax.broadcasted_iota(jnp.int32, (1, 256), 1)
    nt = (((1,), (1,)), ((), ()))
    nn = (((1,), (0,)), ((), ()))

    def pack_block(i, carry):
        at = pl.ds(pl.multiple_of(i * 256, 256), 256)
        own = owner[:, at]
        key = (own & 7) * NW + (own >> 3)
        key = jnp.where(lanes + i * 256 < count, key, 512)
        hit = ids == key
        hot = jnp.where(hit, 1.0, 0.0)
        hot_b = hot.astype(jnp.bfloat16)
        pre = lax.dot_general(hot_b, before, nn, preferred_element_type=F32)
        tot = lax.dot_general(hot_b, ones, nn, preferred_element_type=F32)
        rank = jnp.sum(jnp.where(hit, pre + carry, 0.0), axis=0, keepdims=True)
        place = ranks == rank
        load = [forces[c : c + 1, at] for c in range(3)] + [cells[:, at].astype(F32)]
        sums = None
        for _part in range(3):
            head = [x.astype(jnp.bfloat16).astype(F32) for x in load]
            load = [x - y for x, y in zip(load, head)]
            right = jnp.concatenate(
                [jnp.where(place, y, 0.0) for y in head], axis=0
            ).astype(jnp.bfloat16)
            term = lax.dot_general(hot_b, right, nt, preferred_element_type=F32)
            sums = term if sums is None else sums + term
        pack[0] += sums[:, 0:128]
        pack[1] += sums[:, 128:256]
        return carry + tot

    lax.fori_loop(
        0, owner.shape[1] // 256, pack_block, jnp.zeros((NW * NS, 256), F32)
    )

    def p1copy(k):
        to = lax.rem(me_s + k, NS)
        return pltpu.make_async_remote_copy(
            src_ref=pack.at[:, pl.ds(pl.multiple_of(to * NW, NW), NW)],
            dst_ref=recv1.at[:, pl.ds(pl.multiple_of(me_s * NW, NW), NW)],
            send_sem=p1s.at[k],
            recv_sem=p1r.at[k],
            device_id=(me_w, to),
            device_id_type=MESH,
        )

    for k in range(1, NS):
        p1copy(k).start()
    mine = pl.ds(pl.multiple_of(me_s * NW, NW), NW)
    recv1[:, mine, :] = pack[:, mine, :]

    zero = jnp.zeros((1, NW), F32)
    carry_c, carry_b = zero, None
    for j in range(RY):
        low, upp = lu[0, j : j + 1, :], lu[1, j : j + 1, :]
        inv = 1.0 / (1.0 - low * carry_c) if j > 0 else jnp.ones((1, NW), F32)
        carry_c = upp * inv
        dmat[j : j + 1, :] = inv
        cmat[j : j + 1, :] = carry_c
    binv = [None] * RY
    for j in range(RY - 1, -1, -1):
        if j == RY - 1:
            binv[j] = jnp.ones((1, NW), F32)
        else:
            binv[j] = 1.0 / (
                1.0 - lu[1, j : j + 1, :] * lu[0, j + 1 : j + 2, :] * binv[j + 1]
            )
    y = binv[0]
    ymat[0:1, :] = y
    for j in range(1, RY):
        y = -(lu[1, j - 1 : j, :] * binv[j]) * y
        ymat[j : j + 1, :] = y
    z = dmat[RY - 1 : RY, :]
    zmat[RY - 1 : RY, :] = z
    for j in range(RY - 2, -1, -1):
        z = -(lu[0, j + 1 : j + 2, :] * dmat[j : j + 1, :]) * z
        zmat[j : j + 1, :] = z

    lane16 = lax.broadcasted_iota(jnp.int32, (RY, NW), 1)

    def at_slab(values, slab):
        n = values.shape[0]
        col = jnp.sum(jnp.where(lane16[0:n] == slab, values, 0.0), axis=1, keepdims=True)
        return jnp.broadcast_to(col, (n, 128))

    low_all, upp_all = lu[0], lu[1]
    inv_own = at_slab(dmat[...], me_w)
    c_own = at_slab(cmat[...], me_w)
    y_own = at_slab(ymat[...], me_w)
    z_own = at_slab(zmat[...], me_w)
    low_own = at_slab(low_all, me_w)
    low_next = at_slab(low_all[0:1], me_w + 1)
    upp_prev = at_slab(upp_all[RY - 1 : RY], me_w - 1)
    has_under = jnp.where(me_w > 0, 1.0, 0.0)
    has_above = jnp.where(me_w < NW - 1, 1.0, 0.0)

    row_i = lax.broadcasted_iota(jnp.int32, (RY, 128), 0)
    kept = [
        jnp.where(row_i == 0, 0.0, jnp.where(row_i == 1, stc[0] * has_under, stc[0])),
        jnp.where(row_i == 0, 0.0, stc[1]),
        stc[2],
        jnp.where(row_i == RY - 1, 0.0, stc[3]),
        jnp.where(
            row_i == RY - 1, 0.0, jnp.where(row_i == RY - 2, stc[4] * has_above, stc[4])
        ),
    ]
    for m in range(5):
        coef[m] = kept[m] * inv_own
    coef[5] = jnp.where(row_i == 0, 0.0, low_own * inv_own)
    coef[6] = c_own
    coef[7] = inv_own

    tcopy(0).wait()
    tcopy(1).wait()
    for way, own, scale in ((0, z_own, low_next), (1, y_own, upp_prev)):
        wmat[...] = jnp.zeros((RY + 8, 128), F32)
        for m in range(5):
            wmat[m + 2 : m + 2 + RY, :] += kept[m] * own
        wgt[way] = wmat[...] * (-scale)
    wgt[0, RY + 2 : RY + 3, :] += tile_in[1, 0:1, :]
    wgt[0, RY + 3 : RY + 4, :] += tile_in[1, 1:2, :]
    wgt[1, 5:6, :] += tile_in[0, 2:3, :]
    wgt[1, 4:5, :] += tile_in[0, 3:4, :]

    eye16 = lax.broadcasted_iota(jnp.int32, (NW, NW), 0) == lax.broadcasted_iota(
        jnp.int32, (NW, NW), 1
    )
    next16 = lax.broadcasted_iota(jnp.int32, (NW, NW), 0) + 1 == lax.broadcasted_iota(
        jnp.int32, (NW, NW), 1
    )
    prev16 = lax.broadcasted_iota(jnp.int32, (NW, NW), 0) - 1 == lax.broadcasted_iota(
        jnp.int32, (NW, NW), 1
    )
    z0 = column(zmat[0:1, :], eye16, NW)
    z1 = column(zmat[RY - 1 : RY, :], eye16, NW)
    y0 = column(ymat[0:1, :], eye16, NW)
    y1 = column(ymat[RY - 1 : RY, :], eye16, NW)
    low_n = column(low_all[0:1], next16, NW)
    upp_p = column(upp_all[RY - 1 : RY], prev16, NW)
    red[0] = upp_p * y0
    red[1] = low_n * z0
    lz1 = low_n * z1
    uy1 = upp_p * y1
    q = -lz1[0:1]
    for s in range(1, NW):
        dinv = 1.0 / (1.0 + red[0, s : s + 1, :] * q)
        c3 = uy1[s : s + 1] * dinv
        red[2, s : s + 1, :] = q * dinv
        red[3, s : s + 1, :] = dinv
        red[4, s : s + 1, :] = c3
        red[5, s : s + 1, :] = q
        q = red[1, s : s + 1, :] * q * c3 - lz1[s : s + 1]

    for c in range(3):
        for h in range(2):
            vcopy(c, h).wait()

            @pl.loop(0, 2)
            def _(x):
                cols = pl.ds(pl.multiple_of(x * 512, 512), 512)
                up = jnp.zeros((8, 512), F32)
                down = jnp.zeros((8, 512), F32)
                for j in range(RY):
                    u = vbuf[c, j, h * 8 : h * 8 + 8, cols]
                    up = up + wgt[0, j + 4 : j + 5, 0:1] * u
                    down = down + wgt[1, j + 4 : j + 5, 0:1] * u
                for b in range(4):
                    send_a[h * 8 + x * 4 + b, 0, c] = up[:, b * 128 : b * 128 + 128]
                    send_a[h * 8 + x * 4 + b, 1, c] = down[:, b * 128 : b * 128 + 128]

    for k in range(1, NS):
        p1copy(k).wait()
    for w in range(NW):
        for b in range(2):
            pack2[w, b] = recv1[b, pl.ds(w, NS, stride=NW), :]

    def p2copy(k):
        to = lax.rem(me_w + k, NW)
        return pltpu.make_async_remote_copy(
            src_ref=pack2.at[to],
            dst_ref=recv2.at[me_w],
            send_sem=p2s.at[k],
            recv_sem=p2r.at[k],
            device_id=(to, me_s),
            device_id_type=MESH,
        )

    for k in range(1, NW):
        p2copy(k).start()
    recv2[me_w] = pack2[me_w]

    hcopy(0).wait()
    hcopy(1).wait()
    for h in range(2):

        @pl.loop(0, 8)
        def _(x):
            cols = pl.ds(pl.multiple_of(x * 128, 128), 128)
            for c in range(3):
                lo = halo[0, c, h * 8 : h * 8 + 8, cols]
                hi = halo[1, c, h * 8 : h * 8 + 8, cols]
                for way in range(2):
                    send_a[h * 8 + x, way, c] += (
                        wgt[way, 3:4, 0:1] * lo + wgt[way, RY + 4 : RY + 5, 0:1] * hi
                    )

    def acopy(k):
        to = lax.rem(me_w + k, NW)
        return pltpu.make_async_remote_copy(
            src_ref=send_a.at[to],
            dst_ref=recv_a.at[me_w],
            send_sem=as_.at[k],
            recv_sem=ar.at[k],
            device_id=(to, me_s),
            device_id_type=MESH,
        )

    for k in range(1, NW):
        acopy(k).start()
    recv_a[me_w] = send_a[me_w]
    for k in range(1, NW):
        acopy(k).wait()

    p = recv_a[0, 0]
    for s in range(1, NW):
        pbuf[s] = p
        e = recv_a[s, 1] - red[0, s : s + 1, :] * p
        elim[s] = e
        if s < NW - 1:
            p = recv_a[s, 0] - red[1, s : s + 1, :] * (p + red[2, s : s + 1, :] * e)
    down = jnp.zeros((3, 8, 128), F32)
    send_f[NW - 1, 1] = down
    for s in range(NW - 1, 0, -1):
        down = red[3, s : s + 1, :] * elim[s] - red[4, s : s + 1, :] * down
        send_f[s - 1, 1] = down
        send_f[s, 0] = pbuf[s] + red[5, s : s + 1, :] * down
    send_f[0, 0] = jnp.zeros((3, 8, 128), F32)

    def fcopy(k):
        to = lax.rem(me_w + k, NW)
        return pltpu.make_async_remote_copy(
            src_ref=send_f.at[to],
            dst_ref=bound.at[me_w],
            send_sem=fs.at[k],
            recv_sem=fr.at[k],
            device_id=(to, me_s),
            device_id_type=MESH,
        )

    for k in range(1, NW):
        fcopy(k).start()
    bound[me_w] = send_f[me_w]

    for k in range(1, NW):
        p2copy(k).wait()
    part_t[0:128, :] = recv2[:, 0].reshape(NW * NS, 128).T
    rest = recv2[:, 1].reshape(NW * NS, 128)
    flipped = rest.T
    part_t[128:192, :] = flipped[0:64]
    part_t[192:256, :] = (flipped[64:128].astype(jnp.int32) & 127).astype(F32)
    rows_out[...] = (rest[:, 64:128].astype(jnp.int32) >> 7) * 4

    for k in range(1, NW):
        fcopy(k).wait()


def exchange(vel, lu, st, forces, owner, cells, counts):
    vm = pl.BlockSpec(memory_space=pltpu.VMEM)
    dma = pltpu.SemaphoreType.DMA
    return pl.pallas_call(
        exchange_kernel,
        out_shape=(
            jax.ShapeDtypeStruct((2, 3, SZ, NX), F32),
            jax.ShapeDtypeStruct((NW, 2, 3, 8, 128), F32),
            jax.ShapeDtypeStruct((8, RY, 128), F32),
            jax.ShapeDtypeStruct((256, 128), F32),
            jax.ShapeDtypeStruct((128, SLOTS), jnp.int32),
        ),
        in_specs=[pl.BlockSpec(memory_space=pl.ANY)] + [vm] * 5
        + [pl.BlockSpec(memory_space=pltpu.SMEM)],
        out_specs=[vm] * 5,
        scratch_shapes=[
            pltpu.VMEM((3, RY, SZ, NX), F32),
            pltpu.VMEM((NW, 2, 3, 8, 128), F32),
            pltpu.VMEM((NW, 2, 3, 8, 128), F32),
            pltpu.VMEM((NW, 2, 3, 8, 128), F32),
            pltpu.VMEM((NW, 3, 8, 128), F32),
            pltpu.VMEM((NW, 3, 8, 128), F32),
            pltpu.VMEM((8, 128), F32),
            pltpu.VMEM((2, 8, 128), F32),
            pltpu.VMEM((2, NW * NS, 128), F32),
            pltpu.VMEM((2, NW * NS, 128), F32),
            pltpu.VMEM((NW, 2, NS, 128), F32),
            pltpu.VMEM((NW, 2, NS, 128), F32),
            pltpu.VMEM((RY, NW), F32),
            pltpu.VMEM((RY, NW), F32),
            pltpu.VMEM((RY, NW), F32),
            pltpu.VMEM((RY, NW), F32),
            pltpu.VMEM((RY + 8, 128), F32),
            pltpu.VMEM((2, RY + 8, 128), F32),
            pltpu.VMEM((6, NW, 128), F32),
            dma((6,)), dma((2,)), dma((2,)), dma((2,)), dma((2,)),
            dma((NW,)), dma((NW,)), dma((NW,)), dma((NW,)),
            dma((NS,)), dma((NS,)), dma((NW,)), dma((NW,)),
        ],
        compiler_params=pltpu.CompilerParams(
            collective_id=0, has_side_effects=True, vmem_limit_bytes=56 << 20
        ),
        name="exchange",
    )(vel, lu, st, forces, owner, cells, counts)


def deposit_kernel(part_t, rows, inv_vol, out, acc0, acc1, acc2, acc3, even, odd, stage, sem):
    accs = (acc0, acc1, acc2, acc3)
    zeros = jnp.zeros((128, 128), F32)

    @pl.loop(0, 128)
    def _(i):
        at = pl.ds(pl.multiple_of(i * 128, 128), 128)
        for acc in accs:
            acc[at, :] = zeros

    lane = lax.broadcasted_iota(jnp.int32, (8, 128), 1).astype(F32)

    def spread(source, to):
        pick = jnp.full((8, 128), source, jnp.int32)
        for g in range(SLOTS // 8):
            xl = jnp.take_along_axis(part_t[192 + g * 8 : 200 + g * 8, :], pick, axis=1)
            hit = xl == lane
            for c in range(3):
                r0 = c * SLOTS + g * 8
                f = jnp.take_along_axis(part_t[r0 : r0 + 8, :], pick, axis=1)
                to[r0 : r0 + 8, :] = jnp.where(hit, f, 0.0)

    def add(source, frm):
        for r in range(SLOTS):
            at = pl.ds(pl.multiple_of(rows[source, r], 4), 4)
            accs[r % 4][at, :] += frm[pl.ds(r, 4, stride=SLOTS), :]

    spread(0, even)

    @pl.loop(0, 64)
    def _(i):
        spread(2 * i + 1, odd)
        add(2 * i, even)
        spread(jnp.minimum(2 * i + 2, 127), even)
        add(2 * i + 1, odd)

    def put(b):
        part = (slice(None), pl.ds(b * 4, 4))
        return pltpu.make_async_copy(stage.at[part], out.at[part], sem.at[b])

    @pl.loop(0, 8)
    def _(b):
        @pl.loop(0, 4)
        def _(jj):
            j = b * 4 + jj
            scale = -inv_vol[j]
            for h in range(2):
                for x in range(8):
                    for c in range(3):
                        at = pl.ds(((j * SZ + h * 8) * 8 + x) * 4 + c, 8, stride=32)
                        t = (acc0[at, :] + acc1[at, :]) + (acc2[at, :] + acc3[at, :])
                        stage[c, j, h * 8 : h * 8 + 8, x * 128 : x * 128 + 128] = scale * t

        put(b).start()

    @pl.loop(0, 8)
    def _(b):
        put(b).wait()


def deposit(part_t, rows, inv_vol):
    sm = pl.BlockSpec(memory_space=pltpu.SMEM)
    cells = RY * SZ * NX // 128 * 4
    return pl.pallas_call(
        deposit_kernel,
        out_shape=jax.ShapeDtypeStruct((3, RY, SZ, NX), F32),
        in_specs=[pl.BlockSpec(memory_space=pltpu.VMEM), sm, sm],
        out_specs=pl.BlockSpec(memory_space=pl.ANY),
        scratch_shapes=[pltpu.VMEM((cells, 128), F32)] * 4
        + [pltpu.VMEM((256, 128), F32)] * 2
        + [pltpu.VMEM((3, RY, SZ, NX), F32), pltpu.SemaphoreType.DMA((8,))],
        compiler_params=pltpu.CompilerParams(vmem_limit_bytes=56 << 20),
        name="deposit",
    )(part_t, rows, inv_vol)


def sweep_kernel(vel, halo, bound, coef, out):
    for b in range(2):
        for h in range(2):
            cells = (slice(h * 8, h * 8 + 8), slice(b * 128, b * 128 + 128))

            def row(j):
                if j == -1:
                    return halo[0, 0, *cells]
                if j == RY:
                    return halo[1, 0, *cells]
                return vel[0, j, *cells]

            prev = None
            for j in range(RY):
                total = None
                for m in range(5):
                    i = j + m - 2
                    if i < -1 or i > RY or (i == -1 and j == 0) or (i == RY and j == RY - 1):
                        continue
                    term = coef[m, j : j + 1, :] * row(i)
                    total = term if total is None else total + term
                if j == 0:
                    total = total + coef[7, 0:1, :] * bound[h, b, 0, 0]
                if j == RY - 1:
                    total = total + coef[7, RY - 1 : RY, :] * bound[h, b, 1, 0]
                if j > 0:
                    total = total - coef[5, j : j + 1, :] * prev
                prev = total
                out[0, j, *cells] = total
            for j in range(RY - 2, -1, -1):
                prev = out[0, j, *cells] - coef[6, j : j + 1, :] * prev
                out[0, j, *cells] = prev


def sweep(vel, halo, bound, coef):
    return pl.pallas_call(
        sweep_kernel,
        grid=(3, 4),
        out_shape=jax.ShapeDtypeStruct((3, RY, SZ, NX), F32),
        in_specs=[
            pl.BlockSpec((1, RY, SZ, 256), lambda c, x: (c, 0, 0, x)),
            pl.BlockSpec((2, 1, SZ, 256), lambda c, x: (0, c, 0, x)),
            pl.BlockSpec((2, 2, 2, 1, 8, 128), lambda c, x: (0, x, 0, c, 0, 0)),
            pl.BlockSpec((8, RY, 128), lambda c, x: (0, 0, 0)),
        ],
        out_specs=pl.BlockSpec((1, RY, SZ, 256), lambda c, x: (c, 0, 0, x)),
        compiler_params=pltpu.CompilerParams(vmem_limit_bytes=56 << 20),
        name="sweep",
    )(vel, halo, bound.reshape(2, 8, 2, 3, 8, 128), coef)


def body(velocity, lower, upper, stencil, inv_volume, forces, owner, cells, counts):
    lu = jnp.stack([lower, upper]).reshape(2, NW, RY).transpose(0, 2, 1)
    halo, bound, coef, part_t, rows = exchange(
        velocity, lu, stencil, forces, owner.reshape(1, -1), cells.reshape(1, -1), counts
    )
    forcing = deposit(part_t, rows, inv_volume)
    derivative = sweep(velocity, halo, bound, coef)
    return derivative, forcing


def solution(mesh):
    in_specs = (
        P(None, "wall", "span", None),
        P(),
        P(),
        P(None, "wall"),
        P("wall"),
        P(None, ("wall", "span")),
        P(("wall", "span"), None),
        P(("wall", "span")),
        P(("wall", "span")),
    )
    out_specs = (P(None, "wall", "span", None), P(None, "wall", "span", None))
    return jax.shard_map(body, mesh=mesh, in_specs=in_specs, out_specs=out_specs, check_vma=False)
```

```python
import functools

import jax
import jax.numpy as jnp
from jax import lax
from jax.experimental import pallas as pl
from jax.experimental.pallas import tpu as pltpu
from jax.sharding import PartitionSpec as P

F32 = jnp.float32
MESH = pl.DeviceIdType.MESH
NW, NS = 16, 8
RY, SZ, NX = 32, 16, 1024
SLOTS = 64


def exchange_kernel(
    vel, lower, upper, st, forces, owner, cells, counts,
    halo, bound, coef, part_t, rows_out,
    vbuf, send_a, recv_a, send_f, elim, pbuf, tile_out, tile_in,
    pack, recv1, pack2, recv2,
    lmat, umat, dmat, cmat, ymat, zmat, wmat, wgt, red,
    vsem, hs, hr, ts, tr, as_, ar, fs, fr, p1s, p1r, p2s, p2r,
):
    me_w = lax.axis_index("wall")
    me_s = lax.axis_index("span")

    def vcopy(c, h):
        part = (c, slice(None), pl.ds(h * 8, 8), slice(None))
        return pltpu.make_async_copy(vel.at[part], vbuf.at[part], vsem.at[c * 2 + h])

    for c in range(3):
        for h in range(2):
            vcopy(c, h).start()

    barrier = pltpu.get_barrier_semaphore()

    @pl.loop(1, NW)
    def _(k):
        pl.semaphore_signal(
            barrier, inc=1, device_id=(lax.rem(me_w + k, NW), me_s), device_id_type=MESH
        )

    @pl.loop(1, NS)
    def _(k):
        pl.semaphore_signal(
            barrier, inc=1, device_id=(me_w, lax.rem(me_s + k, NS)), device_id_type=MESH
        )

    pl.semaphore_wait(barrier, NW - 1 + NS - 1)

    above = lax.rem(me_w + 1, NW)
    under = lax.rem(me_w + NW - 1, NW)

    def hcopy(way):
        return pltpu.make_async_remote_copy(
            src_ref=vel.at[:, RY - 1] if way == 0 else vel.at[:, 0],
            dst_ref=halo.at[way],
            send_sem=hs.at[way],
            recv_sem=hr.at[way],
            device_id=(above if way == 0 else under, me_s),
            device_id_type=MESH,
        )

    hcopy(0).start()
    hcopy(1).start()

    eye = lax.broadcasted_iota(jnp.int32, (RY, RY), 0) == lax.broadcasted_iota(
        jnp.int32, (RY, RY), 1
    )

    def column(row, mask, n):
        full = jnp.broadcast_to(row, (n, n))
        col = jnp.sum(jnp.where(mask, full, 0.0), axis=1, keepdims=True)
        return jnp.broadcast_to(col, (n, 128))

    stc = [column(st[m : m + 1, :], eye, RY) for m in range(5)]
    tile_out[0:1, :] = stc[0][0:1]
    tile_out[1:2, :] = stc[1][0:1]
    tile_out[2:3, :] = stc[4][RY - 1 : RY]
    tile_out[3:4, :] = stc[3][RY - 1 : RY]
    tile_out[4:8, :] = jnp.zeros((4, 128), F32)

    def tcopy(way):
        return pltpu.make_async_remote_copy(
            src_ref=tile_out,
            dst_ref=tile_in.at[way],
            send_sem=ts.at[way],
            recv_sem=tr.at[way],
            device_id=(above if way == 0 else under, me_s),
            device_id_type=MESH,
        )

    tcopy(0).start()
    tcopy(1).start()

    nn = (((1,), (0,)), ((), ()))
    lane_i = lax.broadcasted_iota(jnp.int32, (RY, NW * RY), 1)
    in_row = (lane_i & (RY - 1)) == lax.broadcasted_iota(jnp.int32, (RY, NW * RY), 0)
    to_slab = (
        lax.broadcasted_iota(jnp.int32, (NW * RY, 128), 0) // RY
        == lax.broadcasted_iota(jnp.int32, (NW * RY, 128), 1)
    ).astype(F32).astype(jnp.bfloat16)
    both = jnp.concatenate(
        [
            jnp.where(in_row, jnp.broadcast_to(v[0:1, :], (RY, NW * RY)), 0.0)
            for v in (lower, upper)
        ],
        axis=0,
    )
    tall = None
    for _part in range(3):
        head = both.astype(jnp.bfloat16)
        both = both - head.astype(F32)
        term = lax.dot_general(head, to_slab, nn, preferred_element_type=F32)
        tall = term if tall is None else tall + term
    lmat[...] = tall[0:RY]
    umat[...] = tall[RY : 2 * RY]

    zero = jnp.zeros((1, 128), F32)
    carry_c, carry_b = zero, None
    for j in range(RY):
        low, upp = lmat[j : j + 1, :], umat[j : j + 1, :]
        inv = 1.0 / (1.0 - low * carry_c) if j > 0 else jnp.ones((1, 128), F32)
        carry_c = upp * inv
        dmat[j : j + 1, :] = inv
        cmat[j : j + 1, :] = carry_c
    binv = [None] * RY
    for j in range(RY - 1, -1, -1):
        if j == RY - 1:
            binv[j] = jnp.ones((1, 128), F32)
        else:
            binv[j] = 1.0 / (
                1.0 - umat[j : j + 1, :] * lmat[j + 1 : j + 2, :] * binv[j + 1]
            )
    y = binv[0]
    ymat[0:1, :] = y
    for j in range(1, RY):
        y = -(umat[j - 1 : j, :] * binv[j]) * y
        ymat[j : j + 1, :] = y
    z = dmat[RY - 1 : RY, :]
    zmat[RY - 1 : RY, :] = z
    for j in range(RY - 2, -1, -1):
        z = -(lmat[j + 1 : j + 2, :] * dmat[j : j + 1, :]) * z
        zmat[j : j + 1, :] = z

    lane16 = lax.broadcasted_iota(jnp.int32, (RY, 128), 1)

    def at_slab(values, slab):
        n = values.shape[0]
        col = jnp.sum(jnp.where(lane16[0:n] == slab, values, 0.0), axis=1, keepdims=True)
        return jnp.broadcast_to(col, (n, 128))

    low_all, upp_all = lmat[...], umat[...]
    inv_own = at_slab(dmat[...], me_w)
    c_own = at_slab(cmat[...], me_w)
    y_own = at_slab(ymat[...], me_w)
    z_own = at_slab(zmat[...], me_w)
    low_own = at_slab(low_all, me_w)
    low_next = at_slab(low_all[0:1], me_w + 1)
    upp_prev = at_slab(upp_all[RY - 1 : RY], me_w - 1)
    has_under = jnp.where(me_w > 0, 1.0, 0.0)
    has_above = jnp.where(me_w < NW - 1, 1.0, 0.0)

    row_i = lax.broadcasted_iota(jnp.int32, (RY, 128), 0)
    kept = [
        jnp.where(row_i == 0, 0.0, jnp.where(row_i == 1, stc[0] * has_under, stc[0])),
        jnp.where(row_i == 0, 0.0, stc[1]),
        stc[2],
        jnp.where(row_i == RY - 1, 0.0, stc[3]),
        jnp.where(
            row_i == RY - 1, 0.0, jnp.where(row_i == RY - 2, stc[4] * has_above, stc[4])
        ),
    ]
    for m in range(5):
        coef[m] = kept[m] * inv_own
    coef[5] = jnp.where(row_i == 0, 0.0, low_own * inv_own)
    coef[6] = c_own
    coef[7] = inv_own

    tcopy(0).wait()
    tcopy(1).wait()
    for way, own, scale in ((0, z_own, low_next), (1, y_own, upp_prev)):
        wmat[...] = jnp.zeros((RY + 8, 128), F32)
        for m in range(5):
            wmat[m + 2 : m + 2 + RY, :] += kept[m] * own
        wgt[way] = wmat[...] * (-scale)
    wgt[0, RY + 2 : RY + 3, :] += tile_in[1, 0:1, :]
    wgt[0, RY + 3 : RY + 4, :] += tile_in[1, 1:2, :]
    wgt[1, 5:6, :] += tile_in[0, 2:3, :]
    wgt[1, 4:5, :] += tile_in[0, 3:4, :]

    eye16 = lax.broadcasted_iota(jnp.int32, (NW, NW), 0) == lax.broadcasted_iota(
        jnp.int32, (NW, NW), 1
    )
    next16 = lax.broadcasted_iota(jnp.int32, (NW, NW), 0) + 1 == lax.broadcasted_iota(
        jnp.int32, (NW, NW), 1
    )
    prev16 = lax.broadcasted_iota(jnp.int32, (NW, NW), 0) - 1 == lax.broadcasted_iota(
        jnp.int32, (NW, NW), 1
    )
    z0 = column(zmat[0:1, 0:NW], eye16, NW)
    z1 = column(zmat[RY - 1 : RY, 0:NW], eye16, NW)
    y0 = column(ymat[0:1, 0:NW], eye16, NW)
    y1 = column(ymat[RY - 1 : RY, 0:NW], eye16, NW)
    low_n = column(low_all[0:1, 0:NW], next16, NW)
    upp_p = column(upp_all[RY - 1 : RY, 0:NW], prev16, NW)
    red[0] = upp_p * y0
    red[1] = low_n * z0
    lz1 = low_n * z1
    uy1 = upp_p * y1
    q = -lz1[0:1]
    for s in range(1, NW):
        dinv = 1.0 / (1.0 + red[0, s : s + 1, :] * q)
        c3 = uy1[s : s + 1] * dinv
        red[2, s : s + 1, :] = q * dinv
        red[3, s : s + 1, :] = dinv
        red[4, s : s + 1, :] = c3
        red[5, s : s + 1, :] = q
        q = red[1, s : s + 1, :] * q * c3 - lz1[s : s + 1]

    for c in range(3):
        for h in range(2):
            vcopy(c, h).wait()

            @pl.loop(0, 2)
            def _(x):
                cols = pl.ds(pl.multiple_of(x * 512, 512), 512)
                up = jnp.zeros((8, 512), F32)
                down = jnp.zeros((8, 512), F32)
                for j in range(RY):
                    u = vbuf[c, j, h * 8 : h * 8 + 8, cols]
                    up = up + wgt[0, j + 4 : j + 5, 0:1] * u
                    down = down + wgt[1, j + 4 : j + 5, 0:1] * u
                for b in range(4):
                    send_a[h * 8 + x * 4 + b, 0, c] = up[:, b * 128 : b * 128 + 128]
                    send_a[h * 8 + x * 4 + b, 1, c] = down[:, b * 128 : b * 128 + 128]

    hcopy(0).wait()
    hcopy(1).wait()
    for h in range(2):

        @pl.loop(0, 8)
        def _(x):
            cols = pl.ds(pl.multiple_of(x * 128, 128), 128)
            for c in range(3):
                lo = halo[0, c, h * 8 : h * 8 + 8, cols]
                hi = halo[1, c, h * 8 : h * 8 + 8, cols]
                for way in range(2):
                    send_a[h * 8 + x, way, c] += (
                        wgt[way, 3:4, 0:1] * lo + wgt[way, RY + 4 : RY + 5, 0:1] * hi
                    )

    def acopy(k):
        to = lax.rem(me_w + k, NW)
        return pltpu.make_async_remote_copy(
            src_ref=send_a.at[to],
            dst_ref=recv_a.at[me_w],
            send_sem=as_.at[k],
            recv_sem=ar.at[k],
            device_id=(to, me_s),
            device_id_type=MESH,
        )

    for k in range(1, NW):
        acopy(k).start()
    recv_a[me_w] = send_a[me_w]

    count = counts[0]
    pack[...] = jnp.zeros((2, NW * NS, 128), F32)
    up_i = lax.broadcasted_iota(jnp.int32, (256, 256), 0)
    up_j = lax.broadcasted_iota(jnp.int32, (256, 256), 1)
    before = (up_i < up_j).astype(F32).astype(jnp.bfloat16)
    ones = jnp.ones((256, 256), jnp.bfloat16)
    ids = lax.broadcasted_iota(jnp.int32, (NW * NS, 256), 0)
    ranks = lax.broadcasted_iota(jnp.int32, (SLOTS, 256), 0).astype(F32)
    lanes = lax.broadcasted_iota(jnp.int32, (1, 256), 1)
    nt = (((1,), (1,)), ((), ()))

    def pack_block(i, carry):
        at = pl.ds(pl.multiple_of(i * 256, 256), 256)
        own = owner[:, at]
        key = (own & 7) * NW + (own >> 3)
        key = jnp.where(lanes + i * 256 < count, key, 512)
        hit = ids == key
        hot = jnp.where(hit, 1.0, 0.0)
        hot_b = hot.astype(jnp.bfloat16)
        pre = lax.dot_general(hot_b, before, nn, preferred_element_type=F32)
        tot = lax.dot_general(hot_b, ones, nn, preferred_element_type=F32)
        rank = jnp.sum(jnp.where(hit, pre + carry, 0.0), axis=0, keepdims=True)
        place = ranks == rank
        load = [forces[c : c + 1, at] for c in range(3)] + [cells[:, at].astype(F32)]
        sums = None
        for _part in range(3):
            head = [x.astype(jnp.bfloat16).astype(F32) for x in load]
            load = [x - y for x, y in zip(load, head)]
            right = jnp.concatenate(
                [jnp.where(place, y, 0.0) for y in head], axis=0
            ).astype(jnp.bfloat16)
            term = lax.dot_general(hot_b, right, nt, preferred_element_type=F32)
            sums = term if sums is None else sums + term
        pack[0] += sums[:, 0:128]
        pack[1] += sums[:, 128:256]
        return carry + tot

    lax.fori_loop(
        0, owner.shape[1] // 256, pack_block, jnp.zeros((NW * NS, 256), F32)
    )

    def p1copy(k):
        to = lax.rem(me_s + k, NS)
        return pltpu.make_async_remote_copy(
            src_ref=pack.at[:, pl.ds(pl.multiple_of(to * NW, NW), NW)],
            dst_ref=recv1.at[:, pl.ds(pl.multiple_of(me_s * NW, NW), NW)],
            send_sem=p1s.at[k],
            recv_sem=p1r.at[k],
            device_id=(me_w, to),
            device_id_type=MESH,
        )

    for k in range(1, NS):
        p1copy(k).start()
    mine = pl.ds(pl.multiple_of(me_s * NW, NW), NW)
    recv1[:, mine, :] = pack[:, mine, :]

    for k in range(1, NW):
        acopy(k).wait()

    p = recv_a[0, 0]
    for s in range(1, NW):
        pbuf[s] = p
        e = recv_a[s, 1] - red[0, s : s + 1, :] * p
        elim[s] = e
        if s < NW - 1:
            p = recv_a[s, 0] - red[1, s : s + 1, :] * (p + red[2, s : s + 1, :] * e)
    down = jnp.zeros((3, 8, 128), F32)
    send_f[NW - 1, 1] = down
    for s in range(NW - 1, 0, -1):
        down = red[3, s : s + 1, :] * elim[s] - red[4, s : s + 1, :] * down
        send_f[s - 1, 1] = down
        send_f[s, 0] = pbuf[s] + red[5, s : s + 1, :] * down
    send_f[0, 0] = jnp.zeros((3, 8, 128), F32)

    def fcopy(k):
        to = lax.rem(me_w + k, NW)
        return pltpu.make_async_remote_copy(
            src_ref=send_f.at[to],
            dst_ref=bound.at[me_w],
            send_sem=fs.at[k],
            recv_sem=fr.at[k],
            device_id=(to, me_s),
            device_id_type=MESH,
        )

    for k in range(1, NW):
        fcopy(k).start()
    bound[me_w] = send_f[me_w]

    for k in range(1, NS):
        p1copy(k).wait()
    for w in range(NW):
        for b in range(2):
            pack2[w, b] = recv1[b, pl.ds(w, NS, stride=NW), :]

    def p2copy(k):
        to = lax.rem(me_w + k, NW)
        return pltpu.make_async_remote_copy(
            src_ref=pack2.at[to],
            dst_ref=recv2.at[me_w],
            send_sem=p2s.at[k],
            recv_sem=p2r.at[k],
            device_id=(to, me_s),
            device_id_type=MESH,
        )

    for k in range(1, NW):
        p2copy(k).start()
    recv2[me_w] = pack2[me_w]

    for k in range(1, NW):
        p2copy(k).wait()
    part_t[0:128, :] = recv2[:, 0].reshape(NW * NS, 128).T
    rest = recv2[:, 1].reshape(NW * NS, 128)
    flipped = rest.T
    part_t[128:192, :] = flipped[0:64]
    part_t[192:256, :] = (flipped[64:128].astype(jnp.int32) & 127).astype(F32)
    place = rest[:, 64:128].astype(jnp.int32)
    rows_out[...] = (
        (place >> 13) * 64 + ((place >> 7) & 7) * 8 + ((place >> 10) & 7)
    ) * 4

    for k in range(1, NW):
        fcopy(k).wait()


def exchange(vel, lower, upper, st, forces, owner, cells, counts):
    vm = pl.BlockSpec(memory_space=pltpu.VMEM)
    dma = pltpu.SemaphoreType.DMA
    return pl.pallas_call(
        exchange_kernel,
        out_shape=(
            jax.ShapeDtypeStruct((2, 3, SZ, NX), F32),
            jax.ShapeDtypeStruct((NW, 2, 3, 8, 128), F32),
            jax.ShapeDtypeStruct((8, RY, 128), F32),
            jax.ShapeDtypeStruct((256, 128), F32),
            jax.ShapeDtypeStruct((128, SLOTS), jnp.int32),
        ),
        in_specs=[pl.BlockSpec(memory_space=pl.ANY)] + [vm] * 6
        + [pl.BlockSpec(memory_space=pltpu.SMEM)],
        out_specs=[vm] * 5,
        scratch_shapes=[
            pltpu.VMEM((3, RY, SZ, NX), F32),
            pltpu.VMEM((NW, 2, 3, 8, 128), F32),
            pltpu.VMEM((NW, 2, 3, 8, 128), F32),
            pltpu.VMEM((NW, 2, 3, 8, 128), F32),
            pltpu.VMEM((NW, 3, 8, 128), F32),
            pltpu.VMEM((NW, 3, 8, 128), F32),
            pltpu.VMEM((8, 128), F32),
            pltpu.VMEM((2, 8, 128), F32),
            pltpu.VMEM((2, NW * NS, 128), F32),
            pltpu.VMEM((2, NW * NS, 128), F32),
            pltpu.VMEM((NW, 2, NS, 128), F32),
            pltpu.VMEM((NW, 2, NS, 128), F32),
            pltpu.VMEM((RY, 128), F32),
            pltpu.VMEM((RY, 128), F32),
            pltpu.VMEM((RY, 128), F32),
            pltpu.VMEM((RY, 128), F32),
            pltpu.VMEM((RY, 128), F32),
            pltpu.VMEM((RY, 128), F32),
            pltpu.VMEM((RY + 8, 128), F32),
            pltpu.VMEM((2, RY + 8, 128), F32),
            pltpu.VMEM((6, NW, 128), F32),
            dma((6,)), dma((2,)), dma((2,)), dma((2,)), dma((2,)),
            dma((NW,)), dma((NW,)), dma((NW,)), dma((NW,)),
            dma((NS,)), dma((NS,)), dma((NW,)), dma((NW,)),
        ],
        compiler_params=pltpu.CompilerParams(
            collective_id=0, has_side_effects=True, vmem_limit_bytes=56 << 20
        ),
        name="exchange",
    )(vel, lower, upper, st, forces, owner, cells, counts)


def local_kernel(
    vel, halo, bound, coef, part_t, rows, inv_vol,
    derivative, forcing,
    acc0, acc1, acc2, acc3, even, odd, mixed, vbuf, stage, vsem, dsem, fsem,
):
    def take(c):
        return pltpu.make_async_copy(vel.at[c], vbuf.at[c], vsem.at[c])

    for c in range(3):
        take(c).start()

    accs = (acc0, acc1, acc2, acc3)
    zeros = jnp.zeros((128, 128), F32)

    @pl.loop(0, 128)
    def _(i):
        at = pl.ds(pl.multiple_of(i * 128, 128), 128)
        for acc in accs:
            acc[at, :] = zeros

    lane = lax.broadcasted_iota(jnp.int32, (8, 128), 1).astype(F32)

    def spread(source, to):
        pick = jnp.full((8, 128), source, jnp.int32)
        for g in range(SLOTS // 8):
            xl = jnp.take_along_axis(part_t[192 + g * 8 : 200 + g * 8, :], pick, axis=1)
            hit = xl == lane
            for c in range(3):
                r0 = c * SLOTS + g * 8
                f = jnp.take_along_axis(part_t[r0 : r0 + 8, :], pick, axis=1)
                to[r0 : r0 + 8, :] = jnp.where(hit, f, 0.0)

    def add(source, frm):
        for r in range(SLOTS):
            at = pl.ds(pl.multiple_of(rows[source, r], 4), 4)
            accs[r % 4][at, :] += frm[pl.ds(r, 4, stride=SLOTS), :]

    even[192:256, :] = jnp.zeros((64, 128), F32)
    odd[192:256, :] = jnp.zeros((64, 128), F32)
    spread(0, even)

    @pl.loop(0, 64)
    def _(i):
        spread(2 * i + 1, odd)
        add(2 * i, even)
        spread(jnp.minimum(2 * i + 2, 127), even)
        add(2 * i + 1, odd)

    def put_f(b):
        part = (slice(None), pl.ds(b * 4, 4))
        return pltpu.make_async_copy(stage.at[part], forcing.at[part], fsem.at[b])

    @pl.loop(0, 8)
    def _(b):
        @pl.loop(0, 8)
        def _(jh):
            j, h = b * 4 + jh // 2, jh % 2
            scale = -inv_vol[j]
            cells = pl.ds(pl.multiple_of(h * 8, 8), 8)
            for x in range(8):
                at = pl.ds(pl.multiple_of(((j * 2 + h) * 8 + x) * 32, 32), 32)
                mixed[x * 32 : x * 32 + 32, :] = scale * (
                    (acc0[at, :] + acc1[at, :]) + (acc2[at, :] + acc3[at, :])
                )
            for x in range(8):
                for c in range(3):
                    stage[c, j, cells, x * 128 : x * 128 + 128] = mixed[
                        pl.ds(x * 32 + c, 8, stride=4), :
                    ]

        put_f(b).start()

    def put_d(c, x):
        part = (c, slice(None), slice(None), pl.ds(x * 512, 512))
        return pltpu.make_async_copy(vbuf.at[part], derivative.at[part], dsem.at[c * 2 + x])

    for c in range(3):
        take(c).wait()
        for half in range(2):

            @pl.loop(0, 4)
            def _(xx):
                x = half * 4 + xx
                cols = pl.ds(pl.multiple_of(x * 128, 128), 128)

                def row(i):
                    if i < -1 or i > RY:
                        return None
                    if i == -1:
                        return halo[0, c, :, cols]
                    if i == RY:
                        return halo[1, c, :, cols]
                    return vbuf[c, i, :, cols]

                def edge(way):
                    return jnp.concatenate([bound[x, way, c], bound[8 + x, way, c]], axis=0)

                window = [row(i) for i in range(-2, 3)]
                prev = None
                for j in range(RY):
                    total = None
                    for m in range(5):
                        if window[m] is None or j + m - 2 == -1 and j == 0:
                            continue
                        if j + m - 2 == RY and j == RY - 1:
                            continue
                        term = coef[m, j : j + 1, :] * window[m]
                        total = term if total is None else total + term
                    if j == 0:
                        total = total + coef[7, 0:1, :] * edge(0)
                    if j == RY - 1:
                        total = total + coef[7, RY - 1 : RY, :] * edge(1)
                    if j > 0:
                        total = total - coef[5, j : j + 1, :] * prev
                    prev = total
                    window = window[1:] + [row(j + 3)]
                    vbuf[c, j, :, cols] = total
                for j in range(RY - 2, -1, -1):
                    prev = vbuf[c, j, :, cols] - coef[6, j : j + 1, :] * prev
                    vbuf[c, j, :, cols] = prev

            put_d(c, half).start()

    for c in range(3):
        for half in range(2):
            put_d(c, half).wait()

    @pl.loop(0, 8)
    def _(b):
        put_f(b).wait()


def local(vel, halo, bound, coef, part_t, rows, inv_vol):
    sm = pl.BlockSpec(memory_space=pltpu.SMEM)
    vm = pl.BlockSpec(memory_space=pltpu.VMEM)
    hbm = pl.BlockSpec(memory_space=pl.ANY)
    depth = RY * SZ * NX // 128 * 4
    whole = (3, RY, SZ, NX)
    return pl.pallas_call(
        local_kernel,
        out_shape=(jax.ShapeDtypeStruct(whole, F32), jax.ShapeDtypeStruct(whole, F32)),
        in_specs=[hbm, vm, vm, vm, vm, sm, sm],
        out_specs=(hbm, hbm),
        scratch_shapes=[pltpu.VMEM((depth, 128), F32)] * 4
        + [pltpu.VMEM((256, 128), F32)] * 3
        + [pltpu.VMEM(whole, F32)] * 2
        + [pltpu.SemaphoreType.DMA((n,)) for n in (3, 6, 8)],
        compiler_params=pltpu.CompilerParams(vmem_limit_bytes=58 << 20),
        name="local",
    )(vel, halo, bound, coef, part_t, rows, inv_vol)


def body(velocity, lower, upper, stencil, inv_volume, forces, owner, cells, counts):
    halo, bound, coef, part_t, rows = exchange(
        velocity, lower.reshape(1, -1), upper.reshape(1, -1), stencil, forces,
        owner.reshape(1, -1), cells.reshape(1, -1), counts,
    )
    derivative, forcing = local(velocity, halo, bound, coef, part_t, rows, inv_volume)
    return derivative, forcing


def solution(mesh):
    in_specs = (
        P(None, "wall", "span", None),
        P(),
        P(),
        P(None, "wall"),
        P("wall"),
        P(None, ("wall", "span")),
        P(("wall", "span"), None),
        P(("wall", "span")),
        P(("wall", "span")),
    )
    out_specs = (P(None, "wall", "span", None), P(None, "wall", "span", None))
    return jax.shard_map(body, mesh=mesh, in_specs=in_specs, out_specs=out_specs, check_vma=False)
```

```python
import functools

import jax
import jax.numpy as jnp
from jax import lax
from jax.experimental import pallas as pl
from jax.experimental.pallas import tpu as pltpu
from jax.sharding import PartitionSpec as P

F32 = jnp.float32
MESH = pl.DeviceIdType.MESH
NW, NS = 16, 8
RY, SZ, NX = 32, 16, 1024
SLOTS = 64


def exchange_kernel(
    vel, lower_h, upper_h, st_h, forces_h, owner_h, cells_h, counts_h,
    halo_h, bound, coef_h, part_h, rows_h,
    lower, upper, st, forces, owner, cells, counts, halo, coef, part_t, rows_v,
    vbuf, send_a, recv_a, send_f, elim, pbuf, tile_out, tile_in,
    pack, recv1, pack2, recv2,
    lmat, umat, dmat, cmat, ymat, zmat, wmat, wgt, red,
    isem, osem, vsem, hs, hr, ts, tr, as_, ar, fs, fr, p1s, p1r, p2s, p2r,
):
    me_w = lax.axis_index("wall")
    me_s = lax.axis_index("span")

    def vcopy(c, h):
        part = (c, slice(None), pl.ds(h * 8, 8), slice(None))
        return pltpu.make_async_copy(vel.at[part], vbuf.at[part], vsem.at[c * 2 + h])

    barrier = pltpu.get_barrier_semaphore()

    @pl.loop(1, NW)
    def _(k):
        pl.semaphore_signal(
            barrier, inc=1, device_id=(lax.rem(me_w + k, NW), me_s), device_id_type=MESH
        )

    @pl.loop(1, NS)
    def _(k):
        pl.semaphore_signal(
            barrier, inc=1, device_id=(me_w, lax.rem(me_s + k, NS)), device_id_type=MESH
        )

    staged = (
        (st_h, st), (lower_h, lower), (upper_h, upper),
        (forces_h, forces), (owner_h, owner), (cells_h, cells), (counts_h, counts),
    )
    loads = [
        pltpu.make_async_copy(src, dst, isem.at[i]) for i, (src, dst) in enumerate(staged)
    ]
    for i in range(3):
        loads[i].start()
    for c in range(3):
        for h in range(2):
            vcopy(c, h).start()
    for i in range(3, 7):
        loads[i].start()
    pl.semaphore_wait(barrier, NW - 1 + NS - 1)

    above = lax.rem(me_w + 1, NW)
    under = lax.rem(me_w + NW - 1, NW)

    def hcopy(way):
        return pltpu.make_async_remote_copy(
            src_ref=vel.at[:, RY - 1] if way == 0 else vel.at[:, 0],
            dst_ref=halo.at[way],
            send_sem=hs.at[way],
            recv_sem=hr.at[way],
            device_id=(above if way == 0 else under, me_s),
            device_id_type=MESH,
        )

    hcopy(0).start()
    hcopy(1).start()

    for i in range(3):
        loads[i].wait()
    eye = lax.broadcasted_iota(jnp.int32, (RY, RY), 0) == lax.broadcasted_iota(
        jnp.int32, (RY, RY), 1
    )

    def column(row, mask, n):
        full = jnp.broadcast_to(row, (n, n))
        col = jnp.sum(jnp.where(mask, full, 0.0), axis=1, keepdims=True)
        return jnp.broadcast_to(col, (n, 128))

    stc = [column(st[m : m + 1, :], eye, RY) for m in range(5)]
    tile_out[0:1, :] = stc[0][0:1]
    tile_out[1:2, :] = stc[1][0:1]
    tile_out[2:3, :] = stc[4][RY - 1 : RY]
    tile_out[3:4, :] = stc[3][RY - 1 : RY]
    tile_out[4:8, :] = jnp.zeros((4, 128), F32)

    def tcopy(way):
        return pltpu.make_async_remote_copy(
            src_ref=tile_out,
            dst_ref=tile_in.at[way],
            send_sem=ts.at[way],
            recv_sem=tr.at[way],
            device_id=(above if way == 0 else under, me_s),
            device_id_type=MESH,
        )

    tcopy(0).start()
    tcopy(1).start()

    nn = (((1,), (0,)), ((), ()))
    lane_i = lax.broadcasted_iota(jnp.int32, (RY, NW * RY), 1)
    in_row = (lane_i & (RY - 1)) == lax.broadcasted_iota(jnp.int32, (RY, NW * RY), 0)
    to_slab = (
        lax.broadcasted_iota(jnp.int32, (NW * RY, 128), 0) // RY
        == lax.broadcasted_iota(jnp.int32, (NW * RY, 128), 1)
    ).astype(F32).astype(jnp.bfloat16)
    both = jnp.concatenate(
        [
            jnp.where(in_row, jnp.broadcast_to(v[0:1, :], (RY, NW * RY)), 0.0)
            for v in (lower, upper)
        ],
        axis=0,
    )
    tall = None
    for _part in range(3):
        head = both.astype(jnp.bfloat16)
        both = both - head.astype(F32)
        term = lax.dot_general(head, to_slab, nn, preferred_element_type=F32)
        tall = term if tall is None else tall + term
    lmat[...] = tall[0:RY]
    umat[...] = tall[RY : 2 * RY]

    zero = jnp.zeros((1, 128), F32)
    carry_c, carry_b = zero, None
    for j in range(RY):
        low, upp = lmat[j : j + 1, :], umat[j : j + 1, :]
        inv = 1.0 / (1.0 - low * carry_c) if j > 0 else jnp.ones((1, 128), F32)
        carry_c = upp * inv
        dmat[j : j + 1, :] = inv
        cmat[j : j + 1, :] = carry_c
    binv = [None] * RY
    for j in range(RY - 1, -1, -1):
        if j == RY - 1:
            binv[j] = jnp.ones((1, 128), F32)
        else:
            binv[j] = 1.0 / (
                1.0 - umat[j : j + 1, :] * lmat[j + 1 : j + 2, :] * binv[j + 1]
            )
    y = binv[0]
    ymat[0:1, :] = y
    for j in range(1, RY):
        y = -(umat[j - 1 : j, :] * binv[j]) * y
        ymat[j : j + 1, :] = y
    z = dmat[RY - 1 : RY, :]
    zmat[RY - 1 : RY, :] = z
    for j in range(RY - 2, -1, -1):
        z = -(lmat[j + 1 : j + 2, :] * dmat[j : j + 1, :]) * z
        zmat[j : j + 1, :] = z

    lane16 = lax.broadcasted_iota(jnp.int32, (RY, 128), 1)

    def at_slab(values, slab):
        n = values.shape[0]
        col = jnp.sum(jnp.where(lane16[0:n] == slab, values, 0.0), axis=1, keepdims=True)
        return jnp.broadcast_to(col, (n, 128))

    low_all, upp_all = lmat[...], umat[...]
    inv_own = at_slab(dmat[...], me_w)
    c_own = at_slab(cmat[...], me_w)
    y_own = at_slab(ymat[...], me_w)
    z_own = at_slab(zmat[...], me_w)
    low_own = at_slab(low_all, me_w)
    low_next = at_slab(low_all[0:1], me_w + 1)
    upp_prev = at_slab(upp_all[RY - 1 : RY], me_w - 1)
    has_under = jnp.where(me_w > 0, 1.0, 0.0)
    has_above = jnp.where(me_w < NW - 1, 1.0, 0.0)

    row_i = lax.broadcasted_iota(jnp.int32, (RY, 128), 0)
    kept = [
        jnp.where(row_i == 0, 0.0, jnp.where(row_i == 1, stc[0] * has_under, stc[0])),
        jnp.where(row_i == 0, 0.0, stc[1]),
        stc[2],
        jnp.where(row_i == RY - 1, 0.0, stc[3]),
        jnp.where(
            row_i == RY - 1, 0.0, jnp.where(row_i == RY - 2, stc[4] * has_above, stc[4])
        ),
    ]
    for m in range(5):
        coef[m] = kept[m] * inv_own
    coef[5] = jnp.where(row_i == 0, 0.0, low_own * inv_own)
    coef[6] = c_own
    coef[7] = inv_own
    keep_coef = pltpu.make_async_copy(coef, coef_h, osem.at[0])
    keep_coef.start()

    tcopy(0).wait()
    tcopy(1).wait()
    for way, own, scale in ((0, z_own, low_next), (1, y_own, upp_prev)):
        wmat[...] = jnp.zeros((RY + 8, 128), F32)
        for m in range(5):
            wmat[m + 2 : m + 2 + RY, :] += kept[m] * own
        wgt[way] = wmat[...] * (-scale)
    wgt[0, RY + 2 : RY + 3, :] += tile_in[1, 0:1, :]
    wgt[0, RY + 3 : RY + 4, :] += tile_in[1, 1:2, :]
    wgt[1, 5:6, :] += tile_in[0, 2:3, :]
    wgt[1, 4:5, :] += tile_in[0, 3:4, :]

    eye16 = lax.broadcasted_iota(jnp.int32, (NW, NW), 0) == lax.broadcasted_iota(
        jnp.int32, (NW, NW), 1
    )
    next16 = lax.broadcasted_iota(jnp.int32, (NW, NW), 0) + 1 == lax.broadcasted_iota(
        jnp.int32, (NW, NW), 1
    )
    prev16 = lax.broadcasted_iota(jnp.int32, (NW, NW), 0) - 1 == lax.broadcasted_iota(
        jnp.int32, (NW, NW), 1
    )
    z0 = column(zmat[0:1, 0:NW], eye16, NW)
    z1 = column(zmat[RY - 1 : RY, 0:NW], eye16, NW)
    y0 = column(ymat[0:1, 0:NW], eye16, NW)
    y1 = column(ymat[RY - 1 : RY, 0:NW], eye16, NW)
    low_n = column(low_all[0:1, 0:NW], next16, NW)
    upp_p = column(upp_all[RY - 1 : RY, 0:NW], prev16, NW)
    red[0] = upp_p * y0
    red[1] = low_n * z0
    lz1 = low_n * z1
    uy1 = upp_p * y1
    q = -lz1[0:1]
    for s in range(1, NW):
        dinv = 1.0 / (1.0 + red[0, s : s + 1, :] * q)
        c3 = uy1[s : s + 1] * dinv
        red[2, s : s + 1, :] = q * dinv
        red[3, s : s + 1, :] = dinv
        red[4, s : s + 1, :] = c3
        red[5, s : s + 1, :] = q
        q = red[1, s : s + 1, :] * q * c3 - lz1[s : s + 1]

    for c in range(3):
        for h in range(2):
            vcopy(c, h).wait()

            @pl.loop(0, 2)
            def _(x):
                cols = [
                    pl.ds(pl.multiple_of(x * 512 + b * 128, 128), 128) for b in range(4)
                ]
                up, down = [None] * 4, [None] * 4
                for j in range(RY):
                    wu, wd = wgt[0, j + 4 : j + 5, :], wgt[1, j + 4 : j + 5, :]
                    for b in range(4):
                        u = vbuf[c, j, h * 8 : h * 8 + 8, cols[b]]
                        up[b] = wu * u if j == 0 else up[b] + wu * u
                        down[b] = wd * u if j == 0 else down[b] + wd * u
                for b in range(4):
                    send_a[h * 8 + x * 4 + b, 0, c] = up[b]
                    send_a[h * 8 + x * 4 + b, 1, c] = down[b]

    hcopy(0).wait()
    hcopy(1).wait()
    keep_halo = pltpu.make_async_copy(halo, halo_h, osem.at[1])
    keep_halo.start()
    for h in range(2):

        @pl.loop(0, 8)
        def _(x):
            cols = pl.ds(pl.multiple_of(x * 128, 128), 128)
            for c in range(3):
                lo = halo[0, c, h * 8 : h * 8 + 8, cols]
                hi = halo[1, c, h * 8 : h * 8 + 8, cols]
                for way in range(2):
                    send_a[h * 8 + x, way, c] += (
                        wgt[way, 3:4, :] * lo + wgt[way, RY + 4 : RY + 5, :] * hi
                    )

    def acopy(k):
        to = lax.rem(me_w + k, NW)
        return pltpu.make_async_remote_copy(
            src_ref=send_a.at[to],
            dst_ref=recv_a.at[me_w],
            send_sem=as_.at[k],
            recv_sem=ar.at[k],
            device_id=(to, me_s),
            device_id_type=MESH,
        )

    for k in range(1, NW):
        acopy(k).start()
    recv_a[me_w] = send_a[me_w]

    for i in range(3, 7):
        loads[i].wait()
    count = counts[0]
    pack[...] = jnp.zeros((2, NW * NS, 128), F32)
    up_i = lax.broadcasted_iota(jnp.int32, (256, 256), 0)
    up_j = lax.broadcasted_iota(jnp.int32, (256, 256), 1)
    before = (up_i < up_j).astype(F32).astype(jnp.bfloat16)
    ones = jnp.ones((256, 256), jnp.bfloat16)
    ids = lax.broadcasted_iota(jnp.int32, (NW * NS, 256), 0)
    ranks = lax.broadcasted_iota(jnp.int32, (SLOTS, 256), 0).astype(F32)
    lanes = lax.broadcasted_iota(jnp.int32, (1, 256), 1)
    nt = (((1,), (1,)), ((), ()))

    def pack_block(i, carry):
        at = pl.ds(pl.multiple_of(i * 256, 256), 256)
        own = owner[:, at]
        key = (own & 7) * NW + (own >> 3)
        key = jnp.where(lanes + i * 256 < count, key, 512)
        hit = ids == key
        hot = jnp.where(hit, 1.0, 0.0)
        hot_b = hot.astype(jnp.bfloat16)
        pre = lax.dot_general(hot_b, before, nn, preferred_element_type=F32)
        tot = lax.dot_general(hot_b, ones, nn, preferred_element_type=F32)
        rank = jnp.sum(jnp.where(hit, pre + carry, 0.0), axis=0, keepdims=True)
        place = ranks == rank
        load = [forces[c : c + 1, at] for c in range(3)] + [cells[:, at].astype(F32)]
        sums = None
        for _part in range(3):
            head = [x.astype(jnp.bfloat16).astype(F32) for x in load]
            load = [x - y for x, y in zip(load, head)]
            right = jnp.concatenate(
                [jnp.where(place, y, 0.0) for y in head], axis=0
            ).astype(jnp.bfloat16)
            term = lax.dot_general(hot_b, right, nt, preferred_element_type=F32)
            sums = term if sums is None else sums + term
        pack[0] += sums[:, 0:128]
        pack[1] += sums[:, 128:256]
        return carry + tot

    lax.fori_loop(
        0, owner.shape[1] // 256, pack_block, jnp.zeros((NW * NS, 256), F32), unroll=4
    )

    def p1copy(k):
        to = lax.rem(me_s + k, NS)
        return pltpu.make_async_remote_copy(
            src_ref=pack.at[:, pl.ds(pl.multiple_of(to * NW, NW), NW)],
            dst_ref=recv1.at[:, pl.ds(pl.multiple_of(me_s * NW, NW), NW)],
            send_sem=p1s.at[k],
            recv_sem=p1r.at[k],
            device_id=(me_w, to),
            device_id_type=MESH,
        )

    for k in range(1, NS):
        p1copy(k).start()
    mine = pl.ds(pl.multiple_of(me_s * NW, NW), NW)
    recv1[:, mine, :] = pack[:, mine, :]

    for k in range(1, NS):
        p1copy(k).wait()
    for w in range(NW):
        for b in range(2):
            pack2[w, b] = recv1[b, pl.ds(w, NS, stride=NW), :]

    def p2copy(k):
        to = lax.rem(me_w + k, NW)
        return pltpu.make_async_remote_copy(
            src_ref=pack2.at[to],
            dst_ref=recv2.at[me_w],
            send_sem=p2s.at[k],
            recv_sem=p2r.at[k],
            device_id=(to, me_s),
            device_id_type=MESH,
        )

    for k in range(1, NW):
        p2copy(k).start()
    recv2[me_w] = pack2[me_w]

    for k in range(1, NW):
        acopy(k).wait()

    p = recv_a[0, 0]
    for s in range(1, NW):
        pbuf[s] = p
        e = recv_a[s, 1] - red[0, s : s + 1, :] * p
        elim[s] = e
        if s < NW - 1:
            p = recv_a[s, 0] - red[1, s : s + 1, :] * (p + red[2, s : s + 1, :] * e)
    down = jnp.zeros((3, 8, 128), F32)
    send_f[NW - 1, 1] = down
    for s in range(NW - 1, 0, -1):
        down = red[3, s : s + 1, :] * elim[s] - red[4, s : s + 1, :] * down
        send_f[s - 1, 1] = down
        send_f[s, 0] = pbuf[s] + red[5, s : s + 1, :] * down
    send_f[0, 0] = jnp.zeros((3, 8, 128), F32)

    def fcopy(k):
        to = lax.rem(me_w + k, NW)
        return pltpu.make_async_remote_copy(
            src_ref=send_f.at[to],
            dst_ref=bound.at[me_w],
            send_sem=fs.at[k],
            recv_sem=fr.at[k],
            device_id=(to, me_s),
            device_id_type=MESH,
        )

    for k in range(1, NW):
        fcopy(k).start()
    keep_own = pltpu.make_async_copy(send_f.at[me_w], bound.at[me_w], osem.at[2])
    keep_own.start()

    for k in range(1, NW):
        p2copy(k).wait()
    part_t[0:128, :] = recv2[:, 0].reshape(NW * NS, 128).T
    rest = recv2[:, 1].reshape(NW * NS, 128)
    flipped = rest.T
    part_t[128:192, :] = flipped[0:64]
    part_t[192:256, :] = (flipped[64:128].astype(jnp.int32) & 127).astype(F32)
    place = rest.astype(jnp.int32)
    rows_v[...] = (
        (place >> 13) * 64 + ((place >> 7) & 7) * 8 + ((place >> 10) & 7)
    ) * 4
    keep_part = pltpu.make_async_copy(part_t, part_h, osem.at[3])
    keep_part.start()
    keep_rows = pltpu.make_async_copy(rows_v, rows_h, osem.at[4])
    keep_rows.start()

    for k in range(1, NW):
        fcopy(k).wait()
    for keep in (keep_coef, keep_halo, keep_own, keep_part, keep_rows):
        keep.wait()


def exchange(vel, lower, upper, st, forces, owner, cells, counts):
    hbm = pl.BlockSpec(memory_space=pl.ANY)
    dma = pltpu.SemaphoreType.DMA
    return pl.pallas_call(
        exchange_kernel,
        out_shape=(
            jax.ShapeDtypeStruct((2, 3, SZ, NX), F32),
            jax.ShapeDtypeStruct((NW, 2, 3, 8, 128), F32),
            jax.ShapeDtypeStruct((8, RY, 128), F32),
            jax.ShapeDtypeStruct((256, 128), F32),
            jax.ShapeDtypeStruct((128, 128), jnp.int32),
        ),
        in_specs=[hbm] * 8,
        out_specs=[hbm] * 5,
        scratch_shapes=[
            pltpu.VMEM((1, NW * RY), F32),
            pltpu.VMEM((1, NW * RY), F32),
            pltpu.VMEM(st.shape, F32),
            pltpu.VMEM(forces.shape, F32),
            pltpu.VMEM(owner.shape, jnp.int32),
            pltpu.VMEM(cells.shape, jnp.int32),
            pltpu.SMEM((1,), jnp.int32),
            pltpu.VMEM((2, 3, SZ, NX), F32),
            pltpu.VMEM((8, RY, 128), F32),
            pltpu.VMEM((256, 128), F32),
            pltpu.VMEM((128, 128), jnp.int32),
            pltpu.VMEM((3, RY, SZ, NX), F32),
            pltpu.VMEM((NW, 2, 3, 8, 128), F32),
            pltpu.VMEM((NW, 2, 3, 8, 128), F32),
            pltpu.VMEM((NW, 2, 3, 8, 128), F32),
            pltpu.VMEM((NW, 3, 8, 128), F32),
            pltpu.VMEM((NW, 3, 8, 128), F32),
            pltpu.VMEM((8, 128), F32),
            pltpu.VMEM((2, 8, 128), F32),
            pltpu.VMEM((2, NW * NS, 128), F32),
            pltpu.VMEM((2, NW * NS, 128), F32),
            pltpu.VMEM((NW, 2, NS, 128), F32),
            pltpu.VMEM((NW, 2, NS, 128), F32),
            pltpu.VMEM((RY, 128), F32),
            pltpu.VMEM((RY, 128), F32),
            pltpu.VMEM((RY, 128), F32),
            pltpu.VMEM((RY, 128), F32),
            pltpu.VMEM((RY, 128), F32),
            pltpu.VMEM((RY, 128), F32),
            pltpu.VMEM((RY + 8, 128), F32),
            pltpu.VMEM((2, RY + 8, 128), F32),
            pltpu.VMEM((6, NW, 128), F32),
            dma((7,)), dma((5,)), dma((6,)), dma((2,)), dma((2,)), dma((2,)), dma((2,)),
            dma((NW,)), dma((NW,)), dma((NW,)), dma((NW,)),
            dma((NS,)), dma((NS,)), dma((NW,)), dma((NW,)),
        ],
        compiler_params=pltpu.CompilerParams(
            collective_id=0, has_side_effects=True, vmem_limit_bytes=56 << 20
        ),
        name="exchange",
    )(vel, lower, upper, st, forces, owner, cells, counts)


def local_kernel(
    vel, halo_h, bound_h, coef_h, part_h, rows_h, inv_vol,
    derivative, forcing,
    halo, bound, coef, part_t, rows,
    acc0, acc1, acc2, acc3, even, odd, mixed, vbuf, stage, isem, vsem, dsem, fsem,
):
    def take(c):
        return pltpu.make_async_copy(vel.at[c], vbuf.at[c], vsem.at[c])

    staged = ((coef_h, coef), (bound_h, bound), (halo_h, halo), (part_h, part_t), (rows_h, rows))
    loads = [
        pltpu.make_async_copy(src, dst, isem.at[i]) for i, (src, dst) in enumerate(staged)
    ]
    for i in range(3):
        loads[i].start()
    for c in range(3):
        take(c).start()
    loads[3].start()
    loads[4].start()

    accs = (acc0, acc1, acc2, acc3)
    zeros = jnp.zeros((128, 128), F32)

    @pl.loop(0, 128)
    def _(i):
        at = pl.ds(pl.multiple_of(i * 128, 128), 128)
        for acc in accs:
            acc[at, :] = zeros

    def put_d(c, x):
        part = (c, slice(None), slice(None), pl.ds(x * 512, 512))
        return pltpu.make_async_copy(vbuf.at[part], derivative.at[part], dsem.at[c * 2 + x])

    for i in range(3):
        loads[i].wait()
    for c in range(3):
        take(c).wait()
        for half in range(2):

            @pl.loop(0, 4)
            def _(xx):
                x = half * 4 + xx
                cols = pl.ds(pl.multiple_of(x * 128, 128), 128)

                def row(i):
                    if i < -1 or i > RY:
                        return None
                    if i == -1:
                        return halo[0, c, :, cols]
                    if i == RY:
                        return halo[1, c, :, cols]
                    return vbuf[c, i, :, cols]

                def edge(way):
                    return jnp.concatenate([bound[x, way, c], bound[8 + x, way, c]], axis=0)

                window = [row(i) for i in range(-2, 3)]
                prev = None
                for j in range(RY):
                    total = None
                    for m in range(5):
                        if window[m] is None or j + m - 2 == -1 and j == 0:
                            continue
                        if j + m - 2 == RY and j == RY - 1:
                            continue
                        term = coef[m, j : j + 1, :] * window[m]
                        total = term if total is None else total + term
                    if j == 0:
                        total = total + coef[7, 0:1, :] * edge(0)
                    if j == RY - 1:
                        total = total + coef[7, RY - 1 : RY, :] * edge(1)
                    if j > 0:
                        total = total - coef[5, j : j + 1, :] * prev
                    prev = total
                    window = window[1:] + [row(j + 3)]
                    vbuf[c, j, :, cols] = total
                for j in range(RY - 2, -1, -1):
                    prev = vbuf[c, j, :, cols] - coef[6, j : j + 1, :] * prev
                    vbuf[c, j, :, cols] = prev

            put_d(c, half).start()

    lane = lax.broadcasted_iota(jnp.int32, (8, 128), 1).astype(F32)

    def spread(source, to):
        pick = jnp.full((8, 128), source, jnp.int32)
        for g in range(SLOTS // 8):
            xl = jnp.take_along_axis(part_t[192 + g * 8 : 200 + g * 8, :], pick, axis=1)
            hit = xl == lane
            for c in range(3):
                r0 = c * SLOTS + g * 8
                f = jnp.take_along_axis(part_t[r0 : r0 + 8, :], pick, axis=1)
                to[pl.ds(g * 32 + c, 8, stride=4), :] = jnp.where(hit, f, 0.0)

    def add(source, frm):
        base = source * 128 + SLOTS
        for r in range(SLOTS):
            at = pl.ds(pl.multiple_of(rows[base + r], 4), 4)
            accs[r % 4][at, :] += frm[r * 4 : r * 4 + 4, :]

    even[...] = jnp.zeros((256, 128), F32)
    odd[...] = jnp.zeros((256, 128), F32)
    loads[3].wait()
    loads[4].wait()
    spread(0, even)

    @pl.loop(0, 64)
    def _(i):
        spread(2 * i + 1, odd)
        add(2 * i, even)
        spread(jnp.minimum(2 * i + 2, 127), even)
        add(2 * i + 1, odd)

    def put_f(b):
        part = (slice(None), pl.ds(b * 4, 4))
        return pltpu.make_async_copy(stage.at[part], forcing.at[part], fsem.at[b])

    @pl.loop(0, 8)
    def _(b):
        @pl.loop(0, 8)
        def _(jh):
            j, h = b * 4 + jh // 2, jh % 2
            scale = -inv_vol[j]
            cells = pl.ds(pl.multiple_of(h * 8, 8), 8)
            for x in range(8):
                at = pl.ds(pl.multiple_of(((j * 2 + h) * 8 + x) * 32, 32), 32)
                mixed[x * 32 : x * 32 + 32, :] = scale * (
                    (acc0[at, :] + acc1[at, :]) + (acc2[at, :] + acc3[at, :])
                )
            for x in range(8):
                for c in range(3):
                    stage[c, j, cells, x * 128 : x * 128 + 128] = mixed[
                        pl.ds(x * 32 + c, 8, stride=4), :
                    ]

        put_f(b).start()

    for c in range(3):
        for half in range(2):
            put_d(c, half).wait()

    @pl.loop(0, 8)
    def _(b):
        put_f(b).wait()


def local(vel, halo, bound, coef, part_t, rows, inv_vol):
    sm = pl.BlockSpec(memory_space=pltpu.SMEM)
    hbm = pl.BlockSpec(memory_space=pl.ANY)
    depth = RY * SZ * NX // 128 * 4
    whole = (3, RY, SZ, NX)
    return pl.pallas_call(
        local_kernel,
        out_shape=(jax.ShapeDtypeStruct(whole, F32), jax.ShapeDtypeStruct(whole, F32)),
        in_specs=[hbm] * 6 + [sm],
        out_specs=(hbm, hbm),
        scratch_shapes=[
            pltpu.VMEM(halo.shape, F32),
            pltpu.VMEM(bound.shape, F32),
            pltpu.VMEM(coef.shape, F32),
            pltpu.VMEM(part_t.shape, F32),
            pltpu.SMEM(rows.shape, jnp.int32),
        ]
        + [pltpu.VMEM((depth, 128), F32)] * 4
        + [pltpu.VMEM((256, 128), F32)] * 3
        + [pltpu.VMEM(whole, F32)] * 2
        + [pltpu.SemaphoreType.DMA((n,)) for n in (5, 3, 6, 8)],
        compiler_params=pltpu.CompilerParams(vmem_limit_bytes=58 << 20),
        name="local",
    )(vel, halo, bound, coef, part_t, rows, inv_vol)


def body(velocity, lower, upper, stencil, inv_volume, forces, owner, cells, counts):
    halo, bound, coef, part_t, rows = exchange(
        velocity, lower.reshape(1, -1), upper.reshape(1, -1), stencil, forces,
        owner.reshape(1, -1), cells.reshape(1, -1), counts,
    )
    derivative, forcing = local(
        velocity, halo, bound, coef, part_t, rows.reshape(-1), inv_volume
    )
    return derivative, forcing


def solution(mesh):
    in_specs = (
        P(None, "wall", "span", None),
        P(),
        P(),
        P(None, "wall"),
        P("wall"),
        P(None, ("wall", "span")),
        P(("wall", "span"), None),
        P(("wall", "span")),
        P(("wall", "span")),
    )
    out_specs = (P(None, "wall", "span", None), P(None, "wall", "span", None))
    return jax.shard_map(body, mesh=mesh, in_specs=in_specs, out_specs=out_specs, check_vma=False)
```

```python
import functools

import jax
import jax.numpy as jnp
from jax import lax
from jax.experimental import pallas as pl
from jax.experimental.pallas import tpu as pltpu
from jax.sharding import PartitionSpec as P

F32 = jnp.float32
MESH = pl.DeviceIdType.MESH
NW, NS = 16, 8
RY, SZ, NX = 32, 16, 1024
SLOTS = 64


def exchange_kernel(
    vel, lower_h, upper_h, st_h, forces_h, owner_h, cells_h, counts_h,
    halo_h, bound, coef_h, part_h, rows_h,
    lower, upper, st, forces, owner, cells, counts, halo, coef, part_t, rows_v,
    key_row, left, right, vbuf, send_a, recv_a, send_f, elim, pbuf, tile_out, tile_in,
    pack, recv1, pack2, recv2,
    lmat, umat, dmat, cmat, ymat, zmat, wmat, wgt, red,
    isem, osem, vsem, hs, hr, ts, tr, as_, ar, fs, fr, p1s, p1r, p2s, p2r,
):
    me_w = lax.axis_index("wall")
    me_s = lax.axis_index("span")

    def wait_all(src, dst, sent, got):
        group = pltpu.make_async_remote_copy(
            src_ref=src,
            dst_ref=dst,
            send_sem=sent.at[0],
            recv_sem=got.at[0],
            device_id=(me_w, me_s),
            device_id_type=MESH,
        )
        group.wait_send()
        group.wait_recv()

    def vcopy(c, h):
        part = (c, slice(None), pl.ds(h * 8, 8), slice(None))
        return pltpu.make_async_copy(vel.at[part], vbuf.at[part], vsem.at[c * 2 + h])

    barrier = pltpu.get_barrier_semaphore()

    @pl.loop(1, NW)
    def _(k):
        pl.semaphore_signal(
            barrier, inc=1, device_id=(lax.rem(me_w + k, NW), me_s), device_id_type=MESH
        )

    @pl.loop(1, NS)
    def _(k):
        pl.semaphore_signal(
            barrier, inc=1, device_id=(me_w, lax.rem(me_s + k, NS)), device_id_type=MESH
        )

    staged = (
        (st_h, st), (lower_h, lower), (upper_h, upper),
        (forces_h, forces), (owner_h, owner), (cells_h, cells), (counts_h, counts),
    )
    loads = [
        pltpu.make_async_copy(src, dst, isem.at[i]) for i, (src, dst) in enumerate(staged)
    ]
    for i in range(3):
        loads[i].start()
    for c in range(3):
        for h in range(2):
            vcopy(c, h).start()
    for i in range(3, 7):
        loads[i].start()
    for i in range(3):
        loads[i].wait()
    eye = lax.broadcasted_iota(jnp.int32, (RY, RY), 0) == lax.broadcasted_iota(
        jnp.int32, (RY, RY), 1
    )

    def column(row, mask, n):
        full = jnp.broadcast_to(row, (n, n))
        col = jnp.sum(jnp.where(mask, full, 0.0), axis=1, keepdims=True)
        return jnp.broadcast_to(col, (n, 128))

    stc = [column(st[m : m + 1, :], eye, RY) for m in range(5)]
    tile_out[0:1, :] = stc[0][0:1]
    tile_out[1:2, :] = stc[1][0:1]
    tile_out[2:3, :] = stc[4][RY - 1 : RY]
    tile_out[3:4, :] = stc[3][RY - 1 : RY]
    tile_out[4:8, :] = jnp.zeros((4, 128), F32)

    pl.semaphore_wait(barrier, NW - 1 + NS - 1)

    above = lax.rem(me_w + 1, NW)
    under = lax.rem(me_w + NW - 1, NW)

    def tcopy(way):
        return pltpu.make_async_remote_copy(
            src_ref=tile_out,
            dst_ref=tile_in.at[way],
            send_sem=ts.at[way],
            recv_sem=tr.at[way],
            device_id=(above if way == 0 else under, me_s),
            device_id_type=MESH,
        )

    tcopy(0).start()
    tcopy(1).start()

    def hcopy(way):
        return pltpu.make_async_remote_copy(
            src_ref=vel.at[:, RY - 1] if way == 0 else vel.at[:, 0],
            dst_ref=halo.at[way],
            send_sem=hs.at[way],
            recv_sem=hr.at[way],
            device_id=(above if way == 0 else under, me_s),
            device_id_type=MESH,
        )

    hcopy(0).start()
    hcopy(1).start()

    for i in range(3, 7):
        loads[i].wait()
    slots = owner.shape[1]
    nn = (((1,), (0,)), ((), ()))
    own = owner[...]
    live = lax.broadcasted_iota(jnp.int32, (1, slots), 1) < counts[0]
    wall_row = jnp.where(live, own >> 3, NW)
    key_row[0:1, :] = jnp.where(live, (own & 7) * NW + (own >> 3), 512).astype(F32)
    key_row[1:8, :] = jnp.zeros((7, slots), F32)
    in_wall = lax.broadcasted_iota(jnp.int32, (NW, slots), 0) == wall_row
    load = [forces[c : c + 1, :] for c in range(3)] + [cells[...].astype(F32)]
    for part in range(3):
        head = [x.astype(jnp.bfloat16).astype(F32) for x in load]
        load = [x - y for x, y in zip(load, head)]
        for c in range(4):
            r0 = (part * 4 + c) * NW
            left[r0 : r0 + NW, :] = jnp.where(in_wall, head[c], 0.0).astype(jnp.bfloat16)

    lane_f = lax.broadcasted_iota(jnp.int32, (256, 128), 1).astype(F32)
    sub_f = lax.broadcasted_iota(jnp.int32, (256, 128), 0).astype(F32)
    lower_tri = [
        jnp.where(lane_f + 128.0 * b < sub_f, 1.0, 0.0) for b in range(2)
    ]

    def rank_block(i, carry):
        at = pl.ds(pl.multiple_of(i * 256, 256), 256)
        tile = key_row[:, at]
        col = jnp.broadcast_to(tile.T[:, 0:1], (256, 128))
        hit = col == lane_f
        score = jnp.where(hit, carry, 0.0)
        for b in range(2):
            same = col == tile[0:1, b * 128 : b * 128 + 128]
            score = score + jnp.where(same, lower_tri[b], 0.0)
        rank = jnp.sum(score, axis=1, keepdims=True)
        place = jnp.broadcast_to(
            jnp.floor(col[:, 0:1] * (1.0 / NW)) * SLOTS + rank, (256, 128)
        )
        for b in range(4):
            right[at, b * 128 : b * 128 + 128] = jnp.where(
                place == lane_f + 128.0 * b, 1.0, 0.0
            ).astype(jnp.bfloat16)
        return carry + jnp.sum(jnp.where(hit, 1.0, 0.0), axis=0, keepdims=True)

    lax.fori_loop(0, slots // 256, rank_block, jnp.zeros((1, 128), F32), unroll=4)
    made = lax.dot_general(left[...], right[...], nn, preferred_element_type=F32)
    made = made[0:64] + made[64:128] + made[128:192]
    first = lax.broadcasted_iota(jnp.int32, (NW, 128), 1) < SLOTS
    for k in range(NS):
        for b in range(2):
            pair = [
                made[c * NW : c * NW + NW, k // 2 * 128 : k // 2 * 128 + 128]
                for c in (2 * b, 2 * b + 1)
            ]
            turn = 1 - k % 2
            pair[turn] = pltpu.roll(pair[turn], SLOTS, 1)
            pack[b, k * NW : k * NW + NW, :] = jnp.where(first, pair[0], pair[1])

    def p1copy(k):
        to = lax.rem(me_s + k, NS)
        return pltpu.make_async_remote_copy(
            src_ref=pack.at[:, pl.ds(pl.multiple_of(to * NW, NW), NW)],
            dst_ref=recv1.at[:, pl.ds(pl.multiple_of(me_s * NW, NW), NW)],
            send_sem=p1s.at[0],
            recv_sem=p1r.at[0],
            device_id=(me_w, to),
            device_id_type=MESH,
        )

    for k in range(1, NS):
        p1copy(k).start()
    mine = pl.ds(pl.multiple_of(me_s * NW, NW), NW)
    recv1[:, mine, :] = pack[:, mine, :]

    lane_i = lax.broadcasted_iota(jnp.int32, (RY, NW * RY), 1)
    in_row = (lane_i & (RY - 1)) == lax.broadcasted_iota(jnp.int32, (RY, NW * RY), 0)
    to_slab = (
        lax.broadcasted_iota(jnp.int32, (NW * RY, 128), 0) // RY
        == lax.broadcasted_iota(jnp.int32, (NW * RY, 128), 1)
    ).astype(F32).astype(jnp.bfloat16)
    both = jnp.concatenate(
        [
            jnp.where(in_row, jnp.broadcast_to(v[0:1, :], (RY, NW * RY)), 0.0)
            for v in (lower, upper)
        ],
        axis=0,
    )
    tall = None
    for _part in range(3):
        head = both.astype(jnp.bfloat16)
        both = both - head.astype(F32)
        term = lax.dot_general(head, to_slab, nn, preferred_element_type=F32)
        tall = term if tall is None else tall + term
    lmat[...] = tall[0:RY]
    umat[...] = tall[RY : 2 * RY]

    zero = jnp.zeros((1, 128), F32)
    carry_c, carry_b = zero, None
    for j in range(RY):
        low, upp = lmat[j : j + 1, :], umat[j : j + 1, :]
        inv = 1.0 / (1.0 - low * carry_c) if j > 0 else jnp.ones((1, 128), F32)
        carry_c = upp * inv
        dmat[j : j + 1, :] = inv
        cmat[j : j + 1, :] = carry_c
    binv = [None] * RY
    for j in range(RY - 1, -1, -1):
        if j == RY - 1:
            binv[j] = jnp.ones((1, 128), F32)
        else:
            binv[j] = 1.0 / (
                1.0 - umat[j : j + 1, :] * lmat[j + 1 : j + 2, :] * binv[j + 1]
            )
    y = binv[0]
    ymat[0:1, :] = y
    for j in range(1, RY):
        y = -(umat[j - 1 : j, :] * binv[j]) * y
        ymat[j : j + 1, :] = y
    z = dmat[RY - 1 : RY, :]
    zmat[RY - 1 : RY, :] = z
    for j in range(RY - 2, -1, -1):
        z = -(lmat[j + 1 : j + 2, :] * dmat[j : j + 1, :]) * z
        zmat[j : j + 1, :] = z

    lane16 = lax.broadcasted_iota(jnp.int32, (RY, 128), 1)

    def at_slab(values, slab):
        n = values.shape[0]
        col = jnp.sum(jnp.where(lane16[0:n] == slab, values, 0.0), axis=1, keepdims=True)
        return jnp.broadcast_to(col, (n, 128))

    low_all, upp_all = lmat[...], umat[...]
    inv_own = at_slab(dmat[...], me_w)
    c_own = at_slab(cmat[...], me_w)
    y_own = at_slab(ymat[...], me_w)
    z_own = at_slab(zmat[...], me_w)
    low_own = at_slab(low_all, me_w)
    low_next = at_slab(low_all[0:1], me_w + 1)
    upp_prev = at_slab(upp_all[RY - 1 : RY], me_w - 1)
    has_under = jnp.where(me_w > 0, 1.0, 0.0)
    has_above = jnp.where(me_w < NW - 1, 1.0, 0.0)

    row_i = lax.broadcasted_iota(jnp.int32, (RY, 128), 0)
    kept = [
        jnp.where(row_i == 0, 0.0, jnp.where(row_i == 1, stc[0] * has_under, stc[0])),
        jnp.where(row_i == 0, 0.0, stc[1]),
        stc[2],
        jnp.where(row_i == RY - 1, 0.0, stc[3]),
        jnp.where(
            row_i == RY - 1, 0.0, jnp.where(row_i == RY - 2, stc[4] * has_above, stc[4])
        ),
    ]
    for m in range(5):
        coef[m] = kept[m] * inv_own
    coef[5] = jnp.where(row_i == 0, 0.0, low_own * inv_own)
    coef[6] = c_own
    coef[7] = inv_own
    keep_coef = pltpu.make_async_copy(coef, coef_h, osem.at[0])
    keep_coef.start()

    tcopy(0).wait()
    tcopy(1).wait()
    for way, own, scale in ((0, z_own, low_next), (1, y_own, upp_prev)):
        wmat[...] = jnp.zeros((RY + 8, 128), F32)
        for m in range(5):
            wmat[m + 2 : m + 2 + RY, :] += kept[m] * own
        wgt[way] = wmat[...] * (-scale)
    wgt[0, RY + 2 : RY + 3, :] += tile_in[1, 0:1, :]
    wgt[0, RY + 3 : RY + 4, :] += tile_in[1, 1:2, :]
    wgt[1, 5:6, :] += tile_in[0, 2:3, :]
    wgt[1, 4:5, :] += tile_in[0, 3:4, :]

    eye16 = lax.broadcasted_iota(jnp.int32, (NW, NW), 0) == lax.broadcasted_iota(
        jnp.int32, (NW, NW), 1
    )
    next16 = lax.broadcasted_iota(jnp.int32, (NW, NW), 0) + 1 == lax.broadcasted_iota(
        jnp.int32, (NW, NW), 1
    )
    prev16 = lax.broadcasted_iota(jnp.int32, (NW, NW), 0) - 1 == lax.broadcasted_iota(
        jnp.int32, (NW, NW), 1
    )
    z0 = column(zmat[0:1, 0:NW], eye16, NW)
    z1 = column(zmat[RY - 1 : RY, 0:NW], eye16, NW)
    y0 = column(ymat[0:1, 0:NW], eye16, NW)
    y1 = column(ymat[RY - 1 : RY, 0:NW], eye16, NW)
    low_n = column(low_all[0:1, 0:NW], next16, NW)
    upp_p = column(upp_all[RY - 1 : RY, 0:NW], prev16, NW)
    red[0] = upp_p * y0
    red[1] = low_n * z0
    lz1 = low_n * z1
    uy1 = upp_p * y1
    q = -lz1[0:1]
    for s in range(1, NW):
        dinv = 1.0 / (1.0 + red[0, s : s + 1, :] * q)
        c3 = uy1[s : s + 1] * dinv
        red[2, s : s + 1, :] = q * dinv
        red[3, s : s + 1, :] = dinv
        red[4, s : s + 1, :] = c3
        red[5, s : s + 1, :] = q
        q = red[1, s : s + 1, :] * q * c3 - lz1[s : s + 1]

    for c in range(3):
        for h in range(2):
            vcopy(c, h).wait()

            @pl.loop(0, 2)
            def _(x):
                cols = [
                    pl.ds(pl.multiple_of(x * 512 + b * 128, 128), 128) for b in range(4)
                ]
                up, down = [None] * 4, [None] * 4
                for j in range(RY):
                    wu, wd = wgt[0, j + 4 : j + 5, :], wgt[1, j + 4 : j + 5, :]
                    for b in range(4):
                        u = vbuf[c, j, h * 8 : h * 8 + 8, cols[b]]
                        up[b] = wu * u if j == 0 else up[b] + wu * u
                        down[b] = wd * u if j == 0 else down[b] + wd * u
                for b in range(4):
                    send_a[h * 8 + x * 4 + b, 0, c] = up[b]
                    send_a[h * 8 + x * 4 + b, 1, c] = down[b]

    hcopy(0).wait()
    hcopy(1).wait()
    keep_halo = pltpu.make_async_copy(halo, halo_h, osem.at[1])
    keep_halo.start()
    for h in range(2):

        @pl.loop(0, 8)
        def _(x):
            cols = pl.ds(pl.multiple_of(x * 128, 128), 128)
            for c in range(3):
                lo = halo[0, c, h * 8 : h * 8 + 8, cols]
                hi = halo[1, c, h * 8 : h * 8 + 8, cols]
                for way in range(2):
                    send_a[h * 8 + x, way, c] += (
                        wgt[way, 3:4, :] * lo + wgt[way, RY + 4 : RY + 5, :] * hi
                    )

    def acopy(k):
        to = lax.rem(me_w + k, NW)
        return pltpu.make_async_remote_copy(
            src_ref=send_a.at[to],
            dst_ref=recv_a.at[me_w],
            send_sem=as_.at[0],
            recv_sem=ar.at[0],
            device_id=(to, me_s),
            device_id_type=MESH,
        )

    for k in range(1, NW):
        acopy(k).start()
    recv_a[me_w] = send_a[me_w]

    wait_all(pack.at[:, pl.ds(0, NW * (NS - 1))], recv1.at[:, pl.ds(0, NW * (NS - 1))], p1s, p1r)
    for w in range(NW):
        for b in range(2):
            pack2[w, b] = recv1[b, pl.ds(w, NS, stride=NW), :]

    def p2copy(k):
        to = lax.rem(me_w + k, NW)
        return pltpu.make_async_remote_copy(
            src_ref=pack2.at[to],
            dst_ref=recv2.at[me_w],
            send_sem=p2s.at[0],
            recv_sem=p2r.at[0],
            device_id=(to, me_s),
            device_id_type=MESH,
        )

    for k in range(1, NW):
        p2copy(k).start()
    recv2[me_w] = pack2[me_w]

    wait_all(send_a.at[pl.ds(0, NW - 1)], recv_a.at[pl.ds(0, NW - 1)], as_, ar)

    p = recv_a[0, 0]
    for s in range(1, NW):
        pbuf[s] = p
        e = recv_a[s, 1] - red[0, s : s + 1, :] * p
        elim[s] = e
        if s < NW - 1:
            p = recv_a[s, 0] - red[1, s : s + 1, :] * (p + red[2, s : s + 1, :] * e)
    down = jnp.zeros((3, 8, 128), F32)
    send_f[NW - 1, 1] = down
    for s in range(NW - 1, 0, -1):
        down = red[3, s : s + 1, :] * elim[s] - red[4, s : s + 1, :] * down
        send_f[s - 1, 1] = down
        send_f[s, 0] = pbuf[s] + red[5, s : s + 1, :] * down
    send_f[0, 0] = jnp.zeros((3, 8, 128), F32)

    def fcopy(k):
        to = lax.rem(me_w + k, NW)
        return pltpu.make_async_remote_copy(
            src_ref=send_f.at[to],
            dst_ref=bound.at[me_w],
            send_sem=fs.at[0],
            recv_sem=fr.at[0],
            device_id=(to, me_s),
            device_id_type=MESH,
        )

    for k in range(1, NW):
        fcopy(k).start()
    keep_own = pltpu.make_async_copy(send_f.at[me_w], bound.at[me_w], osem.at[2])
    keep_own.start()

    wait_all(pack2.at[pl.ds(0, NW - 1)], recv2.at[pl.ds(0, NW - 1)], p2s, p2r)
    part_t[0:128, :] = recv2[:, 0].reshape(NW * NS, 128).T
    rest = recv2[:, 1].reshape(NW * NS, 128)
    flipped = rest.T
    part_t[128:192, :] = flipped[0:64]
    part_t[192:256, :] = (flipped[64:128].astype(jnp.int32) & 127).astype(F32)
    place = rest.astype(jnp.int32)
    rows_v[...] = (
        (place >> 13) * 64 + ((place >> 7) & 7) * 8 + ((place >> 10) & 7)
    ) * 4
    keep_part = pltpu.make_async_copy(part_t, part_h, osem.at[3])
    keep_part.start()
    keep_rows = pltpu.make_async_copy(rows_v, rows_h, osem.at[4])
    keep_rows.start()

    wait_all(send_f.at[pl.ds(0, NW - 1)], bound.at[pl.ds(0, NW - 1)], fs, fr)
    for keep in (keep_coef, keep_halo, keep_own, keep_part, keep_rows):
        keep.wait()


def exchange(vel, lower, upper, st, forces, owner, cells, counts):
    hbm = pl.BlockSpec(memory_space=pl.ANY)
    dma = pltpu.SemaphoreType.DMA
    return pl.pallas_call(
        exchange_kernel,
        out_shape=(
            jax.ShapeDtypeStruct((2, 3, SZ, NX), F32),
            jax.ShapeDtypeStruct((NW, 2, 3, 8, 128), F32),
            jax.ShapeDtypeStruct((8, RY, 128), F32),
            jax.ShapeDtypeStruct((256, 128), F32),
            jax.ShapeDtypeStruct((128, 128), jnp.int32),
        ),
        in_specs=[hbm] * 8,
        out_specs=[hbm] * 5,
        scratch_shapes=[
            pltpu.VMEM((1, NW * RY), F32),
            pltpu.VMEM((1, NW * RY), F32),
            pltpu.VMEM(st.shape, F32),
            pltpu.VMEM(forces.shape, F32),
            pltpu.VMEM(owner.shape, jnp.int32),
            pltpu.VMEM(cells.shape, jnp.int32),
            pltpu.SMEM((1,), jnp.int32),
            pltpu.VMEM((2, 3, SZ, NX), F32),
            pltpu.VMEM((8, RY, 128), F32),
            pltpu.VMEM((256, 128), F32),
            pltpu.VMEM((128, 128), jnp.int32),
            pltpu.VMEM((8, owner.shape[1]), F32),
            pltpu.VMEM((12 * NW, owner.shape[1]), jnp.bfloat16),
            pltpu.VMEM((owner.shape[1], NS * SLOTS), jnp.bfloat16),
            pltpu.VMEM((3, RY, SZ, NX), F32),
            pltpu.VMEM((NW, 2, 3, 8, 128), F32),
            pltpu.VMEM((NW, 2, 3, 8, 128), F32),
            pltpu.VMEM((NW, 2, 3, 8, 128), F32),
            pltpu.VMEM((NW, 3, 8, 128), F32),
            pltpu.VMEM((NW, 3, 8, 128), F32),
            pltpu.VMEM((8, 128), F32),
            pltpu.VMEM((2, 8, 128), F32),
            pltpu.VMEM((2, NW * NS, 128), F32),
            pltpu.VMEM((2, NW * NS, 128), F32),
            pltpu.VMEM((NW, 2, NS, 128), F32),
            pltpu.VMEM((NW, 2, NS, 128), F32),
            pltpu.VMEM((RY, 128), F32),
            pltpu.VMEM((RY, 128), F32),
            pltpu.VMEM((RY, 128), F32),
            pltpu.VMEM((RY, 128), F32),
            pltpu.VMEM((RY, 128), F32),
            pltpu.VMEM((RY, 128), F32),
            pltpu.VMEM((RY + 8, 128), F32),
            pltpu.VMEM((2, RY + 8, 128), F32),
            pltpu.VMEM((6, NW, 128), F32),
            dma((7,)), dma((5,)), dma((6,)), dma((2,)), dma((2,)), dma((2,)), dma((2,)),
            *[dma((1,))] * 8,
        ],
        compiler_params=pltpu.CompilerParams(
            collective_id=0, has_side_effects=True, vmem_limit_bytes=56 << 20
        ),
        name="exchange",
    )(vel, lower, upper, st, forces, owner, cells, counts)


def local_kernel(
    vel, halo_h, bound_h, coef_h, part_h, rows_h, inv_vol,
    derivative, forcing,
    halo, bound, coef, part_t, rows,
    acc0, acc1, acc2, acc3, even, odd, mixed, vbuf, stage, isem, vsem, dsem, fsem,
):
    def take(c):
        return pltpu.make_async_copy(vel.at[c], vbuf.at[c], vsem.at[c])

    staged = ((coef_h, coef), (bound_h, bound), (halo_h, halo), (part_h, part_t), (rows_h, rows))
    loads = [
        pltpu.make_async_copy(src, dst, isem.at[i]) for i, (src, dst) in enumerate(staged)
    ]
    for i in range(3):
        loads[i].start()
    for c in range(3):
        take(c).start()
    loads[3].start()
    loads[4].start()

    accs = (acc0, acc1, acc2, acc3)
    zeros = jnp.zeros((128, 128), F32)

    @pl.loop(0, 128)
    def _(i):
        at = pl.ds(pl.multiple_of(i * 128, 128), 128)
        for acc in accs:
            acc[at, :] = zeros

    def put_d(c, x):
        part = (c, slice(None), slice(None), pl.ds(x * 512, 512))
        return pltpu.make_async_copy(vbuf.at[part], derivative.at[part], dsem.at[c * 2 + x])

    for i in range(3):
        loads[i].wait()
    for c in range(3):
        take(c).wait()
        for half in range(2):

            @pl.loop(0, 4)
            def _(xx):
                x = half * 4 + xx
                cols = pl.ds(pl.multiple_of(x * 128, 128), 128)

                def row(i):
                    if i < -1 or i > RY:
                        return None
                    if i == -1:
                        return halo[0, c, :, cols]
                    if i == RY:
                        return halo[1, c, :, cols]
                    return vbuf[c, i, :, cols]

                def edge(way):
                    return jnp.concatenate([bound[x, way, c], bound[8 + x, way, c]], axis=0)

                window = [row(i) for i in range(-2, 3)]
                prev = None
                for j in range(RY):
                    total = None
                    for m in range(5):
                        if window[m] is None or j + m - 2 == -1 and j == 0:
                            continue
                        if j + m - 2 == RY and j == RY - 1:
                            continue
                        term = coef[m, j : j + 1, :] * window[m]
                        total = term if total is None else total + term
                    if j == 0:
                        total = total + coef[7, 0:1, :] * edge(0)
                    if j == RY - 1:
                        total = total + coef[7, RY - 1 : RY, :] * edge(1)
                    if j > 0:
                        total = total - coef[5, j : j + 1, :] * prev
                    prev = total
                    window = window[1:] + [row(j + 3)]
                    vbuf[c, j, :, cols] = total
                for j in range(RY - 2, -1, -1):
                    prev = vbuf[c, j, :, cols] - coef[6, j : j + 1, :] * prev
                    vbuf[c, j, :, cols] = prev

            put_d(c, half).start()

    lane = lax.broadcasted_iota(jnp.int32, (8, 128), 1).astype(F32)

    def spread(source, to):
        pick = jnp.full((8, 128), source, jnp.int32)
        for g in range(SLOTS // 8):
            xl = jnp.take_along_axis(part_t[192 + g * 8 : 200 + g * 8, :], pick, axis=1)
            hit = xl == lane
            for c in range(3):
                r0 = c * SLOTS + g * 8
                f = jnp.take_along_axis(part_t[r0 : r0 + 8, :], pick, axis=1)
                to[pl.ds(g * 32 + c, 8, stride=4), :] = jnp.where(hit, f, 0.0)

    def add(source, frm):
        base = source * 128 + SLOTS
        for r in range(SLOTS):
            at = pl.ds(pl.multiple_of(rows[base + r], 4), 4)
            accs[r % 4][at, :] += frm[r * 4 : r * 4 + 4, :]

    even[...] = jnp.zeros((256, 128), F32)
    odd[...] = jnp.zeros((256, 128), F32)
    loads[3].wait()
    loads[4].wait()
    spread(0, even)

    @pl.loop(0, 64)
    def _(i):
        spread(2 * i + 1, odd)
        add(2 * i, even)
        spread(jnp.minimum(2 * i + 2, 127), even)
        add(2 * i + 1, odd)

    def put_f(b):
        part = (slice(None), pl.ds(b * 4, 4))
        return pltpu.make_async_copy(stage.at[part], forcing.at[part], fsem.at[b])

    @pl.loop(0, 8)
    def _(b):
        @pl.loop(0, 8)
        def _(jh):
            j, h = b * 4 + jh // 2, jh % 2
            scale = -inv_vol[j]
            cells = pl.ds(pl.multiple_of(h * 8, 8), 8)
            for x in range(8):
                at = pl.ds(pl.multiple_of(((j * 2 + h) * 8 + x) * 32, 32), 32)
                mixed[x * 32 : x * 32 + 32, :] = scale * (
                    (acc0[at, :] + acc1[at, :]) + (acc2[at, :] + acc3[at, :])
                )
            for x in range(8):
                for c in range(3):
                    stage[c, j, cells, x * 128 : x * 128 + 128] = mixed[
                        pl.ds(x * 32 + c, 8, stride=4), :
                    ]

        put_f(b).start()

    for c in range(3):
        for half in range(2):
            put_d(c, half).wait()

    @pl.loop(0, 8)
    def _(b):
        put_f(b).wait()


def local(vel, halo, bound, coef, part_t, rows, inv_vol):
    sm = pl.BlockSpec(memory_space=pltpu.SMEM)
    hbm = pl.BlockSpec(memory_space=pl.ANY)
    depth = RY * SZ * NX // 128 * 4
    whole = (3, RY, SZ, NX)
    return pl.pallas_call(
        local_kernel,
        out_shape=(jax.ShapeDtypeStruct(whole, F32), jax.ShapeDtypeStruct(whole, F32)),
        in_specs=[hbm] * 6 + [sm],
        out_specs=(hbm, hbm),
        scratch_shapes=[
            pltpu.VMEM(halo.shape, F32),
            pltpu.VMEM(bound.shape, F32),
            pltpu.VMEM(coef.shape, F32),
            pltpu.VMEM(part_t.shape, F32),
            pltpu.SMEM(rows.shape, jnp.int32),
        ]
        + [pltpu.VMEM((depth, 128), F32)] * 4
        + [pltpu.VMEM((256, 128), F32)] * 3
        + [pltpu.VMEM(whole, F32)] * 2
        + [pltpu.SemaphoreType.DMA((n,)) for n in (5, 3, 6, 8)],
        compiler_params=pltpu.CompilerParams(vmem_limit_bytes=58 << 20),
        name="local",
    )(vel, halo, bound, coef, part_t, rows, inv_vol)


def body(velocity, lower, upper, stencil, inv_volume, forces, owner, cells, counts):
    halo, bound, coef, part_t, rows = exchange(
        velocity, lower.reshape(1, -1), upper.reshape(1, -1), stencil, forces,
        owner.reshape(1, -1), cells.reshape(1, -1), counts,
    )
    derivative, forcing = local(
        velocity, halo, bound, coef, part_t, rows.reshape(-1), inv_volume
    )
    return derivative, forcing


def solution(mesh):
    in_specs = (
        P(None, "wall", "span", None),
        P(),
        P(),
        P(None, "wall"),
        P("wall"),
        P(None, ("wall", "span")),
        P(("wall", "span"), None),
        P(("wall", "span")),
        P(("wall", "span")),
    )
    out_specs = (P(None, "wall", "span", None), P(None, "wall", "span", None))
    return jax.shard_map(body, mesh=mesh, in_specs=in_specs, out_specs=out_specs, check_vma=False)
```

```python
import functools

import jax
import jax.numpy as jnp
from jax import lax
from jax.experimental import pallas as pl
from jax.experimental.pallas import tpu as pltpu
from jax.sharding import PartitionSpec as P

F32 = jnp.float32
MESH = pl.DeviceIdType.MESH
NW, NS = 16, 8
RY, SZ, NX = 32, 16, 1024
SLOTS = 64


def exchange_kernel(
    vel, lower_h, upper_h, st_h, forces_h, owner_h, cells_h, counts_h,
    halo_h, bound, coef_h, part_h, rows_h,
    lower, upper, st, forces, owner, cells, counts, halo, coef, part_t, rows_v,
    key_row, left, right, vbuf, send_a, recv_a, send_f, elim, pbuf, tile_out, tile_in,
    pack, recv1, pack2, recv2,
    lmat, umat, dmat, cmat, ymat, zmat, wmat, wgt, red,
    isem, osem, vsem, hs, hr, ts, tr, as_, ar, fs, fr, p1s, p1r, p2s, p2r,
):
    me_w = lax.axis_index("wall")
    me_s = lax.axis_index("span")

    def wait_all(src, dst, sent, got, i=0):
        group = pltpu.make_async_remote_copy(
            src_ref=src,
            dst_ref=dst,
            send_sem=sent.at[i],
            recv_sem=got.at[i],
            device_id=(me_w, me_s),
            device_id_type=MESH,
        )
        group.wait_send()
        group.wait_recv()

    def vcopy(c, h):
        part = (c, slice(None), pl.ds(h * 8, 8), slice(None))
        return pltpu.make_async_copy(vel.at[part], vbuf.at[part], vsem.at[c * 2 + h])

    barrier = pltpu.get_barrier_semaphore()

    @pl.loop(1, NW)
    def _(k):
        pl.semaphore_signal(
            barrier, inc=1, device_id=(lax.rem(me_w + k, NW), me_s), device_id_type=MESH
        )

    @pl.loop(1, NS)
    def _(k):
        pl.semaphore_signal(
            barrier, inc=1, device_id=(me_w, lax.rem(me_s + k, NS)), device_id_type=MESH
        )

    staged = (
        (st_h, st), (lower_h, lower), (upper_h, upper),
        (forces_h, forces), (owner_h, owner), (cells_h, cells), (counts_h, counts),
    )
    loads = [
        pltpu.make_async_copy(src, dst, isem.at[i]) for i, (src, dst) in enumerate(staged)
    ]
    for i in range(3):
        loads[i].start()
    for c in range(3):
        for h in range(2):
            vcopy(c, h).start()
    for i in range(3, 7):
        loads[i].start()
    pl.semaphore_wait(barrier, NW - 1 + NS - 1)

    above = lax.rem(me_w + 1, NW)
    under = lax.rem(me_w + NW - 1, NW)

    def hcopy(way, c):
        return pltpu.make_async_remote_copy(
            src_ref=vel.at[c, RY - 1 if way == 0 else 0],
            dst_ref=halo.at[way, c],
            send_sem=hs.at[way * 3 + c],
            recv_sem=hr.at[way * 3 + c],
            device_id=(above if way == 0 else under, me_s),
            device_id_type=MESH,
        )

    hcopy(0, 0).start()
    hcopy(1, 0).start()

    for i in range(3):
        loads[i].wait()
    eye = lax.broadcasted_iota(jnp.int32, (RY, RY), 0) == lax.broadcasted_iota(
        jnp.int32, (RY, RY), 1
    )

    def column(row, mask, n):
        full = jnp.broadcast_to(row, (n, n))
        col = jnp.sum(jnp.where(mask, full, 0.0), axis=1, keepdims=True)
        return jnp.broadcast_to(col, (n, 128))

    stc = [column(st[m : m + 1, :], eye, RY) for m in range(5)]
    tile_out[0:1, :] = stc[0][0:1]
    tile_out[1:2, :] = stc[1][0:1]
    tile_out[2:3, :] = stc[4][RY - 1 : RY]
    tile_out[3:4, :] = stc[3][RY - 1 : RY]
    tile_out[4:8, :] = jnp.zeros((4, 128), F32)

    def tcopy(way):
        return pltpu.make_async_remote_copy(
            src_ref=tile_out,
            dst_ref=tile_in.at[way],
            send_sem=ts.at[way],
            recv_sem=tr.at[way],
            device_id=(above if way == 0 else under, me_s),
            device_id_type=MESH,
        )

    tcopy(0).start()
    tcopy(1).start()
    for c in (1, 2):
        hcopy(0, c).start()
        hcopy(1, c).start()


    nn = (((1,), (0,)), ((), ()))
    lane_i = lax.broadcasted_iota(jnp.int32, (RY, NW * RY), 1)
    in_row = (lane_i & (RY - 1)) == lax.broadcasted_iota(jnp.int32, (RY, NW * RY), 0)
    to_slab = (
        lax.broadcasted_iota(jnp.int32, (NW * RY, 128), 0) // RY
        == lax.broadcasted_iota(jnp.int32, (NW * RY, 128), 1)
    ).astype(F32).astype(jnp.bfloat16)
    both = jnp.concatenate(
        [
            jnp.where(in_row, jnp.broadcast_to(v[0:1, :], (RY, NW * RY)), 0.0)
            for v in (lower, upper)
        ],
        axis=0,
    )
    tall = None
    for _part in range(3):
        head = both.astype(jnp.bfloat16)
        both = both - head.astype(F32)
        term = lax.dot_general(head, to_slab, nn, preferred_element_type=F32)
        tall = term if tall is None else tall + term
    lmat[...] = tall[0:RY]
    umat[...] = tall[RY : 2 * RY]

    zero = jnp.zeros((1, 128), F32)
    carry_c, carry_b = zero, None
    for j in range(RY):
        low, upp = lmat[j : j + 1, :], umat[j : j + 1, :]
        inv = 1.0 / (1.0 - low * carry_c) if j > 0 else jnp.ones((1, 128), F32)
        carry_c = upp * inv
        dmat[j : j + 1, :] = inv
        cmat[j : j + 1, :] = carry_c
    binv = [None] * RY
    for j in range(RY - 1, -1, -1):
        if j == RY - 1:
            binv[j] = jnp.ones((1, 128), F32)
        else:
            binv[j] = 1.0 / (
                1.0 - umat[j : j + 1, :] * lmat[j + 1 : j + 2, :] * binv[j + 1]
            )
    y = binv[0]
    ymat[0:1, :] = y
    for j in range(1, RY):
        y = -(umat[j - 1 : j, :] * binv[j]) * y
        ymat[j : j + 1, :] = y
    z = dmat[RY - 1 : RY, :]
    zmat[RY - 1 : RY, :] = z
    for j in range(RY - 2, -1, -1):
        z = -(lmat[j + 1 : j + 2, :] * dmat[j : j + 1, :]) * z
        zmat[j : j + 1, :] = z

    lane16 = lax.broadcasted_iota(jnp.int32, (RY, 128), 1)

    def at_slab(values, slab):
        n = values.shape[0]
        col = jnp.sum(jnp.where(lane16[0:n] == slab, values, 0.0), axis=1, keepdims=True)
        return jnp.broadcast_to(col, (n, 128))

    low_all, upp_all = lmat[...], umat[...]
    inv_own = at_slab(dmat[...], me_w)
    c_own = at_slab(cmat[...], me_w)
    y_own = at_slab(ymat[...], me_w)
    z_own = at_slab(zmat[...], me_w)
    low_own = at_slab(low_all, me_w)
    low_next = at_slab(low_all[0:1], me_w + 1)
    upp_prev = at_slab(upp_all[RY - 1 : RY], me_w - 1)
    has_under = jnp.where(me_w > 0, 1.0, 0.0)
    has_above = jnp.where(me_w < NW - 1, 1.0, 0.0)

    row_i = lax.broadcasted_iota(jnp.int32, (RY, 128), 0)
    kept = [
        jnp.where(row_i == 0, 0.0, jnp.where(row_i == 1, stc[0] * has_under, stc[0])),
        jnp.where(row_i == 0, 0.0, stc[1]),
        stc[2],
        jnp.where(row_i == RY - 1, 0.0, stc[3]),
        jnp.where(
            row_i == RY - 1, 0.0, jnp.where(row_i == RY - 2, stc[4] * has_above, stc[4])
        ),
    ]
    for m in range(5):
        coef[m] = kept[m] * inv_own
    coef[5] = jnp.where(row_i == 0, 0.0, low_own * inv_own)
    coef[6] = c_own
    coef[7] = inv_own
    keep_coef = pltpu.make_async_copy(coef, coef_h, osem.at[0])
    keep_coef.start()

    for way, own, scale in ((0, z_own, low_next), (1, y_own, upp_prev)):
        wmat[...] = jnp.zeros((RY + 8, 128), F32)
        for m in range(5):
            wmat[m + 2 : m + 2 + RY, :] += kept[m] * own
        wgt[way] = wmat[...] * (-scale)

    eye16 = lax.broadcasted_iota(jnp.int32, (NW, NW), 0) == lax.broadcasted_iota(
        jnp.int32, (NW, NW), 1
    )
    next16 = lax.broadcasted_iota(jnp.int32, (NW, NW), 0) + 1 == lax.broadcasted_iota(
        jnp.int32, (NW, NW), 1
    )
    prev16 = lax.broadcasted_iota(jnp.int32, (NW, NW), 0) - 1 == lax.broadcasted_iota(
        jnp.int32, (NW, NW), 1
    )
    z0 = column(zmat[0:1, 0:NW], eye16, NW)
    z1 = column(zmat[RY - 1 : RY, 0:NW], eye16, NW)
    y0 = column(ymat[0:1, 0:NW], eye16, NW)
    y1 = column(ymat[RY - 1 : RY, 0:NW], eye16, NW)
    low_n = column(low_all[0:1, 0:NW], next16, NW)
    upp_p = column(upp_all[RY - 1 : RY, 0:NW], prev16, NW)
    red[0] = upp_p * y0
    red[1] = low_n * z0
    lz1 = low_n * z1
    uy1 = upp_p * y1
    q = -lz1[0:1]
    for s in range(1, NW):
        dinv = 1.0 / (1.0 + red[0, s : s + 1, :] * q)
        c3 = uy1[s : s + 1] * dinv
        red[2, s : s + 1, :] = q * dinv
        red[3, s : s + 1, :] = dinv
        red[4, s : s + 1, :] = c3
        red[5, s : s + 1, :] = q
        q = red[1, s : s + 1, :] * q * c3 - lz1[s : s + 1]

    def own_rows(c):
        for h in range(2):
            vcopy(c, h).wait()

            @pl.loop(0, 2)
            def _(x):
                cols = [
                    pl.ds(pl.multiple_of(x * 512 + b * 128, 128), 128) for b in range(4)
                ]
                up, down = [None] * 4, [None] * 4
                for j in range(RY):
                    wu, wd = wgt[0, j + 4 : j + 5, :], wgt[1, j + 4 : j + 5, :]
                    for b in range(4):
                        u = vbuf[c, j, h * 8 : h * 8 + 8, cols[b]]
                        up[b] = wu * u if j == 0 else up[b] + wu * u
                        down[b] = wd * u if j == 0 else down[b] + wd * u
                for b in range(4):
                    send_a[c, h * 8 + x * 4 + b, 0] = up[b]
                    send_a[c, h * 8 + x * 4 + b, 1] = down[b]

    def acopy(c, k):
        to = lax.rem(me_w + k, NW)
        return pltpu.make_async_remote_copy(
            src_ref=send_a.at[c, to],
            dst_ref=recv_a.at[c, me_w],
            send_sem=as_.at[c],
            recv_sem=ar.at[c],
            device_id=(to, me_s),
            device_id_type=MESH,
        )

    def add_ends(c):
        for h in range(2):
            cells8 = slice(h * 8, h * 8 + 8)

            @pl.loop(0, 8)
            def _(x):
                cols = pl.ds(pl.multiple_of(x * 128, 128), 128)
                ends = (halo[0, c, cells8, cols], halo[1, c, cells8, cols])
                near = (
                    (tile_in[1, 0:1, :], RY - 2, tile_in[1, 1:2, :], RY - 1),
                    (tile_in[0, 2:3, :], 1, tile_in[0, 3:4, :], 0),
                )
                for way in range(2):
                    wa, ja, wb, jb = near[way]
                    send_a[c, h * 8 + x, way] += (
                        wgt[way, 3:4, :] * ends[0]
                        + wgt[way, RY + 4 : RY + 5, :] * ends[1]
                        + wa * vbuf[c, ja, cells8, cols]
                        + wb * vbuf[c, jb, cells8, cols]
                    )

    def send_up(c):
        hcopy(0, c).wait()
        hcopy(1, c).wait()
        add_ends(c)
        for k in range(1, NW):
            acopy(c, k).start()
        recv_a[c, me_w] = send_a[c, me_w]

    own_rows(0)
    own_rows(1)
    own_rows(2)

    for i in range(3, 7):
        loads[i].wait()
    slots = owner.shape[1]
    own = owner[...]
    live = lax.broadcasted_iota(jnp.int32, (1, slots), 1) < counts[0]
    wall_row = jnp.where(live, own >> 3, NW)
    key_row[0:1, :] = jnp.where(live, (own & 7) * NW + (own >> 3), 512).astype(F32)
    key_row[1:8, :] = jnp.zeros((7, slots), F32)
    lane_f = lax.broadcasted_iota(jnp.int32, (256, 128), 1).astype(F32)
    sub_f = lax.broadcasted_iota(jnp.int32, (256, 128), 0).astype(F32)
    lower_tri = [
        jnp.where(lane_f + 128.0 * b < sub_f, 1.0, 0.0) for b in range(2)
    ]

    ones = jnp.ones((128, 128), jnp.bfloat16)
    head_row = jnp.where(
        lax.broadcasted_iota(jnp.int32, (8, 128), 0) == 0, 1.0, 0.0
    ).astype(jnp.bfloat16)

    def rank_block(i, carry):
        at = pl.ds(pl.multiple_of(i * 256, 256), 256)
        tile = key_row[:, at]
        col = lax.dot_general(
            tile.T.astype(jnp.bfloat16), head_row, nn, preferred_element_type=F32
        )
        hit = col == lane_f
        score = jnp.where(hit, carry, 0.0)
        for b in range(2):
            same = col == tile[0:1, b * 128 : b * 128 + 128]
            score = score + jnp.where(same, lower_tri[b], 0.0)
        rank = lax.dot_general(
            score.astype(jnp.bfloat16), ones, nn, preferred_element_type=F32
        )
        place = jnp.floor(col * (1.0 / NW)) * SLOTS + rank
        for b in range(4):
            right[at, b * 128 : b * 128 + 128] = jnp.where(
                place == lane_f + 128.0 * b, 1.0, 0.0
            ).astype(jnp.bfloat16)
        return carry + jnp.sum(jnp.where(hit, 1.0, 0.0), axis=0, keepdims=True)

    blocks = slots // 256
    carry = lax.fori_loop(
        0, blocks // 2, rank_block, jnp.zeros((1, 128), F32), unroll=4
    )
    tcopy(0).wait()
    tcopy(1).wait()
    send_up(0)
    lax.fori_loop(blocks // 2, blocks, rank_block, carry, unroll=4)
    in_wall = lax.broadcasted_iota(jnp.int32, (NW, slots), 0) == wall_row
    load = [forces[c : c + 1, :] for c in range(3)] + [cells[...].astype(F32)]
    for part in range(3):
        head = [x.astype(jnp.bfloat16).astype(F32) for x in load]
        load = [x - y for x, y in zip(load, head)]
        for c in range(4):
            r0 = (part * 4 + c) * NW
            left[r0 : r0 + NW, :] = jnp.where(in_wall, head[c], 0.0).astype(jnp.bfloat16)

    made = lax.dot_general(left[...], right[...], nn, preferred_element_type=F32)
    made = made[0:64] + made[64:128] + made[128:192]
    first = lax.broadcasted_iota(jnp.int32, (NW, 128), 1) < SLOTS
    for k in range(NS):
        for b in range(2):
            pair = [
                made[c * NW : c * NW + NW, k // 2 * 128 : k // 2 * 128 + 128]
                for c in (2 * b, 2 * b + 1)
            ]
            turn = 1 - k % 2
            pair[turn] = pltpu.roll(pair[turn], SLOTS, 1)
            pack[b, k * NW : k * NW + NW, :] = jnp.where(first, pair[0], pair[1])

    def p1copy(k):
        to = lax.rem(me_s + k, NS)
        return pltpu.make_async_remote_copy(
            src_ref=pack.at[:, pl.ds(pl.multiple_of(to * NW, NW), NW)],
            dst_ref=recv1.at[:, pl.ds(pl.multiple_of(me_s * NW, NW), NW)],
            send_sem=p1s.at[0],
            recv_sem=p1r.at[0],
            device_id=(me_w, to),
            device_id_type=MESH,
        )

    for k in range(1, NS):
        p1copy(k).start()
    mine = pl.ds(pl.multiple_of(me_s * NW, NW), NW)
    recv1[:, mine, :] = pack[:, mine, :]

    send_up(1)
    send_up(2)
    keep_halo = pltpu.make_async_copy(halo, halo_h, osem.at[1])
    keep_halo.start()

    def solve(c):
        wait_all(send_a.at[c, pl.ds(0, NW - 1)], recv_a.at[c, pl.ds(0, NW - 1)], as_, ar, c)
        p = recv_a[c, 0, 0]
        for s in range(1, NW):
            pbuf[s] = p
            e = recv_a[c, s, 1] - red[0, s : s + 1, :] * p
            elim[s] = e
            if s < NW - 1:
                p = recv_a[c, s, 0] - red[1, s : s + 1, :] * (
                    p + red[2, s : s + 1, :] * e
                )
        down = jnp.zeros((8, 128), F32)
        send_f[c, NW - 1, 1] = down
        for s in range(NW - 1, 0, -1):
            down = red[3, s : s + 1, :] * elim[s] - red[4, s : s + 1, :] * down
            send_f[c, s - 1, 1] = down
            send_f[c, s, 0] = pbuf[s] + red[5, s : s + 1, :] * down
        send_f[c, 0, 0] = jnp.zeros((8, 128), F32)
        for k in range(1, NW):
            fcopy(c, k).start()

    def fcopy(c, k):
        to = lax.rem(me_w + k, NW)
        return pltpu.make_async_remote_copy(
            src_ref=send_f.at[c, to],
            dst_ref=bound.at[c, me_w],
            send_sem=fs.at[c],
            recv_sem=fr.at[c],
            device_id=(to, me_s),
            device_id_type=MESH,
        )

    solve(0)
    wait_all(pack.at[:, pl.ds(0, NW * (NS - 1))], recv1.at[:, pl.ds(0, NW * (NS - 1))], p1s, p1r)
    for w in range(NW):
        for b in range(2):
            pack2[w, b] = recv1[b, pl.ds(w, NS, stride=NW), :]

    def p2copy(k):
        to = lax.rem(me_w + k, NW)
        return pltpu.make_async_remote_copy(
            src_ref=pack2.at[to],
            dst_ref=recv2.at[me_w],
            send_sem=p2s.at[0],
            recv_sem=p2r.at[0],
            device_id=(to, me_s),
            device_id_type=MESH,
        )

    for k in range(1, NW):
        p2copy(k).start()
    recv2[me_w] = pack2[me_w]

    solve(1)
    solve(2)
    keep_own = pltpu.make_async_copy(send_f.at[:, me_w], bound.at[:, me_w], osem.at[2])
    keep_own.start()

    wait_all(pack2.at[pl.ds(0, NW - 1)], recv2.at[pl.ds(0, NW - 1)], p2s, p2r)
    part_t[0:128, :] = recv2[:, 0].reshape(NW * NS, 128).T
    rest = recv2[:, 1].reshape(NW * NS, 128)
    flipped = rest.T
    part_t[128:192, :] = flipped[0:64]
    part_t[192:256, :] = (flipped[64:128].astype(jnp.int32) & 127).astype(F32)
    place = rest.astype(jnp.int32)
    rows_v[...] = (
        (place >> 13) * 64 + ((place >> 7) & 7) * 8 + ((place >> 10) & 7)
    ) * 4
    keep_part = pltpu.make_async_copy(part_t, part_h, osem.at[3])
    keep_part.start()
    keep_rows = pltpu.make_async_copy(rows_v, rows_h, osem.at[4])
    keep_rows.start()

    for c in range(3):
        wait_all(send_f.at[c, pl.ds(0, NW - 1)], bound.at[c, pl.ds(0, NW - 1)], fs, fr, c)
    for keep in (keep_coef, keep_halo, keep_own, keep_part, keep_rows):
        keep.wait()


def exchange(vel, lower, upper, st, forces, owner, cells, counts):
    hbm = pl.BlockSpec(memory_space=pl.ANY)
    dma = pltpu.SemaphoreType.DMA
    return pl.pallas_call(
        exchange_kernel,
        out_shape=(
            jax.ShapeDtypeStruct((2, 3, SZ, NX), F32),
            jax.ShapeDtypeStruct((3, NW, 2, 8, 128), F32),
            jax.ShapeDtypeStruct((8, RY, 128), F32),
            jax.ShapeDtypeStruct((256, 128), F32),
            jax.ShapeDtypeStruct((128, 128), jnp.int32),
        ),
        in_specs=[hbm] * 8,
        out_specs=[hbm] * 5,
        scratch_shapes=[
            pltpu.VMEM((1, NW * RY), F32),
            pltpu.VMEM((1, NW * RY), F32),
            pltpu.VMEM(st.shape, F32),
            pltpu.VMEM(forces.shape, F32),
            pltpu.VMEM(owner.shape, jnp.int32),
            pltpu.VMEM(cells.shape, jnp.int32),
            pltpu.SMEM((1,), jnp.int32),
            pltpu.VMEM((2, 3, SZ, NX), F32),
            pltpu.VMEM((8, RY, 128), F32),
            pltpu.VMEM((256, 128), F32),
            pltpu.VMEM((128, 128), jnp.int32),
            pltpu.VMEM((8, owner.shape[1]), F32),
            pltpu.VMEM((12 * NW, owner.shape[1]), jnp.bfloat16),
            pltpu.VMEM((owner.shape[1], NS * SLOTS), jnp.bfloat16),
            pltpu.VMEM((3, RY, SZ, NX), F32),
            pltpu.VMEM((3, NW, 2, 8, 128), F32),
            pltpu.VMEM((3, NW, 2, 8, 128), F32),
            pltpu.VMEM((3, NW, 2, 8, 128), F32),
            pltpu.VMEM((NW, 8, 128), F32),
            pltpu.VMEM((NW, 8, 128), F32),
            pltpu.VMEM((8, 128), F32),
            pltpu.VMEM((2, 8, 128), F32),
            pltpu.VMEM((2, NW * NS, 128), F32),
            pltpu.VMEM((2, NW * NS, 128), F32),
            pltpu.VMEM((NW, 2, NS, 128), F32),
            pltpu.VMEM((NW, 2, NS, 128), F32),
            pltpu.VMEM((RY, 128), F32),
            pltpu.VMEM((RY, 128), F32),
            pltpu.VMEM((RY, 128), F32),
            pltpu.VMEM((RY, 128), F32),
            pltpu.VMEM((RY, 128), F32),
            pltpu.VMEM((RY, 128), F32),
            pltpu.VMEM((RY + 8, 128), F32),
            pltpu.VMEM((2, RY + 8, 128), F32),
            pltpu.VMEM((6, NW, 128), F32),
            dma((7,)), dma((5,)), dma((6,)), dma((6,)), dma((6,)), dma((2,)), dma((2,)),
            *[dma((3,))] * 4, *[dma((1,))] * 4,
        ],
        compiler_params=pltpu.CompilerParams(
            collective_id=0, has_side_effects=True, vmem_limit_bytes=56 << 20
        ),
        name="exchange",
    )(vel, lower, upper, st, forces, owner, cells, counts)


def local_kernel(
    vel, halo_h, bound_h, coef_h, part_h, rows_h, inv_vol,
    derivative, forcing,
    halo, bound, coef, part_t, rows,
    acc0, acc1, acc2, acc3, even, odd, mixed, vbuf, stage, isem, vsem, dsem, fsem,
):
    def take(c, x):
        part = (c, slice(None), slice(None), pl.ds(pl.multiple_of(x * 512, 512), 512))
        return pltpu.make_async_copy(vel.at[part], vbuf.at[part], vsem.at[c * 2 + x])

    staged = ((coef_h, coef), (bound_h, bound), (halo_h, halo), (part_h, part_t), (rows_h, rows))
    loads = [
        pltpu.make_async_copy(src, dst, isem.at[i]) for i, (src, dst) in enumerate(staged)
    ]
    for i in range(3):
        loads[i].start()
    for c in range(3):
        for half in range(2):
            take(c, half).start()
    loads[3].start()
    loads[4].start()

    accs = (acc0, acc1, acc2, acc3)
    depth = acc0.shape[0]

    @pl.loop(0, 128)
    def _(i):
        at = pl.ds(pl.multiple_of(i * (depth // 128), depth // 128), depth // 128)
        for acc in accs:
            acc[at, :] = jnp.zeros((depth // 128, 128), F32)

    lane = lax.broadcasted_iota(jnp.int32, (8, 128), 1).astype(F32)

    def spread(source, to):
        pick = jnp.full((8, 128), source, jnp.int32)
        for g in range(SLOTS // 8):
            xl = jnp.take_along_axis(part_t[192 + g * 8 : 200 + g * 8, :], pick, axis=1)
            hit = xl == lane
            for c in range(3):
                r0 = c * SLOTS + g * 8
                f = jnp.take_along_axis(part_t[r0 : r0 + 8, :], pick, axis=1)
                to[pl.ds(g * 32 + c, 8, stride=4), :] = jnp.where(hit, f, 0.0)

    group = 2

    def add(source, frm, steps):
        base = source * 128 + SLOTS
        for r0 in range(0, SLOTS, 4 * group):
            for k in range(4):
                slots = [r0 + k + 4 * g for g in range(group)]
                first = [rows[base + r] for r in slots]
                at = [pl.ds(pl.multiple_of(f, 4), 4) for f in first]
                value = [frm[r * 4 : r * 4 + 4, :] for r in slots]
                held = [accs[k][a, :] for a in at]
                for g in range(group):
                    held[g] = held[g] + value[g]
                    for e in range(g):
                        held[g] = held[g] + jnp.where(first[e] == first[g], value[e], 0.0)
                for g in range(group):
                    accs[k][at[g], :] = held[g]
                for _step in range(group // 2):
                    next(steps, None)

    even[...] = jnp.zeros((256, 128), F32)
    odd[...] = jnp.zeros((256, 128), F32)
    loads[3].wait()
    loads[4].wait()
    spread(0, even)

    def put_d(c, x):
        part = (c, slice(None), slice(None), pl.ds(pl.multiple_of(x * 512, 512), 512))
        return pltpu.make_async_copy(vbuf.at[part], derivative.at[part], dsem.at[c * 2 + x])

    def sweep_steps(c, h, x):
        here = (pl.ds(pl.multiple_of(h * 8, 8), 8), pl.ds(pl.multiple_of(x * 128, 128), 128))

        def row(i):
            if i < -1 or i > RY:
                return None
            if i == -1:
                return halo[0, c, *here]
            if i == RY:
                return halo[1, c, *here]
            return vbuf[c, i, *here]

        window = [row(i) for i in range(-2, 3)]
        prev = None
        for j in range(RY):
            total = None
            for m in range(5):
                if window[m] is None or j + m - 2 == -1 and j == 0:
                    continue
                if j + m - 2 == RY and j == RY - 1:
                    continue
                term = coef[m, j : j + 1, :] * window[m]
                total = term if total is None else total + term
            if j == 0:
                total = total + coef[7, 0:1, :] * bound[c, h * 8 + x, 0]
            if j == RY - 1:
                total = total + coef[7, RY - 1 : RY, :] * bound[c, h * 8 + x, 1]
            if j > 0:
                total = total - coef[5, j : j + 1, :] * prev
            prev = total
            window = window[1:] + [row(j + 3)]
            vbuf[c, j, *here] = total
            yield
        for j in range(RY - 2, -1, -1):
            prev = vbuf[c, j, *here] - coef[6, j : j + 1, :] * prev
            vbuf[c, j, *here] = prev
            yield

    def scatter_pair(i, steps):
        spread(2 * i + 1, odd)
        add(2 * i, even, steps)
        spread(jnp.minimum(2 * i + 2, 127), even)
        add(2 * i + 1, odd, steps)
        for _rest in steps:
            pass

    for i in range(3):
        loads[i].wait()

    @pl.loop(0, 6)
    def _(q):
        c, half = q // 2, q % 2
        take(c, half).wait()

        @pl.loop(0, 8)
        def _(t):
            scatter_pair(q * 8 + t, sweep_steps(c, t // 4, half * 4 + t % 4))

        put_d(c, half).start()

    @pl.loop(48, 64)
    def _(i):
        scatter_pair(i, iter(()))

    def put_f(b):
        part = (slice(None), pl.ds(b * 4, 4))
        return pltpu.make_async_copy(stage.at[part], forcing.at[part], fsem.at[b])

    @pl.loop(0, 8)
    def _(b):
        @pl.loop(0, 8)
        def _(jh):
            j, h = b * 4 + jh // 2, jh % 2
            scale = -inv_vol[j]
            cells = pl.ds(pl.multiple_of(h * 8, 8), 8)
            for x in range(8):
                at = pl.ds(pl.multiple_of(((j * 2 + h) * 8 + x) * 32, 32), 32)
                mixed[x * 32 : x * 32 + 32, :] = scale * (
                    (acc0[at, :] + acc1[at, :]) + (acc2[at, :] + acc3[at, :])
                )
            for x in range(8):
                for c in range(3):
                    stage[c, j, cells, x * 128 : x * 128 + 128] = mixed[
                        pl.ds(x * 32 + c, 8, stride=4), :
                    ]

        put_f(b).start()

    for c in range(3):
        for half in range(2):
            put_d(c, half).wait()

    @pl.loop(0, 8)
    def _(b):
        put_f(b).wait()


def local(vel, halo, bound, coef, part_t, rows, inv_vol):
    sm = pl.BlockSpec(memory_space=pltpu.SMEM)
    hbm = pl.BlockSpec(memory_space=pl.ANY)
    depth = RY * SZ * NX // 128 * 4
    whole = (3, RY, SZ, NX)
    return pl.pallas_call(
        local_kernel,
        out_shape=(jax.ShapeDtypeStruct(whole, F32), jax.ShapeDtypeStruct(whole, F32)),
        in_specs=[hbm] * 6 + [sm],
        out_specs=(hbm, hbm),
        scratch_shapes=[
            pltpu.VMEM(halo.shape, F32),
            pltpu.VMEM(bound.shape, F32),
            pltpu.VMEM(coef.shape, F32),
            pltpu.VMEM(part_t.shape, F32),
            pltpu.SMEM(rows.shape, jnp.int32),
        ]
        + [pltpu.VMEM((depth, 128), F32)] * 4
        + [pltpu.VMEM((256, 128), F32)] * 3
        + [pltpu.VMEM(whole, F32)] * 2
        + [pltpu.SemaphoreType.DMA((n,)) for n in (5, 6, 6, 8)],
        compiler_params=pltpu.CompilerParams(vmem_limit_bytes=58 << 20),
        name="local",
    )(vel, halo, bound, coef, part_t, rows, inv_vol)


def body(velocity, lower, upper, stencil, inv_volume, forces, owner, cells, counts):
    halo, bound, coef, part_t, rows = exchange(
        velocity, lower.reshape(1, -1), upper.reshape(1, -1), stencil, forces,
        owner.reshape(1, -1), cells.reshape(1, -1), counts,
    )
    derivative, forcing = local(
        velocity, halo, bound, coef, part_t, rows.reshape(-1), inv_volume
    )
    return derivative, forcing


def solution(mesh):
    in_specs = (
        P(None, "wall", "span", None),
        P(),
        P(),
        P(None, "wall"),
        P("wall"),
        P(None, ("wall", "span")),
        P(("wall", "span"), None),
        P(("wall", "span")),
        P(("wall", "span")),
    )
    out_specs = (P(None, "wall", "span", None), P(None, "wall", "span", None))
    return jax.shard_map(body, mesh=mesh, in_specs=in_specs, out_specs=out_specs, check_vma=False)
```

```python
import functools

import jax
import jax.numpy as jnp
from jax import lax
from jax.experimental import pallas as pl
from jax.experimental.pallas import tpu as pltpu
from jax.sharding import PartitionSpec as P

F32 = jnp.float32
MESH = pl.DeviceIdType.MESH
NW, NS = 16, 8
RY, SZ, NX = 32, 16, 1024
SLOTS = 64


def exchange_kernel(
    vel, lower_h, upper_h, st_h, forces_h, owner_h, cells_h, counts_h,
    base_h, bound, edge_h, part_h, rows_h,
    lower, upper, st, forces, owner, cells, counts, halo, coef, edge, part_t, rows_v,
    key_row, left, right, vbuf, send_a, recv_a, send_f, elim, pbuf, tile_out, tile_in,
    pack, recv1, pack2, recv2,
    lmat, umat, dmat, cmat, ymat, zmat, first_col, last_col, wmat, wgt, red,
    isem, osem, bsem, vsem, hs, hr, ts, tr, as_, ar, fs, fr, p1s, p1r, p2s, p2r,
):
    me_w = lax.axis_index("wall")
    me_s = lax.axis_index("span")

    def wait_all(src, dst, sent, got, i=0):
        group = pltpu.make_async_remote_copy(
            src_ref=src,
            dst_ref=dst,
            send_sem=sent.at[i],
            recv_sem=got.at[i],
            device_id=(me_w, me_s),
            device_id_type=MESH,
        )
        group.wait_send()
        group.wait_recv()

    def vcopy(c, h):
        part = (c, slice(None), pl.ds(h * 8, 8), slice(None))
        return pltpu.make_async_copy(vel.at[part], vbuf.at[part], vsem.at[c * 2 + h])

    barrier = pltpu.get_barrier_semaphore()

    @pl.loop(1, NW)
    def _(k):
        pl.semaphore_signal(
            barrier, inc=1, device_id=(lax.rem(me_w + k, NW), me_s), device_id_type=MESH
        )

    @pl.loop(1, NS)
    def _(k):
        pl.semaphore_signal(
            barrier, inc=1, device_id=(me_w, lax.rem(me_s + k, NS)), device_id_type=MESH
        )

    staged = (
        (st_h, st), (lower_h, lower), (upper_h, upper),
        (forces_h, forces), (owner_h, owner), (cells_h, cells), (counts_h, counts),
    )
    loads = [
        pltpu.make_async_copy(src, dst, isem.at[i]) for i, (src, dst) in enumerate(staged)
    ]
    for i in range(3):
        loads[i].start()
    for c in range(3):
        for h in range(2):
            vcopy(c, h).start()
    for i in range(3, 7):
        loads[i].start()
    pl.semaphore_wait(barrier, NW - 1 + NS - 1)

    above = lax.rem(me_w + 1, NW)
    under = lax.rem(me_w + NW - 1, NW)

    def hcopy(way, c):
        return pltpu.make_async_remote_copy(
            src_ref=vel.at[c, RY - 1 if way == 0 else 0],
            dst_ref=halo.at[way, c],
            send_sem=hs.at[way * 3 + c],
            recv_sem=hr.at[way * 3 + c],
            device_id=(above if way == 0 else under, me_s),
            device_id_type=MESH,
        )

    hcopy(0, 0).start()
    hcopy(1, 0).start()

    for i in range(3):
        loads[i].wait()
    eye = lax.broadcasted_iota(jnp.int32, (RY, RY), 0) == lax.broadcasted_iota(
        jnp.int32, (RY, RY), 1
    )

    def column(row, mask, n):
        full = jnp.broadcast_to(row, (n, n))
        col = jnp.sum(jnp.where(mask, full, 0.0), axis=1, keepdims=True)
        return jnp.broadcast_to(col, (n, 128))

    stc = [column(st[m : m + 1, :], eye, RY) for m in range(5)]
    tile_out[0:1, :] = stc[0][0:1]
    tile_out[1:2, :] = stc[1][0:1]
    tile_out[2:3, :] = stc[4][RY - 1 : RY]
    tile_out[3:4, :] = stc[3][RY - 1 : RY]
    tile_out[4:8, :] = jnp.zeros((4, 128), F32)

    def tcopy(way):
        return pltpu.make_async_remote_copy(
            src_ref=tile_out,
            dst_ref=tile_in.at[way],
            send_sem=ts.at[way],
            recv_sem=tr.at[way],
            device_id=(above if way == 0 else under, me_s),
            device_id_type=MESH,
        )

    tcopy(0).start()
    tcopy(1).start()
    for c in (1, 2):
        hcopy(0, c).start()
        hcopy(1, c).start()


    nn = (((1,), (0,)), ((), ()))
    lane_i = lax.broadcasted_iota(jnp.int32, (RY, NW * RY), 1)
    in_row = (lane_i & (RY - 1)) == lax.broadcasted_iota(jnp.int32, (RY, NW * RY), 0)
    to_slab = (
        lax.broadcasted_iota(jnp.int32, (NW * RY, 128), 0) // RY
        == lax.broadcasted_iota(jnp.int32, (NW * RY, 128), 1)
    ).astype(F32).astype(jnp.bfloat16)
    both = jnp.concatenate(
        [
            jnp.where(in_row, jnp.broadcast_to(v[0:1, :], (RY, NW * RY)), 0.0)
            for v in (lower, upper)
        ],
        axis=0,
    )
    tall = None
    for _part in range(3):
        head = both.astype(jnp.bfloat16)
        both = both - head.astype(F32)
        term = lax.dot_general(head, to_slab, nn, preferred_element_type=F32)
        tall = term if tall is None else tall + term
    lmat[...] = tall[0:RY]
    umat[...] = tall[RY : 2 * RY]

    zero = jnp.zeros((1, 128), F32)
    carry_c, carry_b = zero, None
    for j in range(RY):
        low, upp = lmat[j : j + 1, :], umat[j : j + 1, :]
        inv = 1.0 / (1.0 - low * carry_c) if j > 0 else jnp.ones((1, 128), F32)
        carry_c = upp * inv
        dmat[j : j + 1, :] = inv
        cmat[j : j + 1, :] = carry_c
    binv = [None] * RY
    for j in range(RY - 1, -1, -1):
        if j == RY - 1:
            binv[j] = jnp.ones((1, 128), F32)
        else:
            binv[j] = 1.0 / (
                1.0 - umat[j : j + 1, :] * lmat[j + 1 : j + 2, :] * binv[j + 1]
            )
    y = binv[0]
    ymat[0:1, :] = y
    for j in range(1, RY):
        y = -(umat[j - 1 : j, :] * binv[j]) * y
        ymat[j : j + 1, :] = y
    z = dmat[RY - 1 : RY, :]
    zmat[RY - 1 : RY, :] = z
    for j in range(RY - 2, -1, -1):
        z = -(lmat[j + 1 : j + 2, :] * dmat[j : j + 1, :]) * z
        zmat[j : j + 1, :] = z
    v = binv[0]
    first_col[0:1, :] = v
    for j in range(1, RY):
        v = -(lmat[j : j + 1, :] * binv[j]) * v
        first_col[j : j + 1, :] = v
    v = dmat[RY - 1 : RY, :]
    last_col[RY - 1 : RY, :] = v
    for j in range(RY - 2, -1, -1):
        v = -cmat[j : j + 1, :] * v
        last_col[j : j + 1, :] = v

    lane16 = lax.broadcasted_iota(jnp.int32, (RY, 128), 1)

    def at_slab(values, slab):
        n = values.shape[0]
        col = jnp.sum(jnp.where(lane16[0:n] == slab, values, 0.0), axis=1, keepdims=True)
        return jnp.broadcast_to(col, (n, 128))

    low_all, upp_all = lmat[...], umat[...]
    inv_own = at_slab(dmat[...], me_w)
    c_own = at_slab(cmat[...], me_w)
    y_own = at_slab(ymat[...], me_w)
    z_own = at_slab(zmat[...], me_w)
    low_own = at_slab(low_all, me_w)
    low_next = at_slab(low_all[0:1], me_w + 1)
    upp_prev = at_slab(upp_all[RY - 1 : RY], me_w - 1)
    has_under = jnp.where(me_w > 0, 1.0, 0.0)
    has_above = jnp.where(me_w < NW - 1, 1.0, 0.0)

    row_i = lax.broadcasted_iota(jnp.int32, (RY, 128), 0)
    kept = [
        jnp.where(row_i == 0, 0.0, jnp.where(row_i == 1, stc[0] * has_under, stc[0])),
        jnp.where(row_i == 0, 0.0, stc[1]),
        stc[2],
        jnp.where(row_i == RY - 1, 0.0, stc[3]),
        jnp.where(
            row_i == RY - 1, 0.0, jnp.where(row_i == RY - 2, stc[4] * has_above, stc[4])
        ),
    ]
    for m in range(5):
        coef[m] = kept[m] * inv_own
    coef[5] = jnp.where(row_i == 0, 0.0, low_own * inv_own)
    coef[6] = c_own
    edge[0] = at_slab(first_col[...], me_w)
    edge[1] = at_slab(last_col[...], me_w)
    keep_coef = pltpu.make_async_copy(edge, edge_h, osem.at[0])
    keep_coef.start()

    for way, own, scale in ((0, z_own, low_next), (1, y_own, upp_prev)):
        wmat[...] = jnp.zeros((RY + 8, 128), F32)
        for m in range(5):
            wmat[m + 2 : m + 2 + RY, :] += kept[m] * own
        wgt[way] = wmat[...] * (-scale)

    eye16 = lax.broadcasted_iota(jnp.int32, (NW, NW), 0) == lax.broadcasted_iota(
        jnp.int32, (NW, NW), 1
    )
    next16 = lax.broadcasted_iota(jnp.int32, (NW, NW), 0) + 1 == lax.broadcasted_iota(
        jnp.int32, (NW, NW), 1
    )
    prev16 = lax.broadcasted_iota(jnp.int32, (NW, NW), 0) - 1 == lax.broadcasted_iota(
        jnp.int32, (NW, NW), 1
    )
    z0 = column(zmat[0:1, 0:NW], eye16, NW)
    z1 = column(zmat[RY - 1 : RY, 0:NW], eye16, NW)
    y0 = column(ymat[0:1, 0:NW], eye16, NW)
    y1 = column(ymat[RY - 1 : RY, 0:NW], eye16, NW)
    low_n = column(low_all[0:1, 0:NW], next16, NW)
    upp_p = column(upp_all[RY - 1 : RY, 0:NW], prev16, NW)
    red[0] = upp_p * y0
    red[1] = low_n * z0
    lz1 = low_n * z1
    uy1 = upp_p * y1
    q = -lz1[0:1]
    for s in range(1, NW):
        dinv = 1.0 / (1.0 + red[0, s : s + 1, :] * q)
        c3 = uy1[s : s + 1] * dinv
        red[2, s : s + 1, :] = q * dinv
        red[3, s : s + 1, :] = dinv
        red[4, s : s + 1, :] = c3
        red[5, s : s + 1, :] = q
        q = red[1, s : s + 1, :] * q * c3 - lz1[s : s + 1]

    def own_rows(c):
        for h in range(2):
            vcopy(c, h).wait()

            @pl.loop(0, 2)
            def _(x):
                cols = [
                    pl.ds(pl.multiple_of(x * 512 + b * 128, 128), 128) for b in range(4)
                ]
                up, down = [None] * 4, [None] * 4
                for j in range(RY):
                    wu, wd = wgt[0, j + 4 : j + 5, :], wgt[1, j + 4 : j + 5, :]
                    for b in range(4):
                        u = vbuf[c, j, h * 8 : h * 8 + 8, cols[b]]
                        up[b] = wu * u if j == 0 else up[b] + wu * u
                        down[b] = wd * u if j == 0 else down[b] + wd * u
                for b in range(4):
                    send_a[c, h * 8 + x * 4 + b, 0] = up[b]
                    send_a[c, h * 8 + x * 4 + b, 1] = down[b]

    def acopy(c, k):
        to = lax.rem(me_w + k, NW)
        return pltpu.make_async_remote_copy(
            src_ref=send_a.at[c, to],
            dst_ref=recv_a.at[c, me_w],
            send_sem=as_.at[c],
            recv_sem=ar.at[c],
            device_id=(to, me_s),
            device_id_type=MESH,
        )

    def add_ends(c):
        for h in range(2):
            cells8 = slice(h * 8, h * 8 + 8)

            @pl.loop(0, 8)
            def _(x):
                cols = pl.ds(pl.multiple_of(x * 128, 128), 128)
                ends = (halo[0, c, cells8, cols], halo[1, c, cells8, cols])
                near = (
                    (tile_in[1, 0:1, :], RY - 2, tile_in[1, 1:2, :], RY - 1),
                    (tile_in[0, 2:3, :], 1, tile_in[0, 3:4, :], 0),
                )
                for way in range(2):
                    wa, ja, wb, jb = near[way]
                    send_a[c, h * 8 + x, way] += (
                        wgt[way, 3:4, :] * ends[0]
                        + wgt[way, RY + 4 : RY + 5, :] * ends[1]
                        + wa * vbuf[c, ja, cells8, cols]
                        + wb * vbuf[c, jb, cells8, cols]
                    )

    def send_up(c):
        hcopy(0, c).wait()
        hcopy(1, c).wait()
        add_ends(c)
        for k in range(1, NW):
            acopy(c, k).start()
        recv_a[c, me_w] = send_a[c, me_w]

    own_rows(0)
    own_rows(1)
    own_rows(2)

    for i in range(3, 7):
        loads[i].wait()
    slots = owner.shape[1]
    own = owner[...]
    live = lax.broadcasted_iota(jnp.int32, (1, slots), 1) < counts[0]
    wall_row = jnp.where(live, own >> 3, NW)
    key_row[0:1, :] = jnp.where(live, (own & 7) * NW + (own >> 3), 512).astype(F32)
    key_row[1:8, :] = jnp.zeros((7, slots), F32)
    lane_f = lax.broadcasted_iota(jnp.int32, (256, 128), 1).astype(F32)
    sub_f = lax.broadcasted_iota(jnp.int32, (256, 128), 0).astype(F32)
    lower_tri = [
        jnp.where(lane_f + 128.0 * b < sub_f, 1.0, 0.0) for b in range(2)
    ]

    ones = jnp.ones((128, 128), jnp.bfloat16)
    head_row = jnp.where(
        lax.broadcasted_iota(jnp.int32, (8, 128), 0) == 0, 1.0, 0.0
    ).astype(jnp.bfloat16)

    def rank_block(i, carry):
        at = pl.ds(pl.multiple_of(i * 256, 256), 256)
        tile = key_row[:, at]
        col = lax.dot_general(
            tile.T.astype(jnp.bfloat16), head_row, nn, preferred_element_type=F32
        )
        hit = col == lane_f
        score = jnp.where(hit, carry, 0.0)
        for b in range(2):
            same = col == tile[0:1, b * 128 : b * 128 + 128]
            score = score + jnp.where(same, lower_tri[b], 0.0)
        rank = lax.dot_general(
            score.astype(jnp.bfloat16), ones, nn, preferred_element_type=F32
        )
        place = jnp.floor(col * (1.0 / NW)) * SLOTS + rank
        for b in range(4):
            right[at, b * 128 : b * 128 + 128] = jnp.where(
                place == lane_f + 128.0 * b, 1.0, 0.0
            ).astype(jnp.bfloat16)
        return carry + jnp.sum(jnp.where(hit, 1.0, 0.0), axis=0, keepdims=True)

    blocks = slots // 256
    carry = lax.fori_loop(
        0, blocks // 2, rank_block, jnp.zeros((1, 128), F32), unroll=4
    )
    tcopy(0).wait()
    tcopy(1).wait()
    send_up(0)
    in_wall = lax.broadcasted_iota(jnp.int32, (NW, slots), 0) == wall_row
    load = [forces[c : c + 1, :] for c in range(3)] + [cells[...].astype(F32)]
    for part in range(3):
        head = [x.astype(jnp.bfloat16).astype(F32) for x in load]
        load = [x - y for x, y in zip(load, head)]
        for c in range(4):
            r0 = (part * 4 + c) * NW
            left[r0 : r0 + NW, :] = jnp.where(in_wall, head[c], 0.0).astype(jnp.bfloat16)
    carry = lax.fori_loop(blocks // 2, blocks * 3 // 4, rank_block, carry, unroll=4)
    send_up(1)
    lax.fori_loop(blocks * 3 // 4, blocks, rank_block, carry, unroll=4)
    send_up(2)
    made = lax.dot_general(left[...], right[...], nn, preferred_element_type=F32)
    made = made[0:64] + made[64:128] + made[128:192]
    first = lax.broadcasted_iota(jnp.int32, (NW, 128), 1) < SLOTS
    for k in range(NS):
        for b in range(2):
            pair = [
                made[c * NW : c * NW + NW, k // 2 * 128 : k // 2 * 128 + 128]
                for c in (2 * b, 2 * b + 1)
            ]
            turn = 1 - k % 2
            pair[turn] = pltpu.roll(pair[turn], SLOTS, 1)
            pack[b, k * NW : k * NW + NW, :] = jnp.where(first, pair[0], pair[1])

    def p1copy(k):
        to = lax.rem(me_s + k, NS)
        return pltpu.make_async_remote_copy(
            src_ref=pack.at[:, pl.ds(pl.multiple_of(to * NW, NW), NW)],
            dst_ref=recv1.at[:, pl.ds(pl.multiple_of(me_s * NW, NW), NW)],
            send_sem=p1s.at[0],
            recv_sem=p1r.at[0],
            device_id=(me_w, to),
            device_id_type=MESH,
        )

    for k in range(1, NS):
        p1copy(k).start()
    mine = pl.ds(pl.multiple_of(me_s * NW, NW), NW)
    recv1[:, mine, :] = pack[:, mine, :]

    def solve(c):
        wait_all(send_a.at[c, pl.ds(0, NW - 1)], recv_a.at[c, pl.ds(0, NW - 1)], as_, ar, c)
        p = recv_a[c, 0, 0]
        for s in range(1, NW):
            pbuf[s] = p
            e = recv_a[c, s, 1] - red[0, s : s + 1, :] * p
            elim[s] = e
            if s < NW - 1:
                p = recv_a[c, s, 0] - red[1, s : s + 1, :] * (
                    p + red[2, s : s + 1, :] * e
                )
        down = jnp.zeros((8, 128), F32)
        send_f[c, NW - 1, 1] = down
        for s in range(NW - 1, 0, -1):
            down = red[3, s : s + 1, :] * elim[s] - red[4, s : s + 1, :] * down
            send_f[c, s - 1, 1] = down
            send_f[c, s, 0] = pbuf[s] + red[5, s : s + 1, :] * down
        send_f[c, 0, 0] = jnp.zeros((8, 128), F32)
        for k in range(1, NW):
            fcopy(c, k).start()

    def fcopy(c, k):
        to = lax.rem(me_w + k, NW)
        return pltpu.make_async_remote_copy(
            src_ref=send_f.at[c, to],
            dst_ref=bound.at[c, me_w],
            send_sem=fs.at[c],
            recv_sem=fr.at[c],
            device_id=(to, me_s),
            device_id_type=MESH,
        )

    def keep_base(c):
        return pltpu.make_async_copy(vbuf.at[c], base_h.at[c], bsem.at[c])

    def particular(c):
        @pl.loop(0, 4)
        def _(xx):
            tiles = range(2)
            cols = [
                pl.ds(pl.multiple_of(xx * 256 + t * 128, 128), 128) for t in tiles
            ]

            def row(i):
                if i < -1 or i > RY:
                    return None
                if i == -1:
                    return [halo[0, c, :, cols[t]] for t in tiles]
                if i == RY:
                    return [halo[1, c, :, cols[t]] for t in tiles]
                return [vbuf[c, i, :, cols[t]] for t in tiles]

            window = [row(i) for i in range(-2, 3)]
            prev = [None, None]
            for j in range(RY):
                total = [None, None]
                for m in range(5):
                    if window[m] is None or j + m - 2 == -1 and j == 0:
                        continue
                    if j + m - 2 == RY and j == RY - 1:
                        continue
                    weight = coef[m, j : j + 1, :]
                    for t in tiles:
                        term = weight * window[m][t]
                        total[t] = term if total[t] is None else total[t] + term
                if j > 0:
                    for t in tiles:
                        total[t] = total[t] - coef[5, j : j + 1, :] * prev[t]
                prev = total
                window = window[1:] + [row(j + 3)]
                for t in tiles:
                    vbuf[c, j, :, cols[t]] = total[t]
            for j in range(RY - 2, -1, -1):
                weight = coef[6, j : j + 1, :]
                for t in tiles:
                    prev[t] = vbuf[c, j, :, cols[t]] - weight * prev[t]
                    vbuf[c, j, :, cols[t]] = prev[t]

        keep_base(c).start()

    solve(0)
    particular(0)
    solve(1)
    wait_all(pack.at[:, pl.ds(0, NW * (NS - 1))], recv1.at[:, pl.ds(0, NW * (NS - 1))], p1s, p1r)
    for w in range(NW):
        for b in range(2):
            pack2[w, b] = recv1[b, pl.ds(w, NS, stride=NW), :]

    def p2copy(k):
        to = lax.rem(me_w + k, NW)
        return pltpu.make_async_remote_copy(
            src_ref=pack2.at[to],
            dst_ref=recv2.at[me_w],
            send_sem=p2s.at[0],
            recv_sem=p2r.at[0],
            device_id=(to, me_s),
            device_id_type=MESH,
        )

    for k in range(1, NW):
        p2copy(k).start()
    recv2[me_w] = pack2[me_w]

    solve(2)
    keep_own = pltpu.make_async_copy(send_f.at[:, me_w], bound.at[:, me_w], osem.at[2])
    keep_own.start()
    particular(1)
    particular(2)

    wait_all(pack2.at[pl.ds(0, NW - 1)], recv2.at[pl.ds(0, NW - 1)], p2s, p2r)
    part_t[0:128, :] = recv2[:, 0].reshape(NW * NS, 128).T
    rest = recv2[:, 1].reshape(NW * NS, 128)
    flipped = rest.T
    part_t[128:192, :] = flipped[0:64]
    part_t[192:256, :] = (flipped[64:128].astype(jnp.int32) & 127).astype(F32)
    place = rest.astype(jnp.int32)
    rows_v[...] = (
        (place >> 13) * 64 + ((place >> 7) & 7) * 8 + ((place >> 10) & 7)
    ) * 4
    keep_part = pltpu.make_async_copy(part_t, part_h, osem.at[3])
    keep_part.start()
    keep_rows = pltpu.make_async_copy(rows_v, rows_h, osem.at[4])
    keep_rows.start()

    for c in range(3):
        wait_all(send_f.at[c, pl.ds(0, NW - 1)], bound.at[c, pl.ds(0, NW - 1)], fs, fr, c)
    for c in range(3):
        keep_base(c).wait()
    for keep in (keep_coef, keep_own, keep_part, keep_rows):
        keep.wait()


def exchange(vel, lower, upper, st, forces, owner, cells, counts):
    hbm = pl.BlockSpec(memory_space=pl.ANY)
    dma = pltpu.SemaphoreType.DMA
    return pl.pallas_call(
        exchange_kernel,
        out_shape=(
            jax.ShapeDtypeStruct((3, RY, SZ, NX), F32),
            jax.ShapeDtypeStruct((3, NW, 2, 8, 128), F32),
            jax.ShapeDtypeStruct((2, RY, 128), F32),
            jax.ShapeDtypeStruct((256, 128), F32),
            jax.ShapeDtypeStruct((128, 128), jnp.int32),
        ),
        in_specs=[hbm] * 8,
        out_specs=[hbm] * 5,
        scratch_shapes=[
            pltpu.VMEM((1, NW * RY), F32),
            pltpu.VMEM((1, NW * RY), F32),
            pltpu.VMEM(st.shape, F32),
            pltpu.VMEM(forces.shape, F32),
            pltpu.VMEM(owner.shape, jnp.int32),
            pltpu.VMEM(cells.shape, jnp.int32),
            pltpu.SMEM((1,), jnp.int32),
            pltpu.VMEM((2, 3, SZ, NX), F32),
            pltpu.VMEM((7, RY, 128), F32),
            pltpu.VMEM((2, RY, 128), F32),
            pltpu.VMEM((256, 128), F32),
            pltpu.VMEM((128, 128), jnp.int32),
            pltpu.VMEM((8, owner.shape[1]), F32),
            pltpu.VMEM((12 * NW, owner.shape[1]), jnp.bfloat16),
            pltpu.VMEM((owner.shape[1], NS * SLOTS), jnp.bfloat16),
            pltpu.VMEM((3, RY, SZ, NX), F32),
            pltpu.VMEM((3, NW, 2, 8, 128), F32),
            pltpu.VMEM((3, NW, 2, 8, 128), F32),
            pltpu.VMEM((3, NW, 2, 8, 128), F32),
            pltpu.VMEM((NW, 8, 128), F32),
            pltpu.VMEM((NW, 8, 128), F32),
            pltpu.VMEM((8, 128), F32),
            pltpu.VMEM((2, 8, 128), F32),
            pltpu.VMEM((2, NW * NS, 128), F32),
            pltpu.VMEM((2, NW * NS, 128), F32),
            pltpu.VMEM((NW, 2, NS, 128), F32),
            pltpu.VMEM((NW, 2, NS, 128), F32),
            pltpu.VMEM((RY, 128), F32),
            pltpu.VMEM((RY, 128), F32),
            pltpu.VMEM((RY, 128), F32),
            pltpu.VMEM((RY, 128), F32),
            pltpu.VMEM((RY, 128), F32),
            pltpu.VMEM((RY, 128), F32),
            pltpu.VMEM((RY, 128), F32),
            pltpu.VMEM((RY, 128), F32),
            pltpu.VMEM((RY + 8, 128), F32),
            pltpu.VMEM((2, RY + 8, 128), F32),
            pltpu.VMEM((6, NW, 128), F32),
            dma((7,)), dma((5,)), dma((3,)), dma((6,)), dma((6,)), dma((6,)), dma((2,)), dma((2,)),
            *[dma((3,))] * 4, *[dma((1,))] * 4,
        ],
        compiler_params=pltpu.CompilerParams(
            collective_id=0, has_side_effects=True, vmem_limit_bytes=56 << 20
        ),
        name="exchange",
    )(vel, lower, upper, st, forces, owner, cells, counts)


def local_kernel(
    base, bound_h, edge_h, part_h, rows_h, inv_vol,
    derivative, forcing,
    bound, edge, part_t, rows,
    acc0, acc1, acc2, acc3, even, odd, mixed, vbuf, stage, isem, vsem, dsem, fsem,
):
    def take(c, x):
        part = (c, slice(None), slice(None), pl.ds(pl.multiple_of(x * 512, 512), 512))
        return pltpu.make_async_copy(base.at[part], vbuf.at[part], vsem.at[c * 2 + x])

    staged = ((edge_h, edge), (bound_h, bound), (part_h, part_t), (rows_h, rows))
    loads = [
        pltpu.make_async_copy(src, dst, isem.at[i]) for i, (src, dst) in enumerate(staged)
    ]
    for load in loads:
        load.start()
    for c in range(3):
        for half in range(2):
            take(c, half).start()

    accs = (acc0, acc1, acc2, acc3)
    depth = acc0.shape[0]

    @pl.loop(0, 128)
    def _(i):
        at = pl.ds(pl.multiple_of(i * (depth // 128), depth // 128), depth // 128)
        for acc in accs:
            acc[at, :] = jnp.zeros((depth // 128, 128), F32)

    lane = lax.broadcasted_iota(jnp.int32, (8, 128), 1).astype(F32)

    def spread(source, to):
        pick = jnp.full((8, 128), source, jnp.int32)
        for g in range(SLOTS // 8):
            xl = jnp.take_along_axis(part_t[192 + g * 8 : 200 + g * 8, :], pick, axis=1)
            hit = xl == lane
            for c in range(3):
                r0 = c * SLOTS + g * 8
                f = jnp.take_along_axis(part_t[r0 : r0 + 8, :], pick, axis=1)
                to[pl.ds(g * 32 + c, 8, stride=4), :] = jnp.where(hit, f, 0.0)

    group = 2

    def add(source, frm, steps):
        base = source * 128 + SLOTS
        for r0 in range(0, SLOTS, 4 * group):
            for k in range(4):
                slots = [r0 + k + 4 * g for g in range(group)]
                first = [rows[base + r] for r in slots]
                at = [pl.ds(pl.multiple_of(f, 4), 4) for f in first]
                value = [frm[r * 4 : r * 4 + 4, :] for r in slots]
                held = [accs[k][a, :] for a in at]
                for g in range(group):
                    held[g] = held[g] + value[g]
                    for e in range(g):
                        held[g] = held[g] + jnp.where(first[e] == first[g], value[e], 0.0)
                for g in range(group):
                    accs[k][at[g], :] = held[g]
                if k % 2 == 1:
                    next(steps, None)

    even[...] = jnp.zeros((256, 128), F32)
    odd[...] = jnp.zeros((256, 128), F32)
    for load in loads:
        load.wait()
    spread(0, even)

    def put_d(c, x):
        part = (c, slice(None), slice(None), pl.ds(pl.multiple_of(x * 512, 512), 512))
        return pltpu.make_async_copy(vbuf.at[part], derivative.at[part], dsem.at[c * 2 + x])

    def join_steps(c, h, x):
        here = (pl.ds(pl.multiple_of(h * 8, 8), 8), pl.ds(pl.multiple_of(x * 128, 128), 128))
        under, above = bound[c, h * 8 + x, 0], bound[c, h * 8 + x, 1]
        for j in range(RY):
            vbuf[c, j, *here] = vbuf[c, j, *here] + (
                edge[0, j : j + 1, :] * under + edge[1, j : j + 1, :] * above
            )
            yield

    def scatter_pair(i, steps):
        spread(2 * i + 1, odd)
        add(2 * i, even, steps)
        spread(jnp.minimum(2 * i + 2, 127), even)
        add(2 * i + 1, odd, steps)
        for _rest in steps:
            pass

    @pl.loop(0, 6)
    def _(q):
        c, half = q // 2, q % 2
        take(c, half).wait()

        @pl.loop(0, 8)
        def _(t):
            scatter_pair(q * 8 + t, join_steps(c, t // 4, half * 4 + t % 4))

        put_d(c, half).start()

    @pl.loop(48, 64)
    def _(i):
        scatter_pair(i, iter(()))

    def put_f(b):
        part = (slice(None), pl.ds(b * 4, 4))
        return pltpu.make_async_copy(stage.at[part], forcing.at[part], fsem.at[b])

    @pl.loop(0, 8)
    def _(b):
        @pl.loop(0, 8)
        def _(jh):
            j, h = b * 4 + jh // 2, jh % 2
            scale = -inv_vol[j]
            cells = pl.ds(pl.multiple_of(h * 8, 8), 8)
            for x in range(8):
                at = pl.ds(pl.multiple_of(((j * 2 + h) * 8 + x) * 32, 32), 32)
                mixed[x * 32 : x * 32 + 32, :] = scale * (
                    (acc0[at, :] + acc1[at, :]) + (acc2[at, :] + acc3[at, :])
                )
            for x in range(8):
                for c in range(3):
                    stage[c, j, cells, x * 128 : x * 128 + 128] = mixed[
                        pl.ds(x * 32 + c, 8, stride=4), :
                    ]

        put_f(b).start()

    for c in range(3):
        for half in range(2):
            put_d(c, half).wait()

    @pl.loop(0, 8)
    def _(b):
        put_f(b).wait()


def local(base, bound, edge, part_t, rows, inv_vol):
    sm = pl.BlockSpec(memory_space=pltpu.SMEM)
    hbm = pl.BlockSpec(memory_space=pl.ANY)
    depth = RY * SZ * NX // 128 * 4
    whole = (3, RY, SZ, NX)
    return pl.pallas_call(
        local_kernel,
        out_shape=(jax.ShapeDtypeStruct(whole, F32), jax.ShapeDtypeStruct(whole, F32)),
        in_specs=[hbm] * 5 + [sm],
        out_specs=(hbm, hbm),
        scratch_shapes=[
            pltpu.VMEM(bound.shape, F32),
            pltpu.VMEM(edge.shape, F32),
            pltpu.VMEM(part_t.shape, F32),
            pltpu.SMEM(rows.shape, jnp.int32),
        ]
        + [pltpu.VMEM((depth, 128), F32)] * 4
        + [pltpu.VMEM((256, 128), F32)] * 3
        + [pltpu.VMEM(whole, F32)] * 2
        + [pltpu.SemaphoreType.DMA((n,)) for n in (4, 6, 6, 8)],
        compiler_params=pltpu.CompilerParams(vmem_limit_bytes=58 << 20),
        name="local",
    )(base, bound, edge, part_t, rows, inv_vol)


def body(velocity, lower, upper, stencil, inv_volume, forces, owner, cells, counts):
    base, bound, edge, part_t, rows = exchange(
        velocity, lower.reshape(1, -1), upper.reshape(1, -1), stencil, forces,
        owner.reshape(1, -1), cells.reshape(1, -1), counts,
    )
    derivative, forcing = local(base, bound, edge, part_t, rows.reshape(-1), inv_volume)
    return derivative, forcing


def solution(mesh):
    in_specs = (
        P(None, "wall", "span", None),
        P(),
        P(),
        P(None, "wall"),
        P("wall"),
        P(None, ("wall", "span")),
        P(("wall", "span"), None),
        P(("wall", "span")),
        P(("wall", "span")),
    )
    out_specs = (P(None, "wall", "span", None), P(None, "wall", "span", None))
    return jax.shard_map(body, mesh=mesh, in_specs=in_specs, out_specs=out_specs, check_vma=False)
```

```python
import functools

import jax
import jax.numpy as jnp
from jax import lax
from jax.experimental import pallas as pl
from jax.experimental.pallas import tpu as pltpu
from jax.sharding import PartitionSpec as P

F32 = jnp.float32
MESH = pl.DeviceIdType.MESH
NW, NS = 16, 8
RY, SZ, NX = 32, 16, 1024
SLOTS = 64


def exchange_kernel(
    vel, lower_h, upper_h, st_h, forces_h, owner_h, cells_h, counts_h,
    base_h, bound, edge_h, part_h, rows_h,
    lower, upper, st, forces, owner, cells, counts, halo, coef, edge, part_t, rows_v,
    key_row, left, right, vbuf, send_a, recv_a, send_f, elim, pbuf, tile_out, tile_in,
    pack, recv1, pack2, recv2,
    lmat, umat, dmat, cmat, ymat, zmat, first_col, last_col, wmat, wgt, red,
    isem, osem, bsem, vsem, hs, hr, ts, tr, as_, ar, fs, fr, p1s, p1r, p2s, p2r,
):
    me_w = lax.axis_index("wall")
    me_s = lax.axis_index("span")

    def wait_all(src, dst, sent, got, i=0):
        group = pltpu.make_async_remote_copy(
            src_ref=src,
            dst_ref=dst,
            send_sem=sent.at[i],
            recv_sem=got.at[i],
            device_id=(me_w, me_s),
            device_id_type=MESH,
        )
        group.wait_send()
        group.wait_recv()

    def vcopy(c, h):
        part = (c, slice(None), pl.ds(h * 8, 8), slice(None))
        return pltpu.make_async_copy(vel.at[part], vbuf.at[part], vsem.at[c * 2 + h])

    barrier = pltpu.get_barrier_semaphore()

    @pl.loop(1, NW)
    def _(k):
        pl.semaphore_signal(
            barrier, inc=1, device_id=(lax.rem(me_w + k, NW), me_s), device_id_type=MESH
        )

    @pl.loop(1, NS)
    def _(k):
        pl.semaphore_signal(
            barrier, inc=1, device_id=(me_w, lax.rem(me_s + k, NS)), device_id_type=MESH
        )

    staged = (
        (st_h, st), (lower_h, lower), (upper_h, upper),
        (forces_h, forces), (owner_h, owner), (cells_h, cells), (counts_h, counts),
    )
    loads = [
        pltpu.make_async_copy(src, dst, isem.at[i]) for i, (src, dst) in enumerate(staged)
    ]
    for i in range(3):
        loads[i].start()
    for c in range(3):
        for h in range(2):
            vcopy(c, h).start()
    for i in range(3, 7):
        loads[i].start()
    pl.semaphore_wait(barrier, NW - 1 + NS - 1)

    above = lax.rem(me_w + 1, NW)
    under = lax.rem(me_w + NW - 1, NW)

    def hcopy(way, c):
        return pltpu.make_async_remote_copy(
            src_ref=vel.at[c, RY - 1 if way == 0 else 0],
            dst_ref=halo.at[way, c],
            send_sem=hs.at[way * 3 + c],
            recv_sem=hr.at[way * 3 + c],
            device_id=(above if way == 0 else under, me_s),
            device_id_type=MESH,
        )

    hcopy(0, 0).start()
    hcopy(1, 0).start()

    for i in range(3):
        loads[i].wait()
    eye = lax.broadcasted_iota(jnp.int32, (RY, RY), 0) == lax.broadcasted_iota(
        jnp.int32, (RY, RY), 1
    )

    def column(row, mask, n):
        full = jnp.broadcast_to(row, (n, n))
        col = jnp.sum(jnp.where(mask, full, 0.0), axis=1, keepdims=True)
        return jnp.broadcast_to(col, (n, 128))

    stc = [column(st[m : m + 1, :], eye, RY) for m in range(5)]
    tile_out[0:1, :] = stc[0][0:1]
    tile_out[1:2, :] = stc[1][0:1]
    tile_out[2:3, :] = stc[4][RY - 1 : RY]
    tile_out[3:4, :] = stc[3][RY - 1 : RY]
    tile_out[4:8, :] = jnp.zeros((4, 128), F32)

    def tcopy(way):
        return pltpu.make_async_remote_copy(
            src_ref=tile_out,
            dst_ref=tile_in.at[way],
            send_sem=ts.at[way],
            recv_sem=tr.at[way],
            device_id=(above if way == 0 else under, me_s),
            device_id_type=MESH,
        )

    tcopy(0).start()
    tcopy(1).start()
    for c in (1, 2):
        hcopy(0, c).start()
        hcopy(1, c).start()


    nn = (((1,), (0,)), ((), ()))
    lane_i = lax.broadcasted_iota(jnp.int32, (RY, NW * RY), 1)
    in_row = (lane_i & (RY - 1)) == lax.broadcasted_iota(jnp.int32, (RY, NW * RY), 0)
    to_slab = (
        lax.broadcasted_iota(jnp.int32, (NW * RY, 128), 0) // RY
        == lax.broadcasted_iota(jnp.int32, (NW * RY, 128), 1)
    ).astype(F32).astype(jnp.bfloat16)
    both = jnp.concatenate(
        [
            jnp.where(in_row, jnp.broadcast_to(v[0:1, :], (RY, NW * RY)), 0.0)
            for v in (lower, upper)
        ],
        axis=0,
    )
    tall = None
    for _part in range(3):
        head = both.astype(jnp.bfloat16)
        both = both - head.astype(F32)
        term = lax.dot_general(head, to_slab, nn, preferred_element_type=F32)
        tall = term if tall is None else tall + term
    lmat[...] = tall[0:RY]
    umat[...] = tall[RY : 2 * RY]

    zero = jnp.zeros((1, 128), F32)
    carry_c, carry_b = zero, None
    for j in range(RY):
        low, upp = lmat[j : j + 1, :], umat[j : j + 1, :]
        inv = 1.0 / (1.0 - low * carry_c) if j > 0 else jnp.ones((1, 128), F32)
        carry_c = upp * inv
        dmat[j : j + 1, :] = inv
        cmat[j : j + 1, :] = carry_c
    binv = [None] * RY
    for j in range(RY - 1, -1, -1):
        if j == RY - 1:
            binv[j] = jnp.ones((1, 128), F32)
        else:
            binv[j] = 1.0 / (
                1.0 - umat[j : j + 1, :] * lmat[j + 1 : j + 2, :] * binv[j + 1]
            )
    y = binv[0]
    ymat[0:1, :] = y
    for j in range(1, RY):
        y = -(umat[j - 1 : j, :] * binv[j]) * y
        ymat[j : j + 1, :] = y
    z = dmat[RY - 1 : RY, :]
    zmat[RY - 1 : RY, :] = z
    for j in range(RY - 2, -1, -1):
        z = -(lmat[j + 1 : j + 2, :] * dmat[j : j + 1, :]) * z
        zmat[j : j + 1, :] = z
    v = binv[0]
    first_col[0:1, :] = v
    for j in range(1, RY):
        v = -(lmat[j : j + 1, :] * binv[j]) * v
        first_col[j : j + 1, :] = v
    v = dmat[RY - 1 : RY, :]
    last_col[RY - 1 : RY, :] = v
    for j in range(RY - 2, -1, -1):
        v = -cmat[j : j + 1, :] * v
        last_col[j : j + 1, :] = v

    lane16 = lax.broadcasted_iota(jnp.int32, (RY, 128), 1)

    def at_slab(values, slab):
        n = values.shape[0]
        col = jnp.sum(jnp.where(lane16[0:n] == slab, values, 0.0), axis=1, keepdims=True)
        return jnp.broadcast_to(col, (n, 128))

    low_all, upp_all = lmat[...], umat[...]
    inv_own = at_slab(dmat[...], me_w)
    c_own = at_slab(cmat[...], me_w)
    y_own = at_slab(ymat[...], me_w)
    z_own = at_slab(zmat[...], me_w)
    low_own = at_slab(low_all, me_w)
    low_next = at_slab(low_all[0:1], me_w + 1)
    upp_prev = at_slab(upp_all[RY - 1 : RY], me_w - 1)
    has_under = jnp.where(me_w > 0, 1.0, 0.0)
    has_above = jnp.where(me_w < NW - 1, 1.0, 0.0)

    row_i = lax.broadcasted_iota(jnp.int32, (RY, 128), 0)
    kept = [
        jnp.where(row_i == 0, 0.0, jnp.where(row_i == 1, stc[0] * has_under, stc[0])),
        jnp.where(row_i == 0, 0.0, stc[1]),
        stc[2],
        jnp.where(row_i == RY - 1, 0.0, stc[3]),
        jnp.where(
            row_i == RY - 1, 0.0, jnp.where(row_i == RY - 2, stc[4] * has_above, stc[4])
        ),
    ]
    for m in range(5):
        coef[m] = kept[m] * inv_own
    coef[5] = jnp.where(row_i == 0, 0.0, low_own * inv_own)
    coef[6] = c_own
    edge[0] = at_slab(first_col[...], me_w)
    edge[1] = at_slab(last_col[...], me_w)
    keep_coef = pltpu.make_async_copy(edge, edge_h, osem.at[0])
    keep_coef.start()

    for way, own, scale in ((0, z_own, low_next), (1, y_own, upp_prev)):
        wmat[...] = jnp.zeros((RY + 8, 128), F32)
        for m in range(5):
            wmat[m + 2 : m + 2 + RY, :] += kept[m] * own
        wgt[way] = wmat[...] * (-scale)

    eye16 = lax.broadcasted_iota(jnp.int32, (NW, NW), 0) == lax.broadcasted_iota(
        jnp.int32, (NW, NW), 1
    )
    next16 = lax.broadcasted_iota(jnp.int32, (NW, NW), 0) + 1 == lax.broadcasted_iota(
        jnp.int32, (NW, NW), 1
    )
    prev16 = lax.broadcasted_iota(jnp.int32, (NW, NW), 0) - 1 == lax.broadcasted_iota(
        jnp.int32, (NW, NW), 1
    )
    z0 = column(zmat[0:1, 0:NW], eye16, NW)
    z1 = column(zmat[RY - 1 : RY, 0:NW], eye16, NW)
    y0 = column(ymat[0:1, 0:NW], eye16, NW)
    y1 = column(ymat[RY - 1 : RY, 0:NW], eye16, NW)
    low_n = column(low_all[0:1, 0:NW], next16, NW)
    upp_p = column(upp_all[RY - 1 : RY, 0:NW], prev16, NW)
    red[0] = upp_p * y0
    red[1] = low_n * z0
    lz1 = low_n * z1
    uy1 = upp_p * y1
    q = -lz1[0:1]
    for s in range(1, NW):
        dinv = 1.0 / (1.0 + red[0, s : s + 1, :] * q)
        c3 = uy1[s : s + 1] * dinv
        red[2, s : s + 1, :] = q * dinv
        red[3, s : s + 1, :] = dinv
        red[4, s : s + 1, :] = c3
        red[5, s : s + 1, :] = q
        q = red[1, s : s + 1, :] * q * c3 - lz1[s : s + 1]

    def own_rows(c):
        for h in range(2):
            vcopy(c, h).wait()

            @pl.loop(0, 2)
            def _(x):
                cols = [
                    pl.ds(pl.multiple_of(x * 512 + b * 128, 128), 128) for b in range(4)
                ]
                up, down = [None] * 4, [None] * 4
                for j in range(RY):
                    wu, wd = wgt[0, j + 4 : j + 5, :], wgt[1, j + 4 : j + 5, :]
                    for b in range(4):
                        u = vbuf[c, j, h * 8 : h * 8 + 8, cols[b]]
                        up[b] = wu * u if j == 0 else up[b] + wu * u
                        down[b] = wd * u if j == 0 else down[b] + wd * u
                for b in range(4):
                    send_a[c, h * 8 + x * 4 + b, 0] = up[b]
                    send_a[c, h * 8 + x * 4 + b, 1] = down[b]

    def acopy(c, k):
        to = lax.rem(me_w + k, NW)
        return pltpu.make_async_remote_copy(
            src_ref=send_a.at[c, to],
            dst_ref=recv_a.at[c, me_w],
            send_sem=as_.at[c],
            recv_sem=ar.at[c],
            device_id=(to, me_s),
            device_id_type=MESH,
        )

    def add_ends(c):
        for h in range(2):
            cells8 = slice(h * 8, h * 8 + 8)

            @pl.loop(0, 8)
            def _(x):
                cols = pl.ds(pl.multiple_of(x * 128, 128), 128)
                ends = (halo[0, c, cells8, cols], halo[1, c, cells8, cols])
                near = (
                    (tile_in[1, 0:1, :], RY - 2, tile_in[1, 1:2, :], RY - 1),
                    (tile_in[0, 2:3, :], 1, tile_in[0, 3:4, :], 0),
                )
                for way in range(2):
                    wa, ja, wb, jb = near[way]
                    send_a[c, h * 8 + x, way] += (
                        wgt[way, 3:4, :] * ends[0]
                        + wgt[way, RY + 4 : RY + 5, :] * ends[1]
                        + wa * vbuf[c, ja, cells8, cols]
                        + wb * vbuf[c, jb, cells8, cols]
                    )

    def send_up(c):
        hcopy(0, c).wait()
        hcopy(1, c).wait()
        add_ends(c)
        for k in range(1, NW):
            acopy(c, k).start()
        recv_a[c, me_w] = send_a[c, me_w]

    own_rows(0)
    own_rows(1)
    own_rows(2)

    for i in range(3, 7):
        loads[i].wait()
    slots = owner.shape[1]
    own = owner[...]
    live = lax.broadcasted_iota(jnp.int32, (1, slots), 1) < counts[0]
    wall_row = jnp.where(live, own >> 3, NW)
    key_row[0:1, :] = jnp.where(live, (own & 7) * NW + (own >> 3), 512).astype(F32)
    key_row[1:8, :] = jnp.zeros((7, slots), F32)
    lane_f = lax.broadcasted_iota(jnp.int32, (256, 128), 1).astype(F32)
    sub_f = lax.broadcasted_iota(jnp.int32, (256, 128), 0).astype(F32)
    lower_tri = [
        jnp.where(lane_f + 128.0 * b < sub_f, 1.0, 0.0) for b in range(2)
    ]

    ones = jnp.ones((128, 128), jnp.bfloat16)
    head_row = jnp.where(
        lax.broadcasted_iota(jnp.int32, (8, 128), 0) == 0, 1.0, 0.0
    ).astype(jnp.bfloat16)

    def rank_block(i, carry):
        at = pl.ds(pl.multiple_of(i * 256, 256), 256)
        tile = key_row[:, at]
        col = lax.dot_general(
            tile.T.astype(jnp.bfloat16), head_row, nn, preferred_element_type=F32
        )
        hit = col == lane_f
        score = jnp.where(hit, carry, 0.0)
        for b in range(2):
            same = col == tile[0:1, b * 128 : b * 128 + 128]
            score = score + jnp.where(same, lower_tri[b], 0.0)
        rank = lax.dot_general(
            score.astype(jnp.bfloat16), ones, nn, preferred_element_type=F32
        )
        place = jnp.floor(col * (1.0 / NW)) * SLOTS + rank
        for b in range(4):
            right[at, b * 128 : b * 128 + 128] = jnp.where(
                place == lane_f + 128.0 * b, 1.0, 0.0
            ).astype(jnp.bfloat16)
        return carry + jnp.sum(jnp.where(hit, 1.0, 0.0), axis=0, keepdims=True)

    blocks = slots // 256
    carry = lax.fori_loop(
        0, blocks // 2, rank_block, jnp.zeros((1, 128), F32), unroll=4
    )
    tcopy(0).wait()
    tcopy(1).wait()
    send_up(0)
    in_wall = lax.broadcasted_iota(jnp.int32, (NW, slots), 0) == wall_row
    load = [forces[c : c + 1, :] for c in range(3)] + [cells[...].astype(F32)]
    for part in range(3):
        head = [x.astype(jnp.bfloat16).astype(F32) for x in load]
        load = [x - y for x, y in zip(load, head)]
        for c in range(4):
            r0 = (part * 4 + c) * NW
            left[r0 : r0 + NW, :] = jnp.where(in_wall, head[c], 0.0).astype(jnp.bfloat16)
    send_up(1)
    carry = lax.fori_loop(blocks // 2, blocks * 3 // 4, rank_block, carry, unroll=4)
    send_up(2)
    lax.fori_loop(blocks * 3 // 4, blocks, rank_block, carry, unroll=4)
    made = lax.dot_general(left[...], right[...], nn, preferred_element_type=F32)
    made = made[0:64] + made[64:128] + made[128:192]
    first = lax.broadcasted_iota(jnp.int32, (NW, 128), 1) < SLOTS
    for k in range(NS):
        for b in range(2):
            pair = [
                made[c * NW : c * NW + NW, k // 2 * 128 : k // 2 * 128 + 128]
                for c in (2 * b, 2 * b + 1)
            ]
            turn = 1 - k % 2
            pair[turn] = pltpu.roll(pair[turn], SLOTS, 1)
            pack[b, k * NW : k * NW + NW, :] = jnp.where(first, pair[0], pair[1])

    def p1copy(k):
        to = lax.rem(me_s + k, NS)
        return pltpu.make_async_remote_copy(
            src_ref=pack.at[:, pl.ds(pl.multiple_of(to * NW, NW), NW)],
            dst_ref=recv1.at[:, pl.ds(pl.multiple_of(me_s * NW, NW), NW)],
            send_sem=p1s.at[0],
            recv_sem=p1r.at[0],
            device_id=(me_w, to),
            device_id_type=MESH,
        )

    for k in range(1, NS):
        p1copy(k).start()
    mine = pl.ds(pl.multiple_of(me_s * NW, NW), NW)
    recv1[:, mine, :] = pack[:, mine, :]

    def solve(c):
        wait_all(send_a.at[c, pl.ds(0, NW - 1)], recv_a.at[c, pl.ds(0, NW - 1)], as_, ar, c)
        p = recv_a[c, 0, 0]
        for s in range(1, NW):
            pbuf[s] = p
            e = recv_a[c, s, 1] - red[0, s : s + 1, :] * p
            elim[s] = e
            if s < NW - 1:
                p = recv_a[c, s, 0] - red[1, s : s + 1, :] * (
                    p + red[2, s : s + 1, :] * e
                )
        down = jnp.zeros((8, 128), F32)
        send_f[c, NW - 1, 1] = down
        for s in range(NW - 1, 0, -1):
            down = red[3, s : s + 1, :] * elim[s] - red[4, s : s + 1, :] * down
            send_f[c, s - 1, 1] = down
            send_f[c, s, 0] = pbuf[s] + red[5, s : s + 1, :] * down
        send_f[c, 0, 0] = jnp.zeros((8, 128), F32)

    def send_down(c):
        for k in range(1, NW):
            fcopy(c, k).start()

    def fcopy(c, k):
        to = lax.rem(me_w + k, NW)
        return pltpu.make_async_remote_copy(
            src_ref=send_f.at[c, to],
            dst_ref=bound.at[c, me_w],
            send_sem=fs.at[c],
            recv_sem=fr.at[c],
            device_id=(to, me_s),
            device_id_type=MESH,
        )

    def keep_base(c):
        return pltpu.make_async_copy(vbuf.at[c], base_h.at[c], bsem.at[c])

    def particular(c):
        @pl.loop(0, 4)
        def _(xx):
            tiles = range(2)
            cols = [
                pl.ds(pl.multiple_of(xx * 256 + t * 128, 128), 128) for t in tiles
            ]

            def row(i):
                if i < -1 or i > RY:
                    return None
                if i == -1:
                    return [halo[0, c, :, cols[t]] for t in tiles]
                if i == RY:
                    return [halo[1, c, :, cols[t]] for t in tiles]
                return [vbuf[c, i, :, cols[t]] for t in tiles]

            window = [row(i) for i in range(-2, 3)]
            prev = [None, None]
            for j in range(RY):
                total = [None, None]
                for m in range(5):
                    if window[m] is None or j + m - 2 == -1 and j == 0:
                        continue
                    if j + m - 2 == RY and j == RY - 1:
                        continue
                    weight = coef[m, j : j + 1, :]
                    for t in tiles:
                        term = weight * window[m][t]
                        total[t] = term if total[t] is None else total[t] + term
                if j > 0:
                    for t in tiles:
                        total[t] = total[t] - coef[5, j : j + 1, :] * prev[t]
                prev = total
                window = window[1:] + [row(j + 3)]
                for t in tiles:
                    vbuf[c, j, :, cols[t]] = total[t]
            for j in range(RY - 2, -1, -1):
                weight = coef[6, j : j + 1, :]
                for t in tiles:
                    prev[t] = vbuf[c, j, :, cols[t]] - weight * prev[t]
                    vbuf[c, j, :, cols[t]] = prev[t]

        keep_base(c).start()

    particular(0)
    solve(0)
    send_down(0)
    solve(1)
    send_down(1)
    solve(2)
    wait_all(pack.at[:, pl.ds(0, NW * (NS - 1))], recv1.at[:, pl.ds(0, NW * (NS - 1))], p1s, p1r)
    for w in range(NW):
        for b in range(2):
            pack2[w, b] = recv1[b, pl.ds(w, NS, stride=NW), :]

    def p2copy(k):
        to = lax.rem(me_w + k, NW)
        return pltpu.make_async_remote_copy(
            src_ref=pack2.at[to],
            dst_ref=recv2.at[me_w],
            send_sem=p2s.at[0],
            recv_sem=p2r.at[0],
            device_id=(to, me_s),
            device_id_type=MESH,
        )

    for k in range(1, NW):
        p2copy(k).start()
    recv2[me_w] = pack2[me_w]

    send_down(2)
    keep_own = pltpu.make_async_copy(send_f.at[:, me_w], bound.at[:, me_w], osem.at[2])
    keep_own.start()
    particular(1)
    particular(2)

    wait_all(pack2.at[pl.ds(0, NW - 1)], recv2.at[pl.ds(0, NW - 1)], p2s, p2r)
    part_t[0:128, :] = recv2[:, 0].reshape(NW * NS, 128).T
    rest = recv2[:, 1].reshape(NW * NS, 128)
    flipped = rest.T
    part_t[128:192, :] = flipped[0:64]
    part_t[192:256, :] = (flipped[64:128].astype(jnp.int32) & 127).astype(F32)
    place = rest.astype(jnp.int32)
    rows_v[...] = (
        (place >> 13) * 64 + ((place >> 7) & 7) * 8 + ((place >> 10) & 7)
    ) * 4
    keep_part = pltpu.make_async_copy(part_t, part_h, osem.at[3])
    keep_part.start()
    keep_rows = pltpu.make_async_copy(rows_v, rows_h, osem.at[4])
    keep_rows.start()

    for c in range(3):
        wait_all(send_f.at[c, pl.ds(0, NW - 1)], bound.at[c, pl.ds(0, NW - 1)], fs, fr, c)
    for c in range(3):
        keep_base(c).wait()
    for keep in (keep_coef, keep_own, keep_part, keep_rows):
        keep.wait()


def exchange(vel, lower, upper, st, forces, owner, cells, counts):
    hbm = pl.BlockSpec(memory_space=pl.ANY)
    dma = pltpu.SemaphoreType.DMA
    return pl.pallas_call(
        exchange_kernel,
        out_shape=(
            jax.ShapeDtypeStruct((3, RY, SZ, NX), F32),
            jax.ShapeDtypeStruct((3, NW, 2, 8, 128), F32),
            jax.ShapeDtypeStruct((2, RY, 128), F32),
            jax.ShapeDtypeStruct((256, 128), F32),
            jax.ShapeDtypeStruct((128, 128), jnp.int32),
        ),
        in_specs=[hbm] * 8,
        out_specs=[hbm] * 5,
        scratch_shapes=[
            pltpu.VMEM((1, NW * RY), F32),
            pltpu.VMEM((1, NW * RY), F32),
            pltpu.VMEM(st.shape, F32),
            pltpu.VMEM(forces.shape, F32),
            pltpu.VMEM(owner.shape, jnp.int32),
            pltpu.VMEM(cells.shape, jnp.int32),
            pltpu.SMEM((1,), jnp.int32),
            pltpu.VMEM((2, 3, SZ, NX), F32),
            pltpu.VMEM((7, RY, 128), F32),
            pltpu.VMEM((2, RY, 128), F32),
            pltpu.VMEM((256, 128), F32),
            pltpu.VMEM((128, 128), jnp.int32),
            pltpu.VMEM((8, owner.shape[1]), F32),
            pltpu.VMEM((12 * NW, owner.shape[1]), jnp.bfloat16),
            pltpu.VMEM((owner.shape[1], NS * SLOTS), jnp.bfloat16),
            pltpu.VMEM((3, RY, SZ, NX), F32),
            pltpu.VMEM((3, NW, 2, 8, 128), F32),
            pltpu.VMEM((3, NW, 2, 8, 128), F32),
            pltpu.VMEM((3, NW, 2, 8, 128), F32),
            pltpu.VMEM((NW, 8, 128), F32),
            pltpu.VMEM((NW, 8, 128), F32),
            pltpu.VMEM((8, 128), F32),
            pltpu.VMEM((2, 8, 128), F32),
            pltpu.VMEM((2, NW * NS, 128), F32),
            pltpu.VMEM((2, NW * NS, 128), F32),
            pltpu.VMEM((NW, 2, NS, 128), F32),
            pltpu.VMEM((NW, 2, NS, 128), F32),
            pltpu.VMEM((RY, 128), F32),
            pltpu.VMEM((RY, 128), F32),
            pltpu.VMEM((RY, 128), F32),
            pltpu.VMEM((RY, 128), F32),
            pltpu.VMEM((RY, 128), F32),
            pltpu.VMEM((RY, 128), F32),
            pltpu.VMEM((RY, 128), F32),
            pltpu.VMEM((RY, 128), F32),
            pltpu.VMEM((RY + 8, 128), F32),
            pltpu.VMEM((2, RY + 8, 128), F32),
            pltpu.VMEM((6, NW, 128), F32),
            dma((7,)), dma((5,)), dma((3,)), dma((6,)), dma((6,)), dma((6,)), dma((2,)), dma((2,)),
            *[dma((3,))] * 4, *[dma((1,))] * 4,
        ],
        compiler_params=pltpu.CompilerParams(
            collective_id=0, has_side_effects=True, vmem_limit_bytes=56 << 20
        ),
        name="exchange",
    )(vel, lower, upper, st, forces, owner, cells, counts)


def local_kernel(
    base, bound_h, edge_h, part_h, rows_h, inv_vol,
    derivative, forcing,
    bound, edge, part_t, rows,
    acc0, acc1, acc2, acc3, even, odd, mixed, vbuf, stage, isem, vsem, dsem, fsem,
):
    def take(c, x):
        part = (c, slice(None), slice(None), pl.ds(pl.multiple_of(x * 512, 512), 512))
        return pltpu.make_async_copy(base.at[part], vbuf.at[part], vsem.at[c * 2 + x])

    staged = ((edge_h, edge), (bound_h, bound), (part_h, part_t), (rows_h, rows))
    loads = [
        pltpu.make_async_copy(src, dst, isem.at[i]) for i, (src, dst) in enumerate(staged)
    ]
    for load in loads:
        load.start()
    for c in range(3):
        for half in range(2):
            take(c, half).start()

    accs = (acc0, acc1, acc2, acc3)
    depth = acc0.shape[0]

    @pl.loop(0, 128)
    def _(i):
        at = pl.ds(pl.multiple_of(i * (depth // 128), depth // 128), depth // 128)
        for acc in accs:
            acc[at, :] = jnp.zeros((depth // 128, 128), F32)

    lane = lax.broadcasted_iota(jnp.int32, (8, 128), 1).astype(F32)

    def spread(source, to):
        pick = jnp.full((8, 128), source, jnp.int32)
        for g in range(SLOTS // 8):
            xl = jnp.take_along_axis(part_t[192 + g * 8 : 200 + g * 8, :], pick, axis=1)
            hit = xl == lane
            for c in range(3):
                r0 = c * SLOTS + g * 8
                f = jnp.take_along_axis(part_t[r0 : r0 + 8, :], pick, axis=1)
                to[pl.ds(g * 32 + c, 8, stride=4), :] = jnp.where(hit, f, 0.0)

    group = 2

    def add(source, frm, steps):
        base = source * 128 + SLOTS
        for r0 in range(0, SLOTS, 4 * group):
            for k in range(4):
                slots = [r0 + k + 4 * g for g in range(group)]
                first = [rows[base + r] for r in slots]
                at = [pl.ds(pl.multiple_of(f, 4), 4) for f in first]
                value = [frm[r * 4 : r * 4 + 4, :] for r in slots]
                held = [accs[k][a, :] for a in at]
                for g in range(group):
                    held[g] = held[g] + value[g]
                    for e in range(g):
                        held[g] = held[g] + jnp.where(first[e] == first[g], value[e], 0.0)
                for g in range(group):
                    accs[k][at[g], :] = held[g]
                if k % 2 == 1:
                    next(steps, None)

    even[...] = jnp.zeros((256, 128), F32)
    odd[...] = jnp.zeros((256, 128), F32)
    for load in loads:
        load.wait()
    spread(0, even)

    def put_d(c, x):
        part = (c, slice(None), slice(None), pl.ds(pl.multiple_of(x * 512, 512), 512))
        return pltpu.make_async_copy(vbuf.at[part], derivative.at[part], dsem.at[c * 2 + x])

    def join_steps(c, h, x):
        here = (pl.ds(pl.multiple_of(h * 8, 8), 8), pl.ds(pl.multiple_of(x * 128, 128), 128))
        under, above = bound[c, h * 8 + x, 0], bound[c, h * 8 + x, 1]
        for j in range(RY):
            vbuf[c, j, *here] = vbuf[c, j, *here] + (
                edge[0, j : j + 1, :] * under + edge[1, j : j + 1, :] * above
            )
            yield

    def scatter_pair(i, steps):
        spread(2 * i + 1, odd)
        add(2 * i, even, steps)
        spread(jnp.minimum(2 * i + 2, 127), even)
        add(2 * i + 1, odd, steps)
        for _rest in steps:
            pass

    @pl.loop(0, 6)
    def _(q):
        c, half = q // 2, q % 2
        take(c, half).wait()

        @pl.loop(0, 8)
        def _(t):
            scatter_pair(q * 8 + t, join_steps(c, t // 4, half * 4 + t % 4))

        put_d(c, half).start()

    @pl.loop(48, 64)
    def _(i):
        scatter_pair(i, iter(()))

    def put_f(b):
        part = (slice(None), pl.ds(b * 2, 2))
        return pltpu.make_async_copy(stage.at[part], forcing.at[part], fsem.at[b])

    @pl.loop(0, 16)
    def _(b):
        @pl.loop(0, 4)
        def _(jh):
            j, h = b * 2 + jh // 2, jh % 2
            scale = -inv_vol[j]
            cells = pl.ds(pl.multiple_of(h * 8, 8), 8)
            for x in range(8):
                at = pl.ds(pl.multiple_of(((j * 2 + h) * 8 + x) * 32, 32), 32)
                mixed[x * 32 : x * 32 + 32, :] = scale * (
                    (acc0[at, :] + acc1[at, :]) + (acc2[at, :] + acc3[at, :])
                )
            for x in range(8):
                for c in range(3):
                    stage[c, j, cells, x * 128 : x * 128 + 128] = mixed[
                        pl.ds(x * 32 + c, 8, stride=4), :
                    ]

        put_f(b).start()

    for c in range(3):
        for half in range(2):
            put_d(c, half).wait()

    @pl.loop(0, 16)
    def _(b):
        put_f(b).wait()


def local(base, bound, edge, part_t, rows, inv_vol):
    sm = pl.BlockSpec(memory_space=pltpu.SMEM)
    hbm = pl.BlockSpec(memory_space=pl.ANY)
    depth = RY * SZ * NX // 128 * 4
    whole = (3, RY, SZ, NX)
    return pl.pallas_call(
        local_kernel,
        out_shape=(jax.ShapeDtypeStruct(whole, F32), jax.ShapeDtypeStruct(whole, F32)),
        in_specs=[hbm] * 5 + [sm],
        out_specs=(hbm, hbm),
        scratch_shapes=[
            pltpu.VMEM(bound.shape, F32),
            pltpu.VMEM(edge.shape, F32),
            pltpu.VMEM(part_t.shape, F32),
            pltpu.SMEM(rows.shape, jnp.int32),
        ]
        + [pltpu.VMEM((depth, 128), F32)] * 4
        + [pltpu.VMEM((256, 128), F32)] * 3
        + [pltpu.VMEM(whole, F32)] * 2
        + [pltpu.SemaphoreType.DMA((n,)) for n in (4, 6, 6, 16)],
        compiler_params=pltpu.CompilerParams(vmem_limit_bytes=58 << 20),
        name="local",
    )(base, bound, edge, part_t, rows, inv_vol)


def body(velocity, lower, upper, stencil, inv_volume, forces, owner, cells, counts):
    base, bound, edge, part_t, rows = exchange(
        velocity, lower.reshape(1, -1), upper.reshape(1, -1), stencil, forces,
        owner.reshape(1, -1), cells.reshape(1, -1), counts,
    )
    derivative, forcing = local(base, bound, edge, part_t, rows.reshape(-1), inv_volume)
    return derivative, forcing


def solution(mesh):
    in_specs = (
        P(None, "wall", "span", None),
        P(),
        P(),
        P(None, "wall"),
        P("wall"),
        P(None, ("wall", "span")),
        P(("wall", "span"), None),
        P(("wall", "span")),
        P(("wall", "span")),
    )
    out_specs = (P(None, "wall", "span", None), P(None, "wall", "span", None))
    return jax.shard_map(body, mesh=mesh, in_specs=in_specs, out_specs=out_specs, check_vma=False)
```

```python
import functools

import jax
import jax.numpy as jnp
from jax import lax
from jax.experimental import pallas as pl
from jax.experimental.pallas import tpu as pltpu
from jax.sharding import PartitionSpec as P

F32 = jnp.float32
MESH = pl.DeviceIdType.MESH
NW, NS = 16, 8
RY, SZ, NX = 32, 16, 1024
SLOTS = 64


def exchange_kernel(
    vel, lower_h, upper_h, st_h, forces_h, owner_h, cells_h, counts_h,
    base_h, bound, edge_h, part_h, rows_h,
    lower, upper, st, forces, owner, cells, counts, halo, coef, edge, part_t, rows_v,
    key_row, left, right, vbuf, send_a, recv_a, send_f, land, elim, pbuf, tile_out, tile_in,
    pack, recv1, pack2, recv2,
    lmat, umat, dmat, cmat, ymat, zmat, first_col, last_col, wmat, wgt, red,
    isem, osem, bsem, vsem, hs, hr, ts, tr, as_, ar, fs, fr, p1s, p1r, p2s, p2r,
):
    me_w = lax.axis_index("wall")
    me_s = lax.axis_index("span")

    def wait_all(src, dst, sent, got, i=0):
        group = pltpu.make_async_remote_copy(
            src_ref=src,
            dst_ref=dst,
            send_sem=sent.at[i],
            recv_sem=got.at[i],
            device_id=(me_w, me_s),
            device_id_type=MESH,
        )
        group.wait_send()
        group.wait_recv()

    def vcopy(c, h):
        part = (c, slice(None), pl.ds(h * 8, 8), slice(None))
        return pltpu.make_async_copy(vel.at[part], vbuf.at[part], vsem.at[c * 2 + h])

    barrier = pltpu.get_barrier_semaphore()

    @pl.loop(1, NW)
    def _(k):
        pl.semaphore_signal(
            barrier, inc=1, device_id=(lax.rem(me_w + k, NW), me_s), device_id_type=MESH
        )

    @pl.loop(1, NS)
    def _(k):
        pl.semaphore_signal(
            barrier, inc=1, device_id=(me_w, lax.rem(me_s + k, NS)), device_id_type=MESH
        )

    staged = (
        (st_h, st), (lower_h, lower), (upper_h, upper),
        (forces_h, forces), (owner_h, owner), (cells_h, cells), (counts_h, counts),
    )
    loads = [
        pltpu.make_async_copy(src, dst, isem.at[i]) for i, (src, dst) in enumerate(staged)
    ]
    for i in range(3):
        loads[i].start()
    for c in range(3):
        for h in range(2):
            vcopy(c, h).start()
    for i in range(3, 7):
        loads[i].start()
    pl.semaphore_wait(barrier, NW - 1 + NS - 1)

    above = lax.rem(me_w + 1, NW)
    under = lax.rem(me_w + NW - 1, NW)

    def hcopy(way, c):
        return pltpu.make_async_remote_copy(
            src_ref=vel.at[c, RY - 1 if way == 0 else 0],
            dst_ref=halo.at[way, c],
            send_sem=hs.at[way * 3 + c],
            recv_sem=hr.at[way * 3 + c],
            device_id=(above if way == 0 else under, me_s),
            device_id_type=MESH,
        )

    hcopy(0, 0).start()
    hcopy(1, 0).start()

    for i in range(3):
        loads[i].wait()
    eye = lax.broadcasted_iota(jnp.int32, (RY, RY), 0) == lax.broadcasted_iota(
        jnp.int32, (RY, RY), 1
    )

    def column(row, mask, n):
        full = jnp.broadcast_to(row, (n, n))
        col = jnp.sum(jnp.where(mask, full, 0.0), axis=1, keepdims=True)
        return jnp.broadcast_to(col, (n, 128))

    stc = [column(st[m : m + 1, :], eye, RY) for m in range(5)]
    tile_out[0:1, :] = stc[0][0:1]
    tile_out[1:2, :] = stc[1][0:1]
    tile_out[2:3, :] = stc[4][RY - 1 : RY]
    tile_out[3:4, :] = stc[3][RY - 1 : RY]
    tile_out[4:8, :] = jnp.zeros((4, 128), F32)

    def tcopy(way):
        return pltpu.make_async_remote_copy(
            src_ref=tile_out,
            dst_ref=tile_in.at[way],
            send_sem=ts.at[way],
            recv_sem=tr.at[way],
            device_id=(above if way == 0 else under, me_s),
            device_id_type=MESH,
        )

    tcopy(0).start()
    tcopy(1).start()
    for c in (1, 2):
        hcopy(0, c).start()
        hcopy(1, c).start()


    nn = (((1,), (0,)), ((), ()))
    lane_i = lax.broadcasted_iota(jnp.int32, (RY, NW * RY), 1)
    in_row = (lane_i & (RY - 1)) == lax.broadcasted_iota(jnp.int32, (RY, NW * RY), 0)
    to_slab = (
        lax.broadcasted_iota(jnp.int32, (NW * RY, 128), 0) // RY
        == lax.broadcasted_iota(jnp.int32, (NW * RY, 128), 1)
    ).astype(F32).astype(jnp.bfloat16)
    both = jnp.concatenate(
        [
            jnp.where(in_row, jnp.broadcast_to(v[0:1, :], (RY, NW * RY)), 0.0)
            for v in (lower, upper)
        ],
        axis=0,
    )
    tall = None
    for _part in range(3):
        head = both.astype(jnp.bfloat16)
        both = both - head.astype(F32)
        term = lax.dot_general(head, to_slab, nn, preferred_element_type=F32)
        tall = term if tall is None else tall + term
    lmat[...] = tall[0:RY]
    umat[...] = tall[RY : 2 * RY]

    zero = jnp.zeros((1, 128), F32)
    carry_c, carry_b = zero, None
    for j in range(RY):
        low, upp = lmat[j : j + 1, :], umat[j : j + 1, :]
        inv = 1.0 / (1.0 - low * carry_c) if j > 0 else jnp.ones((1, 128), F32)
        carry_c = upp * inv
        dmat[j : j + 1, :] = inv
        cmat[j : j + 1, :] = carry_c
    binv = [None] * RY
    for j in range(RY - 1, -1, -1):
        if j == RY - 1:
            binv[j] = jnp.ones((1, 128), F32)
        else:
            binv[j] = 1.0 / (
                1.0 - umat[j : j + 1, :] * lmat[j + 1 : j + 2, :] * binv[j + 1]
            )
    y = binv[0]
    ymat[0:1, :] = y
    for j in range(1, RY):
        y = -(umat[j - 1 : j, :] * binv[j]) * y
        ymat[j : j + 1, :] = y
    z = dmat[RY - 1 : RY, :]
    zmat[RY - 1 : RY, :] = z
    for j in range(RY - 2, -1, -1):
        z = -(lmat[j + 1 : j + 2, :] * dmat[j : j + 1, :]) * z
        zmat[j : j + 1, :] = z
    v = binv[0]
    first_col[0:1, :] = v
    for j in range(1, RY):
        v = -(lmat[j : j + 1, :] * binv[j]) * v
        first_col[j : j + 1, :] = v
    v = dmat[RY - 1 : RY, :]
    last_col[RY - 1 : RY, :] = v
    for j in range(RY - 2, -1, -1):
        v = -cmat[j : j + 1, :] * v
        last_col[j : j + 1, :] = v

    lane16 = lax.broadcasted_iota(jnp.int32, (RY, 128), 1)

    def at_slab(values, slab):
        n = values.shape[0]
        col = jnp.sum(jnp.where(lane16[0:n] == slab, values, 0.0), axis=1, keepdims=True)
        return jnp.broadcast_to(col, (n, 128))

    low_all, upp_all = lmat[...], umat[...]
    inv_own = at_slab(dmat[...], me_w)
    c_own = at_slab(cmat[...], me_w)
    y_own = at_slab(ymat[...], me_w)
    z_own = at_slab(zmat[...], me_w)
    low_own = at_slab(low_all, me_w)
    low_next = at_slab(low_all[0:1], me_w + 1)
    upp_prev = at_slab(upp_all[RY - 1 : RY], me_w - 1)
    has_under = jnp.where(me_w > 0, 1.0, 0.0)
    has_above = jnp.where(me_w < NW - 1, 1.0, 0.0)

    row_i = lax.broadcasted_iota(jnp.int32, (RY, 128), 0)
    kept = [
        jnp.where(row_i == 0, 0.0, jnp.where(row_i == 1, stc[0] * has_under, stc[0])),
        jnp.where(row_i == 0, 0.0, stc[1]),
        stc[2],
        jnp.where(row_i == RY - 1, 0.0, stc[3]),
        jnp.where(
            row_i == RY - 1, 0.0, jnp.where(row_i == RY - 2, stc[4] * has_above, stc[4])
        ),
    ]
    for m in range(5):
        coef[m] = kept[m] * inv_own
    coef[5] = jnp.where(row_i == 0, 0.0, low_own * inv_own)
    coef[6] = c_own
    edge[0] = at_slab(first_col[...], me_w)
    edge[1] = at_slab(last_col[...], me_w)
    keep_coef = pltpu.make_async_copy(edge, edge_h, osem.at[0])
    keep_coef.start()

    for way, own, scale in ((0, z_own, low_next), (1, y_own, upp_prev)):
        wmat[...] = jnp.zeros((RY + 8, 128), F32)
        for m in range(5):
            wmat[m + 2 : m + 2 + RY, :] += kept[m] * own
        wgt[way] = wmat[...] * (-scale)

    eye16 = lax.broadcasted_iota(jnp.int32, (NW, NW), 0) == lax.broadcasted_iota(
        jnp.int32, (NW, NW), 1
    )
    next16 = lax.broadcasted_iota(jnp.int32, (NW, NW), 0) + 1 == lax.broadcasted_iota(
        jnp.int32, (NW, NW), 1
    )
    prev16 = lax.broadcasted_iota(jnp.int32, (NW, NW), 0) - 1 == lax.broadcasted_iota(
        jnp.int32, (NW, NW), 1
    )
    z0 = column(zmat[0:1, 0:NW], eye16, NW)
    z1 = column(zmat[RY - 1 : RY, 0:NW], eye16, NW)
    y0 = column(ymat[0:1, 0:NW], eye16, NW)
    y1 = column(ymat[RY - 1 : RY, 0:NW], eye16, NW)
    low_n = column(low_all[0:1, 0:NW], next16, NW)
    upp_p = column(upp_all[RY - 1 : RY, 0:NW], prev16, NW)
    red[0] = upp_p * y0
    red[1] = low_n * z0
    lz1 = low_n * z1
    uy1 = upp_p * y1
    q = -lz1[0:1]
    for s in range(1, NW):
        dinv = 1.0 / (1.0 + red[0, s : s + 1, :] * q)
        c3 = uy1[s : s + 1] * dinv
        red[2, s : s + 1, :] = q * dinv
        red[3, s : s + 1, :] = dinv
        red[4, s : s + 1, :] = c3
        red[5, s : s + 1, :] = q
        q = red[1, s : s + 1, :] * q * c3 - lz1[s : s + 1]

    def own_rows(c):
        for h in range(2):
            vcopy(c, h).wait()

            @pl.loop(0, 2)
            def _(x):
                cols = [
                    pl.ds(pl.multiple_of(x * 512 + b * 128, 128), 128) for b in range(4)
                ]
                up, down = [None] * 4, [None] * 4
                for j in range(RY):
                    wu, wd = wgt[0, j + 4 : j + 5, :], wgt[1, j + 4 : j + 5, :]
                    for b in range(4):
                        u = vbuf[c, j, h * 8 : h * 8 + 8, cols[b]]
                        up[b] = wu * u if j == 0 else up[b] + wu * u
                        down[b] = wd * u if j == 0 else down[b] + wd * u
                for b in range(4):
                    send_a[c, h * 8 + x * 4 + b, 0] = up[b]
                    send_a[c, h * 8 + x * 4 + b, 1] = down[b]

    def acopy(c, k):
        to = lax.rem(me_w + k, NW)
        return pltpu.make_async_remote_copy(
            src_ref=send_a.at[c, to],
            dst_ref=recv_a.at[c, me_w],
            send_sem=as_.at[c],
            recv_sem=ar.at[c],
            device_id=(to, me_s),
            device_id_type=MESH,
        )

    def add_ends(c):
        for h in range(2):
            cells8 = slice(h * 8, h * 8 + 8)

            @pl.loop(0, 8)
            def _(x):
                cols = pl.ds(pl.multiple_of(x * 128, 128), 128)
                ends = (halo[0, c, cells8, cols], halo[1, c, cells8, cols])
                near = (
                    (tile_in[1, 0:1, :], RY - 2, tile_in[1, 1:2, :], RY - 1),
                    (tile_in[0, 2:3, :], 1, tile_in[0, 3:4, :], 0),
                )
                for way in range(2):
                    wa, ja, wb, jb = near[way]
                    send_a[c, h * 8 + x, way] += (
                        wgt[way, 3:4, :] * ends[0]
                        + wgt[way, RY + 4 : RY + 5, :] * ends[1]
                        + wa * vbuf[c, ja, cells8, cols]
                        + wb * vbuf[c, jb, cells8, cols]
                    )

    def send_up(c):
        hcopy(0, c).wait()
        hcopy(1, c).wait()
        add_ends(c)
        for k in range(1, NW):
            acopy(c, k).start()
        recv_a[c, me_w] = send_a[c, me_w]

    own_rows(0)
    own_rows(1)
    own_rows(2)

    for i in range(3, 7):
        loads[i].wait()
    slots = owner.shape[1]
    own = owner[...]
    live = lax.broadcasted_iota(jnp.int32, (1, slots), 1) < counts[0]
    wall_row = jnp.where(live, own >> 3, NW)
    key_row[0:1, :] = jnp.where(live, (own & 7) * NW + (own >> 3), 512).astype(F32)
    key_row[1:8, :] = jnp.zeros((7, slots), F32)
    lane_f = lax.broadcasted_iota(jnp.int32, (256, 128), 1).astype(F32)
    sub_f = lax.broadcasted_iota(jnp.int32, (256, 128), 0).astype(F32)
    lower_tri = [
        jnp.where(lane_f + 128.0 * b < sub_f, 1.0, 0.0) for b in range(2)
    ]

    ones = jnp.ones((128, 128), jnp.bfloat16)
    head_row = jnp.where(
        lax.broadcasted_iota(jnp.int32, (8, 128), 0) == 0, 1.0, 0.0
    ).astype(jnp.bfloat16)

    def rank_block(i, carry):
        at = pl.ds(pl.multiple_of(i * 256, 256), 256)
        tile = key_row[:, at]
        col = lax.dot_general(
            tile.T.astype(jnp.bfloat16), head_row, nn, preferred_element_type=F32
        )
        hit = col == lane_f
        score = jnp.where(hit, carry, 0.0)
        for b in range(2):
            same = col == tile[0:1, b * 128 : b * 128 + 128]
            score = score + jnp.where(same, lower_tri[b], 0.0)
        rank = lax.dot_general(
            score.astype(jnp.bfloat16), ones, nn, preferred_element_type=F32
        )
        place = jnp.floor(col * (1.0 / NW)) * SLOTS + rank
        for b in range(4):
            right[at, b * 128 : b * 128 + 128] = jnp.where(
                place == lane_f + 128.0 * b, 1.0, 0.0
            ).astype(jnp.bfloat16)
        return carry + jnp.sum(jnp.where(hit, 1.0, 0.0), axis=0, keepdims=True)

    blocks = slots // 256
    carry = lax.fori_loop(
        0, blocks // 2, rank_block, jnp.zeros((1, 128), F32), unroll=4
    )
    tcopy(0).wait()
    tcopy(1).wait()
    send_up(0)
    in_wall = lax.broadcasted_iota(jnp.int32, (NW, slots), 0) == wall_row
    load = [forces[c : c + 1, :] for c in range(3)] + [cells[...].astype(F32)]
    for part in range(3):
        head = [x.astype(jnp.bfloat16).astype(F32) for x in load]
        load = [x - y for x, y in zip(load, head)]
        for c in range(4):
            r0 = (part * 4 + c) * NW
            left[r0 : r0 + NW, :] = jnp.where(in_wall, head[c], 0.0).astype(jnp.bfloat16)
    send_up(1)
    carry = lax.fori_loop(blocks // 2, blocks * 3 // 4, rank_block, carry, unroll=4)
    send_up(2)
    lax.fori_loop(blocks * 3 // 4, blocks, rank_block, carry, unroll=4)
    made = lax.dot_general(left[...], right[...], nn, preferred_element_type=F32)
    made = made[0:64] + made[64:128] + made[128:192]
    first = lax.broadcasted_iota(jnp.int32, (NW, 128), 1) < SLOTS
    for k in range(NS):
        for b in range(2):
            pair = [
                made[c * NW : c * NW + NW, k // 2 * 128 : k // 2 * 128 + 128]
                for c in (2 * b, 2 * b + 1)
            ]
            turn = 1 - k % 2
            pair[turn] = pltpu.roll(pair[turn], SLOTS, 1)
            pack[b, k * NW : k * NW + NW, :] = jnp.where(first, pair[0], pair[1])

    def p1copy(k):
        to = lax.rem(me_s + k, NS)
        return pltpu.make_async_remote_copy(
            src_ref=pack.at[:, pl.ds(pl.multiple_of(to * NW, NW), NW)],
            dst_ref=recv1.at[:, pl.ds(pl.multiple_of(me_s * NW, NW), NW)],
            send_sem=p1s.at[0],
            recv_sem=p1r.at[0],
            device_id=(me_w, to),
            device_id_type=MESH,
        )

    for k in range(1, NS):
        p1copy(k).start()
    mine = pl.ds(pl.multiple_of(me_s * NW, NW), NW)
    recv1[:, mine, :] = pack[:, mine, :]

    def solve(c):
        wait_all(send_a.at[c, pl.ds(0, NW - 1)], recv_a.at[c, pl.ds(0, NW - 1)], as_, ar, c)
        p = recv_a[c, 0, 0]
        for s in range(1, NW):
            pbuf[s] = p
            e = recv_a[c, s, 1] - red[0, s : s + 1, :] * p
            elim[s] = e
            if s < NW - 1:
                p = recv_a[c, s, 0] - red[1, s : s + 1, :] * (
                    p + red[2, s : s + 1, :] * e
                )
        down = jnp.zeros((8, 128), F32)
        send_f[c, NW - 1, 1] = down
        for s in range(NW - 1, 0, -1):
            down = red[3, s : s + 1, :] * elim[s] - red[4, s : s + 1, :] * down
            send_f[c, s - 1, 1] = down
            send_f[c, s, 0] = pbuf[s] + red[5, s : s + 1, :] * down
        send_f[c, 0, 0] = jnp.zeros((8, 128), F32)

    def send_down(c):
        for k in range(1, NW):
            fcopy(c, k).start()

    def fcopy(c, k):
        to = lax.rem(me_w + k, NW)
        return pltpu.make_async_remote_copy(
            src_ref=send_f.at[c, to],
            dst_ref=land.at[c, me_w] if c < 2 else bound.at[me_w],
            send_sem=fs.at[c],
            recv_sem=fr.at[c],
            device_id=(to, me_s),
            device_id_type=MESH,
        )

    def keep_base(c):
        return pltpu.make_async_copy(vbuf.at[c], base_h.at[c], bsem.at[c])

    def particular(c):
        @pl.loop(0, 4)
        def _(xx):
            tiles = range(2)
            cols = [
                pl.ds(pl.multiple_of(xx * 256 + t * 128, 128), 128) for t in tiles
            ]

            def row(i):
                if i < -1 or i > RY:
                    return None
                if i == -1:
                    return [halo[0, c, :, cols[t]] for t in tiles]
                if i == RY:
                    return [halo[1, c, :, cols[t]] for t in tiles]
                return [vbuf[c, i, :, cols[t]] for t in tiles]

            window = [row(i) for i in range(-2, 3)]
            prev = [None, None]
            for j in range(RY):
                total = [None, None]
                for m in range(5):
                    if window[m] is None or j + m - 2 == -1 and j == 0:
                        continue
                    if j + m - 2 == RY and j == RY - 1:
                        continue
                    weight = coef[m, j : j + 1, :]
                    for t in tiles:
                        term = weight * window[m][t]
                        total[t] = term if total[t] is None else total[t] + term
                if j > 0:
                    for t in tiles:
                        total[t] = total[t] - coef[5, j : j + 1, :] * prev[t]
                prev = total
                window = window[1:] + [row(j + 3)]
                for t in tiles:
                    vbuf[c, j, :, cols[t]] = total[t]
            for j in range(RY - 2, -1, -1):
                weight = coef[6, j : j + 1, :]
                for t in tiles:
                    prev[t] = vbuf[c, j, :, cols[t]] - weight * prev[t]
                    vbuf[c, j, :, cols[t]] = prev[t]

    def join(c):
        most = pl.ds(0, NW - 1)
        wait_all(send_f.at[c, most], land.at[c, most], fs, fr, c)
        land[c, me_w] = send_f[c, me_w]

        @pl.loop(0, 8)
        def _(x):
            cols = pl.ds(pl.multiple_of(x * 128, 128), 128)
            ends = [[land[c, h * 8 + x, way] for way in range(2)] for h in range(2)]
            for j in range(RY):
                first, last = edge[0, j : j + 1, :], edge[1, j : j + 1, :]
                for h in range(2):
                    here = (c, j, slice(h * 8, h * 8 + 8), cols)
                    vbuf[here] = vbuf[here] + (first * ends[h][0] + last * ends[h][1])

        keep_base(c).start()

    particular(0)
    solve(0)
    send_down(0)
    solve(1)
    send_down(1)
    solve(2)
    wait_all(pack.at[:, pl.ds(0, NW * (NS - 1))], recv1.at[:, pl.ds(0, NW * (NS - 1))], p1s, p1r)
    for w in range(NW):
        for b in range(2):
            pack2[w, b] = recv1[b, pl.ds(w, NS, stride=NW), :]

    def p2copy(k):
        to = lax.rem(me_w + k, NW)
        return pltpu.make_async_remote_copy(
            src_ref=pack2.at[to],
            dst_ref=recv2.at[me_w],
            send_sem=p2s.at[0],
            recv_sem=p2r.at[0],
            device_id=(to, me_s),
            device_id_type=MESH,
        )

    for k in range(1, NW):
        p2copy(k).start()
    recv2[me_w] = pack2[me_w]

    send_down(2)
    keep_own = pltpu.make_async_copy(send_f.at[2, me_w], bound.at[me_w], osem.at[2])
    keep_own.start()
    particular(1)
    particular(2)
    keep_base(2).start()
    join(0)
    join(1)

    wait_all(pack2.at[pl.ds(0, NW - 1)], recv2.at[pl.ds(0, NW - 1)], p2s, p2r)
    part_t[0:128, :] = recv2[:, 0].reshape(NW * NS, 128).T
    rest = recv2[:, 1].reshape(NW * NS, 128)
    flipped = rest.T
    part_t[128:192, :] = flipped[0:64]
    part_t[192:256, :] = (flipped[64:128].astype(jnp.int32) & 127).astype(F32)
    place = rest.astype(jnp.int32)
    rows_v[...] = (
        (place >> 13) * 64 + ((place >> 7) & 7) * 8 + ((place >> 10) & 7)
    ) * 4
    keep_part = pltpu.make_async_copy(part_t, part_h, osem.at[3])
    keep_part.start()
    keep_rows = pltpu.make_async_copy(rows_v, rows_h, osem.at[4])
    keep_rows.start()

    wait_all(send_f.at[2, pl.ds(0, NW - 1)], bound.at[pl.ds(0, NW - 1)], fs, fr, 2)
    for c in range(3):
        keep_base(c).wait()
    for keep in (keep_coef, keep_own, keep_part, keep_rows):
        keep.wait()


def exchange(vel, lower, upper, st, forces, owner, cells, counts):
    hbm = pl.BlockSpec(memory_space=pl.ANY)
    dma = pltpu.SemaphoreType.DMA
    return pl.pallas_call(
        exchange_kernel,
        out_shape=(
            jax.ShapeDtypeStruct((3, RY, SZ, NX), F32),
            jax.ShapeDtypeStruct((NW, 2, 8, 128), F32),
            jax.ShapeDtypeStruct((2, RY, 128), F32),
            jax.ShapeDtypeStruct((256, 128), F32),
            jax.ShapeDtypeStruct((128, 128), jnp.int32),
        ),
        in_specs=[hbm] * 8,
        out_specs=[hbm] * 5,
        scratch_shapes=[
            pltpu.VMEM((1, NW * RY), F32),
            pltpu.VMEM((1, NW * RY), F32),
            pltpu.VMEM(st.shape, F32),
            pltpu.VMEM(forces.shape, F32),
            pltpu.VMEM(owner.shape, jnp.int32),
            pltpu.VMEM(cells.shape, jnp.int32),
            pltpu.SMEM((1,), jnp.int32),
            pltpu.VMEM((2, 3, SZ, NX), F32),
            pltpu.VMEM((7, RY, 128), F32),
            pltpu.VMEM((2, RY, 128), F32),
            pltpu.VMEM((256, 128), F32),
            pltpu.VMEM((128, 128), jnp.int32),
            pltpu.VMEM((8, owner.shape[1]), F32),
            pltpu.VMEM((12 * NW, owner.shape[1]), jnp.bfloat16),
            pltpu.VMEM((owner.shape[1], NS * SLOTS), jnp.bfloat16),
            pltpu.VMEM((3, RY, SZ, NX), F32),
            pltpu.VMEM((3, NW, 2, 8, 128), F32),
            pltpu.VMEM((3, NW, 2, 8, 128), F32),
            pltpu.VMEM((3, NW, 2, 8, 128), F32),
            pltpu.VMEM((2, NW, 2, 8, 128), F32),
            pltpu.VMEM((NW, 8, 128), F32),
            pltpu.VMEM((NW, 8, 128), F32),
            pltpu.VMEM((8, 128), F32),
            pltpu.VMEM((2, 8, 128), F32),
            pltpu.VMEM((2, NW * NS, 128), F32),
            pltpu.VMEM((2, NW * NS, 128), F32),
            pltpu.VMEM((NW, 2, NS, 128), F32),
            pltpu.VMEM((NW, 2, NS, 128), F32),
            pltpu.VMEM((RY, 128), F32),
            pltpu.VMEM((RY, 128), F32),
            pltpu.VMEM((RY, 128), F32),
            pltpu.VMEM((RY, 128), F32),
            pltpu.VMEM((RY, 128), F32),
            pltpu.VMEM((RY, 128), F32),
            pltpu.VMEM((RY, 128), F32),
            pltpu.VMEM((RY, 128), F32),
            pltpu.VMEM((RY + 8, 128), F32),
            pltpu.VMEM((2, RY + 8, 128), F32),
            pltpu.VMEM((6, NW, 128), F32),
            dma((7,)), dma((5,)), dma((3,)), dma((6,)), dma((6,)), dma((6,)), dma((2,)), dma((2,)),
            *[dma((3,))] * 4, *[dma((1,))] * 4,
        ],
        compiler_params=pltpu.CompilerParams(
            collective_id=0, has_side_effects=True, vmem_limit_bytes=56 << 20
        ),
        name="exchange",
    )(vel, lower, upper, st, forces, owner, cells, counts)


def local_kernel(
    base, bound_h, edge_h, part_h, rows_h, inv_vol,
    derivative, forcing,
    bound, edge, part_t, rows,
    acc0, acc1, acc2, acc3, even, odd, mixed, vbuf, stage, isem, vsem, dsem, fsem, csem,
):
    def take(x):
        part = (2, slice(None), slice(None), pl.ds(pl.multiple_of(x * 512, 512), 512))
        return pltpu.make_async_copy(base.at[part], vbuf.at[part[1:]], vsem.at[x])

    staged = ((edge_h, edge), (bound_h, bound), (part_h, part_t), (rows_h, rows))
    loads = [
        pltpu.make_async_copy(src, dst, isem.at[i]) for i, (src, dst) in enumerate(staged)
    ]
    done = pl.ds(0, 2)
    whole = pltpu.make_async_copy(base.at[done], derivative.at[done], csem.at[0])
    for load in loads:
        load.start()
    for half in range(2):
        take(half).start()
    whole.start()

    accs = (acc0, acc1, acc2, acc3)
    depth = acc0.shape[0]

    @pl.loop(0, 128)
    def _(i):
        at = pl.ds(pl.multiple_of(i * (depth // 128), depth // 128), depth // 128)
        for acc in accs:
            acc[at, :] = jnp.zeros((depth // 128, 128), F32)

    lane = lax.broadcasted_iota(jnp.int32, (8, 128), 1).astype(F32)

    def spread(source, to):
        pick = jnp.full((8, 128), source, jnp.int32)
        for g in range(SLOTS // 8):
            xl = jnp.take_along_axis(part_t[192 + g * 8 : 200 + g * 8, :], pick, axis=1)
            hit = xl == lane
            for c in range(3):
                r0 = c * SLOTS + g * 8
                f = jnp.take_along_axis(part_t[r0 : r0 + 8, :], pick, axis=1)
                to[pl.ds(g * 32 + c, 8, stride=4), :] = jnp.where(hit, f, 0.0)

    group = 2

    def add(source, frm, steps):
        base = source * 128 + SLOTS
        for r0 in range(0, SLOTS, 4 * group):
            for k in range(4):
                slots = [r0 + k + 4 * g for g in range(group)]
                first = [rows[base + r] for r in slots]
                at = [pl.ds(pl.multiple_of(f, 4), 4) for f in first]
                value = [frm[r * 4 : r * 4 + 4, :] for r in slots]
                held = [accs[k][a, :] for a in at]
                for g in range(group):
                    held[g] = held[g] + value[g]
                    for e in range(g):
                        held[g] = held[g] + jnp.where(first[e] == first[g], value[e], 0.0)
                for g in range(group):
                    accs[k][at[g], :] = held[g]
                if k % 2 == 1:
                    next(steps, None)

    even[...] = jnp.zeros((256, 128), F32)
    odd[...] = jnp.zeros((256, 128), F32)
    for load in loads:
        load.wait()
    spread(0, even)

    def put_d(x):
        part = (2, slice(None), slice(None), pl.ds(pl.multiple_of(x * 512, 512), 512))
        return pltpu.make_async_copy(vbuf.at[part[1:]], derivative.at[part], dsem.at[x])

    def join_steps(h, x):
        here = (pl.ds(pl.multiple_of(h * 8, 8), 8), pl.ds(pl.multiple_of(x * 128, 128), 128))
        under, above = bound[h * 8 + x, 0], bound[h * 8 + x, 1]
        for j in range(RY):
            vbuf[j, *here] = vbuf[j, *here] + (
                edge[0, j : j + 1, :] * under + edge[1, j : j + 1, :] * above
            )
            yield

    def scatter_pair(i, steps):
        spread(2 * i + 1, odd)
        add(2 * i, even, steps)
        spread(jnp.minimum(2 * i + 2, 127), even)
        add(2 * i + 1, odd, steps)
        for _rest in steps:
            pass

    @pl.loop(0, 2)
    def _(half):
        take(half).wait()

        @pl.loop(0, 8)
        def _(t):
            scatter_pair(half * 8 + t, join_steps(t // 4, half * 4 + t % 4))

        put_d(half).start()

    @pl.loop(16, 64)
    def _(i):
        scatter_pair(i, iter(()))

    def put_f(b):
        part = (slice(None), pl.ds(b * 2, 2))
        return pltpu.make_async_copy(stage.at[part], forcing.at[part], fsem.at[b])

    @pl.loop(0, 16)
    def _(b):
        @pl.loop(0, 4)
        def _(jh):
            j, h = b * 2 + jh // 2, jh % 2
            scale = -inv_vol[j]
            cells = pl.ds(pl.multiple_of(h * 8, 8), 8)
            for x in range(8):
                at = pl.ds(pl.multiple_of(((j * 2 + h) * 8 + x) * 32, 32), 32)
                mixed[x * 32 : x * 32 + 32, :] = scale * (
                    (acc0[at, :] + acc1[at, :]) + (acc2[at, :] + acc3[at, :])
                )
            for x in range(8):
                for c in range(3):
                    stage[c, j, cells, x * 128 : x * 128 + 128] = mixed[
                        pl.ds(x * 32 + c, 8, stride=4), :
                    ]

        put_f(b).start()

    whole.wait()
    for half in range(2):
        put_d(half).wait()

    @pl.loop(0, 16)
    def _(b):
        put_f(b).wait()


def local(base, bound, edge, part_t, rows, inv_vol):
    sm = pl.BlockSpec(memory_space=pltpu.SMEM)
    hbm = pl.BlockSpec(memory_space=pl.ANY)
    depth = RY * SZ * NX // 128 * 4
    whole = (3, RY, SZ, NX)
    return pl.pallas_call(
        local_kernel,
        out_shape=(jax.ShapeDtypeStruct(whole, F32), jax.ShapeDtypeStruct(whole, F32)),
        in_specs=[hbm] * 5 + [sm],
        out_specs=(hbm, hbm),
        scratch_shapes=[
            pltpu.VMEM(bound.shape, F32),
            pltpu.VMEM(edge.shape, F32),
            pltpu.VMEM(part_t.shape, F32),
            pltpu.SMEM(rows.shape, jnp.int32),
        ]
        + [pltpu.VMEM((depth, 128), F32)] * 4
        + [pltpu.VMEM((256, 128), F32)] * 3
        + [pltpu.VMEM(whole[1:], F32), pltpu.VMEM(whole, F32)]
        + [pltpu.SemaphoreType.DMA((n,)) for n in (4, 2, 2, 16, 1)],
        compiler_params=pltpu.CompilerParams(vmem_limit_bytes=58 << 20),
        name="local",
    )(base, bound, edge, part_t, rows, inv_vol)


def body(velocity, lower, upper, stencil, inv_volume, forces, owner, cells, counts):
    base, bound, edge, part_t, rows = exchange(
        velocity, lower.reshape(1, -1), upper.reshape(1, -1), stencil, forces,
        owner.reshape(1, -1), cells.reshape(1, -1), counts,
    )
    derivative, forcing = local(base, bound, edge, part_t, rows.reshape(-1), inv_volume)
    return derivative, forcing


def solution(mesh):
    in_specs = (
        P(None, "wall", "span", None),
        P(),
        P(),
        P(None, "wall"),
        P("wall"),
        P(None, ("wall", "span")),
        P(("wall", "span"), None),
        P(("wall", "span")),
        P(("wall", "span")),
    )
    out_specs = (P(None, "wall", "span", None), P(None, "wall", "span", None))
    return jax.shard_map(body, mesh=mesh, in_specs=in_specs, out_specs=out_specs, check_vma=False)
```

```python
import functools

import jax
import jax.numpy as jnp
from jax import lax
from jax.experimental import pallas as pl
from jax.experimental.pallas import tpu as pltpu
from jax.sharding import PartitionSpec as P

F32 = jnp.float32
MESH = pl.DeviceIdType.MESH
NW, NS = 16, 8
RY, SZ, NX = 32, 16, 1024
SLOTS = 64


def exchange_kernel(
    vel, lower_h, upper_h, st_h, forces_h, owner_h, cells_h, counts_h,
    base_h, bound, edge_h, part_h, rows_h,
    lower, upper, st, forces, owner, cells, counts, halo, coef, edge, part_t, rows_v,
    key_row, left, right, vbuf, send_a, recv_a, send_f, land, elim, pbuf, tile_out, tile_in,
    pack, recv1, pack2, recv2,
    lmat, umat, dmat, cmat, ymat, zmat, first_col, last_col, wmat, wgt, red,
    isem, osem, bsem, vsem, hs, hr, ts, tr, as_, ar, fs, fr, p1s, p1r, p2s, p2r,
):
    me_w = lax.axis_index("wall")
    me_s = lax.axis_index("span")

    def wait_all(src, dst, sent, got, i=0):
        group = pltpu.make_async_remote_copy(
            src_ref=src,
            dst_ref=dst,
            send_sem=sent.at[i],
            recv_sem=got.at[i],
            device_id=(me_w, me_s),
            device_id_type=MESH,
        )
        group.wait_send()
        group.wait_recv()

    def vcopy(c, h):
        part = (c, slice(None), pl.ds(h * 8, 8), slice(None))
        return pltpu.make_async_copy(vel.at[part], vbuf.at[part], vsem.at[c * 2 + h])

    barrier = pltpu.get_barrier_semaphore()

    @pl.loop(1, NW)
    def _(k):
        pl.semaphore_signal(
            barrier, inc=1, device_id=(lax.rem(me_w + k, NW), me_s), device_id_type=MESH
        )

    @pl.loop(1, NS)
    def _(k):
        pl.semaphore_signal(
            barrier, inc=1, device_id=(me_w, lax.rem(me_s + k, NS)), device_id_type=MESH
        )

    staged = (
        (st_h, st), (lower_h, lower), (upper_h, upper),
        (forces_h, forces), (owner_h, owner), (cells_h, cells), (counts_h, counts),
    )
    loads = [
        pltpu.make_async_copy(src, dst, isem.at[i]) for i, (src, dst) in enumerate(staged)
    ]
    for i in range(3):
        loads[i].start()
    for c in range(3):
        for h in range(2):
            vcopy(c, h).start()
    for i in range(3, 7):
        loads[i].start()
    pl.semaphore_wait(barrier, NW - 1 + NS - 1)

    above = lax.rem(me_w + 1, NW)
    under = lax.rem(me_w + NW - 1, NW)

    def hcopy(way, c):
        return pltpu.make_async_remote_copy(
            src_ref=vel.at[c, RY - 1 if way == 0 else 0],
            dst_ref=halo.at[way, c],
            send_sem=hs.at[way * 3 + c],
            recv_sem=hr.at[way * 3 + c],
            device_id=(above if way == 0 else under, me_s),
            device_id_type=MESH,
        )

    hcopy(0, 0).start()
    hcopy(1, 0).start()

    for i in range(3):
        loads[i].wait()
    eye = lax.broadcasted_iota(jnp.int32, (RY, RY), 0) == lax.broadcasted_iota(
        jnp.int32, (RY, RY), 1
    )

    def column(row, mask, n):
        full = jnp.broadcast_to(row, (n, n))
        col = jnp.sum(jnp.where(mask, full, 0.0), axis=1, keepdims=True)
        return jnp.broadcast_to(col, (n, 128))

    stc = [column(st[m : m + 1, :], eye, RY) for m in range(5)]
    tile_out[0:1, :] = stc[0][0:1]
    tile_out[1:2, :] = stc[1][0:1]
    tile_out[2:3, :] = stc[4][RY - 1 : RY]
    tile_out[3:4, :] = stc[3][RY - 1 : RY]
    tile_out[4:8, :] = jnp.zeros((4, 128), F32)

    def tcopy(way):
        return pltpu.make_async_remote_copy(
            src_ref=tile_out,
            dst_ref=tile_in.at[way],
            send_sem=ts.at[way],
            recv_sem=tr.at[way],
            device_id=(above if way == 0 else under, me_s),
            device_id_type=MESH,
        )

    tcopy(0).start()
    tcopy(1).start()
    for c in (1, 2):
        hcopy(0, c).start()
        hcopy(1, c).start()


    nn = (((1,), (0,)), ((), ()))
    lane_i = lax.broadcasted_iota(jnp.int32, (RY, NW * RY), 1)
    in_row = (lane_i & (RY - 1)) == lax.broadcasted_iota(jnp.int32, (RY, NW * RY), 0)
    to_slab = (
        lax.broadcasted_iota(jnp.int32, (NW * RY, 128), 0) // RY
        == lax.broadcasted_iota(jnp.int32, (NW * RY, 128), 1)
    ).astype(F32).astype(jnp.bfloat16)
    both = jnp.concatenate(
        [
            jnp.where(in_row, jnp.broadcast_to(v[0:1, :], (RY, NW * RY)), 0.0)
            for v in (lower, upper)
        ],
        axis=0,
    )
    tall = None
    for _part in range(3):
        head = both.astype(jnp.bfloat16)
        both = both - head.astype(F32)
        term = lax.dot_general(head, to_slab, nn, preferred_element_type=F32)
        tall = term if tall is None else tall + term
    lmat[...] = tall[0:RY]
    umat[...] = tall[RY : 2 * RY]

    zero = jnp.zeros((1, 128), F32)
    carry_c, carry_b = zero, None
    for j in range(RY):
        low, upp = lmat[j : j + 1, :], umat[j : j + 1, :]
        inv = 1.0 / (1.0 - low * carry_c) if j > 0 else jnp.ones((1, 128), F32)
        carry_c = upp * inv
        dmat[j : j + 1, :] = inv
        cmat[j : j + 1, :] = carry_c
    binv = [None] * RY
    for j in range(RY - 1, -1, -1):
        if j == RY - 1:
            binv[j] = jnp.ones((1, 128), F32)
        else:
            binv[j] = 1.0 / (
                1.0 - umat[j : j + 1, :] * lmat[j + 1 : j + 2, :] * binv[j + 1]
            )
    y = binv[0]
    ymat[0:1, :] = y
    for j in range(1, RY):
        y = -(umat[j - 1 : j, :] * binv[j]) * y
        ymat[j : j + 1, :] = y
    z = dmat[RY - 1 : RY, :]
    zmat[RY - 1 : RY, :] = z
    for j in range(RY - 2, -1, -1):
        z = -(lmat[j + 1 : j + 2, :] * dmat[j : j + 1, :]) * z
        zmat[j : j + 1, :] = z
    v = binv[0]
    first_col[0:1, :] = v
    for j in range(1, RY):
        v = -(lmat[j : j + 1, :] * binv[j]) * v
        first_col[j : j + 1, :] = v
    v = dmat[RY - 1 : RY, :]
    last_col[RY - 1 : RY, :] = v
    for j in range(RY - 2, -1, -1):
        v = -cmat[j : j + 1, :] * v
        last_col[j : j + 1, :] = v

    lane16 = lax.broadcasted_iota(jnp.int32, (RY, 128), 1)

    def at_slab(values, slab):
        n = values.shape[0]
        col = jnp.sum(jnp.where(lane16[0:n] == slab, values, 0.0), axis=1, keepdims=True)
        return jnp.broadcast_to(col, (n, 128))

    low_all, upp_all = lmat[...], umat[...]
    inv_own = at_slab(dmat[...], me_w)
    c_own = at_slab(cmat[...], me_w)
    y_own = at_slab(ymat[...], me_w)
    z_own = at_slab(zmat[...], me_w)
    low_own = at_slab(low_all, me_w)
    low_next = at_slab(low_all[0:1], me_w + 1)
    upp_prev = at_slab(upp_all[RY - 1 : RY], me_w - 1)
    has_under = jnp.where(me_w > 0, 1.0, 0.0)
    has_above = jnp.where(me_w < NW - 1, 1.0, 0.0)

    row_i = lax.broadcasted_iota(jnp.int32, (RY, 128), 0)
    kept = [
        jnp.where(row_i == 0, 0.0, jnp.where(row_i == 1, stc[0] * has_under, stc[0])),
        jnp.where(row_i == 0, 0.0, stc[1]),
        stc[2],
        jnp.where(row_i == RY - 1, 0.0, stc[3]),
        jnp.where(
            row_i == RY - 1, 0.0, jnp.where(row_i == RY - 2, stc[4] * has_above, stc[4])
        ),
    ]
    for m in range(5):
        coef[m] = kept[m] * inv_own
    coef[5] = jnp.where(row_i == 0, 0.0, low_own * inv_own)
    coef[6] = c_own
    edge[0] = at_slab(first_col[...], me_w)
    edge[1] = at_slab(last_col[...], me_w)
    keep_coef = pltpu.make_async_copy(edge, edge_h, osem.at[0])
    keep_coef.start()

    for way, own, scale in ((0, z_own, low_next), (1, y_own, upp_prev)):
        wmat[...] = jnp.zeros((RY + 8, 128), F32)
        for m in range(5):
            wmat[m + 2 : m + 2 + RY, :] += kept[m] * own
        wgt[way] = wmat[...] * (-scale)

    eye16 = lax.broadcasted_iota(jnp.int32, (NW, NW), 0) == lax.broadcasted_iota(
        jnp.int32, (NW, NW), 1
    )
    next16 = lax.broadcasted_iota(jnp.int32, (NW, NW), 0) + 1 == lax.broadcasted_iota(
        jnp.int32, (NW, NW), 1
    )
    prev16 = lax.broadcasted_iota(jnp.int32, (NW, NW), 0) - 1 == lax.broadcasted_iota(
        jnp.int32, (NW, NW), 1
    )
    z0 = column(zmat[0:1, 0:NW], eye16, NW)
    z1 = column(zmat[RY - 1 : RY, 0:NW], eye16, NW)
    y0 = column(ymat[0:1, 0:NW], eye16, NW)
    y1 = column(ymat[RY - 1 : RY, 0:NW], eye16, NW)
    low_n = column(low_all[0:1, 0:NW], next16, NW)
    upp_p = column(upp_all[RY - 1 : RY, 0:NW], prev16, NW)
    red[0] = upp_p * y0
    red[1] = low_n * z0
    lz1 = low_n * z1
    uy1 = upp_p * y1
    q = -lz1[0:1]
    for s in range(1, NW):
        dinv = 1.0 / (1.0 + red[0, s : s + 1, :] * q)
        c3 = uy1[s : s + 1] * dinv
        red[2, s : s + 1, :] = q * dinv
        red[3, s : s + 1, :] = dinv
        red[4, s : s + 1, :] = c3
        red[5, s : s + 1, :] = q
        q = red[1, s : s + 1, :] * q * c3 - lz1[s : s + 1]

    def own_rows(c):
        for h in range(2):
            vcopy(c, h).wait()

            @pl.loop(0, 2)
            def _(x):
                cols = [
                    pl.ds(pl.multiple_of(x * 512 + b * 128, 128), 128) for b in range(4)
                ]
                up, down = [None] * 4, [None] * 4
                for j in range(RY):
                    wu, wd = wgt[0, j + 4 : j + 5, :], wgt[1, j + 4 : j + 5, :]
                    for b in range(4):
                        u = vbuf[c, j, h * 8 : h * 8 + 8, cols[b]]
                        up[b] = wu * u if j == 0 else up[b] + wu * u
                        down[b] = wd * u if j == 0 else down[b] + wd * u
                for b in range(4):
                    send_a[c, h * 8 + x * 4 + b, 0] = up[b]
                    send_a[c, h * 8 + x * 4 + b, 1] = down[b]

    def acopy(c, k):
        to = lax.rem(me_w + k, NW)
        return pltpu.make_async_remote_copy(
            src_ref=send_a.at[c, to],
            dst_ref=recv_a.at[c, me_w],
            send_sem=as_.at[c],
            recv_sem=ar.at[c],
            device_id=(to, me_s),
            device_id_type=MESH,
        )

    def add_ends(c):
        for h in range(2):
            cells8 = slice(h * 8, h * 8 + 8)

            @pl.loop(0, 8)
            def _(x):
                cols = pl.ds(pl.multiple_of(x * 128, 128), 128)
                ends = (halo[0, c, cells8, cols], halo[1, c, cells8, cols])
                near = (
                    (tile_in[1, 0:1, :], RY - 2, tile_in[1, 1:2, :], RY - 1),
                    (tile_in[0, 2:3, :], 1, tile_in[0, 3:4, :], 0),
                )
                for way in range(2):
                    wa, ja, wb, jb = near[way]
                    send_a[c, h * 8 + x, way] += (
                        wgt[way, 3:4, :] * ends[0]
                        + wgt[way, RY + 4 : RY + 5, :] * ends[1]
                        + wa * vbuf[c, ja, cells8, cols]
                        + wb * vbuf[c, jb, cells8, cols]
                    )

    def send_up(c):
        hcopy(0, c).wait()
        hcopy(1, c).wait()
        add_ends(c)
        for k in range(1, NW):
            acopy(c, k).start()
        recv_a[c, me_w] = send_a[c, me_w]

    own_rows(0)
    own_rows(1)
    own_rows(2)

    for i in range(3, 7):
        loads[i].wait()
    slots = owner.shape[1]
    own = owner[...]
    live = lax.broadcasted_iota(jnp.int32, (1, slots), 1) < counts[0]
    wall_row = jnp.where(live, own >> 3, NW)
    key_row[0:1, :] = jnp.where(live, (own & 7) * NW + (own >> 3), 512).astype(F32)
    key_row[1:8, :] = jnp.zeros((7, slots), F32)
    lane_f = lax.broadcasted_iota(jnp.int32, (256, 128), 1).astype(F32)
    sub_f = lax.broadcasted_iota(jnp.int32, (256, 128), 0).astype(F32)
    lower_tri = [
        jnp.where(lane_f + 128.0 * b < sub_f, 1.0, 0.0) for b in range(2)
    ]

    ones = jnp.ones((128, 128), jnp.bfloat16)
    head_row = jnp.where(
        lax.broadcasted_iota(jnp.int32, (8, 128), 0) == 0, 1.0, 0.0
    ).astype(jnp.bfloat16)

    def rank_block(i, carry):
        at = pl.ds(pl.multiple_of(i * 256, 256), 256)
        tile = key_row[:, at]
        col = lax.dot_general(
            tile.T.astype(jnp.bfloat16), head_row, nn, preferred_element_type=F32
        )
        hit = col == lane_f
        score = jnp.where(hit, carry, 0.0)
        for b in range(2):
            same = col == tile[0:1, b * 128 : b * 128 + 128]
            score = score + jnp.where(same, lower_tri[b], 0.0)
        rank = lax.dot_general(
            score.astype(jnp.bfloat16), ones, nn, preferred_element_type=F32
        )
        place = jnp.floor(col * (1.0 / NW)) * SLOTS + rank
        for b in range(4):
            right[at, b * 128 : b * 128 + 128] = jnp.where(
                place == lane_f + 128.0 * b, 1.0, 0.0
            ).astype(jnp.bfloat16)
        return carry + jnp.sum(jnp.where(hit, 1.0, 0.0), axis=0, keepdims=True)

    blocks = slots // 256
    carry = lax.fori_loop(
        0, blocks // 2, rank_block, jnp.zeros((1, 128), F32), unroll=4
    )
    tcopy(0).wait()
    tcopy(1).wait()
    send_up(0)
    in_wall = lax.broadcasted_iota(jnp.int32, (NW, slots), 0) == wall_row
    load = [forces[c : c + 1, :] for c in range(3)] + [cells[...].astype(F32)]
    for part in range(3):
        head = [x.astype(jnp.bfloat16).astype(F32) for x in load]
        load = [x - y for x, y in zip(load, head)]
        for c in range(4):
            r0 = (part * 4 + c) * NW
            left[r0 : r0 + NW, :] = jnp.where(in_wall, head[c], 0.0).astype(jnp.bfloat16)
    send_up(1)
    carry = lax.fori_loop(blocks // 2, blocks * 3 // 4, rank_block, carry, unroll=4)
    send_up(2)
    lax.fori_loop(blocks * 3 // 4, blocks, rank_block, carry, unroll=4)
    made = lax.dot_general(left[...], right[...], nn, preferred_element_type=F32)
    made = made[0:64] + made[64:128] + made[128:192]
    first = lax.broadcasted_iota(jnp.int32, (NW, 128), 1) < SLOTS
    for k in range(NS):
        for b in range(2):
            pair = [
                made[c * NW : c * NW + NW, k // 2 * 128 : k // 2 * 128 + 128]
                for c in (2 * b, 2 * b + 1)
            ]
            turn = 1 - k % 2
            pair[turn] = pltpu.roll(pair[turn], SLOTS, 1)
            pack[b, k * NW : k * NW + NW, :] = jnp.where(first, pair[0], pair[1])

    def p1copy(k):
        to = lax.rem(me_s + k, NS)
        return pltpu.make_async_remote_copy(
            src_ref=pack.at[:, pl.ds(pl.multiple_of(to * NW, NW), NW)],
            dst_ref=recv1.at[:, pl.ds(pl.multiple_of(me_s * NW, NW), NW)],
            send_sem=p1s.at[0],
            recv_sem=p1r.at[0],
            device_id=(me_w, to),
            device_id_type=MESH,
        )

    for k in range(1, NS):
        p1copy(k).start()
    mine = pl.ds(pl.multiple_of(me_s * NW, NW), NW)
    recv1[:, mine, :] = pack[:, mine, :]

    def solve(c):
        wait_all(send_a.at[c, pl.ds(0, NW - 1)], recv_a.at[c, pl.ds(0, NW - 1)], as_, ar, c)
        p = recv_a[c, 0, 0]
        for s in range(1, NW):
            pbuf[s] = p
            e = recv_a[c, s, 1] - red[0, s : s + 1, :] * p
            elim[s] = e
            if s < NW - 1:
                p = recv_a[c, s, 0] - red[1, s : s + 1, :] * (
                    p + red[2, s : s + 1, :] * e
                )
        down = jnp.zeros((8, 128), F32)
        send_f[c, NW - 1, 1] = down
        for s in range(NW - 1, 0, -1):
            down = red[3, s : s + 1, :] * elim[s] - red[4, s : s + 1, :] * down
            send_f[c, s - 1, 1] = down
            send_f[c, s, 0] = pbuf[s] + red[5, s : s + 1, :] * down
        send_f[c, 0, 0] = jnp.zeros((8, 128), F32)

    def send_down(c):
        for k in range(1, NW):
            fcopy(c, k).start()

    def fcopy(c, k):
        to = lax.rem(me_w + k, NW)
        return pltpu.make_async_remote_copy(
            src_ref=send_f.at[c, to],
            dst_ref=land.at[c, me_w] if c < 2 else bound.at[me_w],
            send_sem=fs.at[c],
            recv_sem=fr.at[c],
            device_id=(to, me_s),
            device_id_type=MESH,
        )

    def keep_base(c):
        return pltpu.make_async_copy(vbuf.at[c], base_h.at[c], bsem.at[c])

    def particular(c):
        @pl.loop(0, 4)
        def _(xx):
            tiles = range(2)
            cols = [
                pl.ds(pl.multiple_of(xx * 256 + t * 128, 128), 128) for t in tiles
            ]

            def row(i):
                if i < -1 or i > RY:
                    return None
                if i == -1:
                    return [halo[0, c, :, cols[t]] for t in tiles]
                if i == RY:
                    return [halo[1, c, :, cols[t]] for t in tiles]
                return [vbuf[c, i, :, cols[t]] for t in tiles]

            window = [row(i) for i in range(-2, 3)]
            prev = [None, None]
            for j in range(RY):
                total = [None, None]
                for m in range(5):
                    if window[m] is None or j + m - 2 == -1 and j == 0:
                        continue
                    if j + m - 2 == RY and j == RY - 1:
                        continue
                    weight = coef[m, j : j + 1, :]
                    for t in tiles:
                        term = weight * window[m][t]
                        total[t] = term if total[t] is None else total[t] + term
                if j > 0:
                    for t in tiles:
                        total[t] = total[t] - coef[5, j : j + 1, :] * prev[t]
                prev = total
                window = window[1:] + [row(j + 3)]
                for t in tiles:
                    vbuf[c, j, :, cols[t]] = total[t]
            for j in range(RY - 2, -1, -1):
                weight = coef[6, j : j + 1, :]
                for t in tiles:
                    prev[t] = vbuf[c, j, :, cols[t]] - weight * prev[t]
                    vbuf[c, j, :, cols[t]] = prev[t]

    def join(c):
        most = pl.ds(0, NW - 1)
        wait_all(send_f.at[c, most], land.at[c, most], fs, fr, c)
        land[c, me_w] = send_f[c, me_w]

        @pl.loop(0, 8)
        def _(x):
            cols = pl.ds(pl.multiple_of(x * 128, 128), 128)
            ends = [[land[c, h * 8 + x, way] for way in range(2)] for h in range(2)]
            for j in range(RY):
                first, last = edge[0, j : j + 1, :], edge[1, j : j + 1, :]
                for h in range(2):
                    here = (c, j, slice(h * 8, h * 8 + 8), cols)
                    vbuf[here] = vbuf[here] + (first * ends[h][0] + last * ends[h][1])

        keep_base(c).start()

    particular(0)
    solve(0)
    send_down(0)
    solve(1)
    send_down(1)
    solve(2)
    wait_all(pack.at[:, pl.ds(0, NW * (NS - 1))], recv1.at[:, pl.ds(0, NW * (NS - 1))], p1s, p1r)
    for w in range(NW):
        for b in range(2):
            pack2[w, b] = recv1[b, pl.ds(w, NS, stride=NW), :]

    def p2copy(k):
        to = lax.rem(me_w + k, NW)
        return pltpu.make_async_remote_copy(
            src_ref=pack2.at[to],
            dst_ref=recv2.at[me_w],
            send_sem=p2s.at[0],
            recv_sem=p2r.at[0],
            device_id=(to, me_s),
            device_id_type=MESH,
        )

    for k in range(1, NW):
        p2copy(k).start()
    recv2[me_w] = pack2[me_w]

    send_down(2)
    keep_own = pltpu.make_async_copy(send_f.at[2, me_w], bound.at[me_w], osem.at[2])
    keep_own.start()
    particular(1)
    particular(2)
    keep_base(2).start()
    join(0)
    join(1)

    wait_all(pack2.at[pl.ds(0, NW - 1)], recv2.at[pl.ds(0, NW - 1)], p2s, p2r)
    part_t[0:128, :] = recv2[:, 0].reshape(NW * NS, 128).T
    rest = recv2[:, 1].reshape(NW * NS, 128)
    flipped = rest.T
    part_t[128:192, :] = flipped[0:64]
    part_t[192:256, :] = (flipped[64:128].astype(jnp.int32) & 127).astype(F32)
    place = rest.astype(jnp.int32)
    rows_v[...] = (
        (place >> 13) * 64 + ((place >> 7) & 7) * 8 + ((place >> 10) & 7)
    ) * 4
    keep_part = pltpu.make_async_copy(part_t, part_h, osem.at[3])
    keep_part.start()
    keep_rows = pltpu.make_async_copy(rows_v, rows_h, osem.at[4])
    keep_rows.start()

    wait_all(send_f.at[2, pl.ds(0, NW - 1)], bound.at[pl.ds(0, NW - 1)], fs, fr, 2)
    for c in range(3):
        keep_base(c).wait()
    for keep in (keep_coef, keep_own, keep_part, keep_rows):
        keep.wait()


def exchange(vel, lower, upper, st, forces, owner, cells, counts):
    hbm = pl.BlockSpec(memory_space=pl.ANY)
    dma = pltpu.SemaphoreType.DMA
    return pl.pallas_call(
        exchange_kernel,
        out_shape=(
            jax.ShapeDtypeStruct((3, RY, SZ, NX), F32),
            jax.ShapeDtypeStruct((NW, 2, 8, 128), F32),
            jax.ShapeDtypeStruct((2, RY, 128), F32),
            jax.ShapeDtypeStruct((256, 128), F32),
            jax.ShapeDtypeStruct((128, 128), jnp.int32),
        ),
        in_specs=[hbm] * 8,
        out_specs=[hbm] * 5,
        scratch_shapes=[
            pltpu.VMEM((1, NW * RY), F32),
            pltpu.VMEM((1, NW * RY), F32),
            pltpu.VMEM(st.shape, F32),
            pltpu.VMEM(forces.shape, F32),
            pltpu.VMEM(owner.shape, jnp.int32),
            pltpu.VMEM(cells.shape, jnp.int32),
            pltpu.SMEM((1,), jnp.int32),
            pltpu.VMEM((2, 3, SZ, NX), F32),
            pltpu.VMEM((7, RY, 128), F32),
            pltpu.VMEM((2, RY, 128), F32),
            pltpu.VMEM((256, 128), F32),
            pltpu.VMEM((128, 128), jnp.int32),
            pltpu.VMEM((8, owner.shape[1]), F32),
            pltpu.VMEM((12 * NW, owner.shape[1]), jnp.bfloat16),
            pltpu.VMEM((owner.shape[1], NS * SLOTS), jnp.bfloat16),
            pltpu.VMEM((3, RY, SZ, NX), F32),
            pltpu.VMEM((3, NW, 2, 8, 128), F32),
            pltpu.VMEM((3, NW, 2, 8, 128), F32),
            pltpu.VMEM((3, NW, 2, 8, 128), F32),
            pltpu.VMEM((2, NW, 2, 8, 128), F32),
            pltpu.VMEM((NW, 8, 128), F32),
            pltpu.VMEM((NW, 8, 128), F32),
            pltpu.VMEM((8, 128), F32),
            pltpu.VMEM((2, 8, 128), F32),
            pltpu.VMEM((2, NW * NS, 128), F32),
            pltpu.VMEM((2, NW * NS, 128), F32),
            pltpu.VMEM((NW, 2, NS, 128), F32),
            pltpu.VMEM((NW, 2, NS, 128), F32),
            pltpu.VMEM((RY, 128), F32),
            pltpu.VMEM((RY, 128), F32),
            pltpu.VMEM((RY, 128), F32),
            pltpu.VMEM((RY, 128), F32),
            pltpu.VMEM((RY, 128), F32),
            pltpu.VMEM((RY, 128), F32),
            pltpu.VMEM((RY, 128), F32),
            pltpu.VMEM((RY, 128), F32),
            pltpu.VMEM((RY + 8, 128), F32),
            pltpu.VMEM((2, RY + 8, 128), F32),
            pltpu.VMEM((6, NW, 128), F32),
            dma((7,)), dma((5,)), dma((3,)), dma((6,)), dma((6,)), dma((6,)), dma((2,)), dma((2,)),
            *[dma((3,))] * 4, *[dma((1,))] * 4,
        ],
        compiler_params=pltpu.CompilerParams(
            collective_id=0, has_side_effects=True, vmem_limit_bytes=56 << 20
        ),
        name="exchange",
    )(vel, lower, upper, st, forces, owner, cells, counts)


def local_kernel(
    base, bound_h, edge_h, part_h, rows_h, inv_vol,
    derivative, forcing,
    bound, edge, part_t, rows,
    acc0, acc1, acc2, acc3, even, odd, mixed, vbuf, through, stage, isem, vsem, dsem, fsem, csem,
):
    def take(x):
        part = (2, slice(None), slice(None), pl.ds(pl.multiple_of(x * 512, 512), 512))
        return pltpu.make_async_copy(base.at[part], vbuf.at[part[1:]], vsem.at[x])

    staged = ((edge_h, edge), (bound_h, bound), (part_h, part_t), (rows_h, rows))
    loads = [
        pltpu.make_async_copy(src, dst, isem.at[i]) for i, (src, dst) in enumerate(staged)
    ]
    done = pl.ds(0, 2)
    whole_in = pltpu.make_async_copy(base.at[done], through, csem.at[0])
    whole = pltpu.make_async_copy(through, derivative.at[done], csem.at[1])
    for load in loads:
        load.start()
    for half in range(2):
        take(half).start()
    whole_in.start()

    accs = (acc0, acc1, acc2, acc3)
    depth = acc0.shape[0]

    @pl.loop(0, 128)
    def _(i):
        at = pl.ds(pl.multiple_of(i * (depth // 128), depth // 128), depth // 128)
        for acc in accs:
            acc[at, :] = jnp.zeros((depth // 128, 128), F32)

    lane = lax.broadcasted_iota(jnp.int32, (8, 128), 1).astype(F32)

    def spread(source, to):
        pick = jnp.full((8, 128), source, jnp.int32)
        for g in range(SLOTS // 8):
            xl = jnp.take_along_axis(part_t[192 + g * 8 : 200 + g * 8, :], pick, axis=1)
            hit = xl == lane
            for c in range(3):
                r0 = c * SLOTS + g * 8
                f = jnp.take_along_axis(part_t[r0 : r0 + 8, :], pick, axis=1)
                to[pl.ds(g * 32 + c, 8, stride=4), :] = jnp.where(hit, f, 0.0)

    group = 2

    def add(source, frm, steps):
        base = source * 128 + SLOTS
        for r0 in range(0, SLOTS, 4 * group):
            for k in range(4):
                slots = [r0 + k + 4 * g for g in range(group)]
                first = [rows[base + r] for r in slots]
                at = [pl.ds(pl.multiple_of(f, 4), 4) for f in first]
                value = [frm[r * 4 : r * 4 + 4, :] for r in slots]
                held = [accs[k][a, :] for a in at]
                for g in range(group):
                    held[g] = held[g] + value[g]
                    for e in range(g):
                        held[g] = held[g] + jnp.where(first[e] == first[g], value[e], 0.0)
                for g in range(group):
                    accs[k][at[g], :] = held[g]
                if k % 2 == 1:
                    next(steps, None)

    even[...] = jnp.zeros((256, 128), F32)
    odd[...] = jnp.zeros((256, 128), F32)
    for load in loads:
        load.wait()
    spread(0, even)

    def put_d(x):
        part = (2, slice(None), slice(None), pl.ds(pl.multiple_of(x * 512, 512), 512))
        return pltpu.make_async_copy(vbuf.at[part[1:]], derivative.at[part], dsem.at[x])

    def join_steps(h, x):
        here = (pl.ds(pl.multiple_of(h * 8, 8), 8), pl.ds(pl.multiple_of(x * 128, 128), 128))
        under, above = bound[h * 8 + x, 0], bound[h * 8 + x, 1]
        for j in range(RY):
            vbuf[j, *here] = vbuf[j, *here] + (
                edge[0, j : j + 1, :] * under + edge[1, j : j + 1, :] * above
            )
            yield

    def scatter_pair(i, steps):
        spread(2 * i + 1, odd)
        add(2 * i, even, steps)
        spread(jnp.minimum(2 * i + 2, 127), even)
        add(2 * i + 1, odd, steps)
        for _rest in steps:
            pass

    @pl.loop(0, 2)
    def _(half):
        take(half).wait()

        @pl.loop(0, 8)
        def _(t):
            scatter_pair(half * 8 + t, join_steps(t // 4, half * 4 + t % 4))

        put_d(half).start()

    whole_in.wait()
    whole.start()

    @pl.loop(16, 64)
    def _(i):
        scatter_pair(i, iter(()))

    def put_f(b):
        part = (slice(None), pl.ds(b * 2, 2))
        return pltpu.make_async_copy(stage.at[part], forcing.at[part], fsem.at[b])

    @pl.loop(0, 16)
    def _(b):
        @pl.loop(0, 4)
        def _(jh):
            j, h = b * 2 + jh // 2, jh % 2
            scale = -inv_vol[j]
            cells = pl.ds(pl.multiple_of(h * 8, 8), 8)
            for x in range(8):
                at = pl.ds(pl.multiple_of(((j * 2 + h) * 8 + x) * 32, 32), 32)
                mixed[x * 32 : x * 32 + 32, :] = scale * (
                    (acc0[at, :] + acc1[at, :]) + (acc2[at, :] + acc3[at, :])
                )
            for x in range(8):
                for c in range(3):
                    stage[c, j, cells, x * 128 : x * 128 + 128] = mixed[
                        pl.ds(x * 32 + c, 8, stride=4), :
                    ]

        put_f(b).start()

    whole.wait()
    for half in range(2):
        put_d(half).wait()

    @pl.loop(0, 16)
    def _(b):
        put_f(b).wait()


def local(base, bound, edge, part_t, rows, inv_vol):
    sm = pl.BlockSpec(memory_space=pltpu.SMEM)
    hbm = pl.BlockSpec(memory_space=pl.ANY)
    depth = RY * SZ * NX // 128 * 4
    whole = (3, RY, SZ, NX)
    return pl.pallas_call(
        local_kernel,
        out_shape=(jax.ShapeDtypeStruct(whole, F32), jax.ShapeDtypeStruct(whole, F32)),
        in_specs=[hbm] * 5 + [sm],
        out_specs=(hbm, hbm),
        scratch_shapes=[
            pltpu.VMEM(bound.shape, F32),
            pltpu.VMEM(edge.shape, F32),
            pltpu.VMEM(part_t.shape, F32),
            pltpu.SMEM(rows.shape, jnp.int32),
        ]
        + [pltpu.VMEM((depth, 128), F32)] * 4
        + [pltpu.VMEM((256, 128), F32)] * 3
        + [
            pltpu.VMEM(whole[1:], F32),
            pltpu.VMEM((2, *whole[1:]), F32),
            pltpu.VMEM(whole, F32),
        ]
        + [pltpu.SemaphoreType.DMA((n,)) for n in (4, 2, 2, 16, 2)],
        compiler_params=pltpu.CompilerParams(vmem_limit_bytes=58 << 20),
        name="local",
    )(base, bound, edge, part_t, rows, inv_vol)


def body(velocity, lower, upper, stencil, inv_volume, forces, owner, cells, counts):
    base, bound, edge, part_t, rows = exchange(
        velocity, lower.reshape(1, -1), upper.reshape(1, -1), stencil, forces,
        owner.reshape(1, -1), cells.reshape(1, -1), counts,
    )
    derivative, forcing = local(base, bound, edge, part_t, rows.reshape(-1), inv_volume)
    return derivative, forcing


def solution(mesh):
    in_specs = (
        P(None, "wall", "span", None),
        P(),
        P(),
        P(None, "wall"),
        P("wall"),
        P(None, ("wall", "span")),
        P(("wall", "span"), None),
        P(("wall", "span")),
        P(("wall", "span")),
    )
    out_specs = (P(None, "wall", "span", None), P(None, "wall", "span", None))
    return jax.shard_map(body, mesh=mesh, in_specs=in_specs, out_specs=out_specs, check_vma=False)
```
